128 devices in a mesh: cascade: 2 (over y_lo), coil: 8 (over z, core), readout: 8 (over x, y_hi).
Axes of the slice: x: 4, y: 4 (y_hi: 2, y_lo: 2; y = y_hi * 2 + y_lo), z: 4, core: 2. Of those that a mesh axis runs over, the one named last changes fastest.
Arguments:
- initial: bfloat16 [2, 4, 16, 128, 2, 128], P(None, None, 'readout'), may hold values from -6 to 6
- coil_maps: bfloat16 [2, 16, 16, 128, 2, 128], P(None, 'coil', 'readout'), may hold values from -1.5 to 1.5
- kspace: bfloat16 [2, 16, 4, 16, 128, 2, 128], P(None, 'coil', None, 'readout'), may hold values from -6 to 6
- sampled: int32 [16, 4, 128, 128], P('coil'), may hold values 0 or 1
- first_w: bfloat16 [2, 27, 2, 64], P('cascade'), may hold values from -0.875 to 0.875
- time_w: bfloat16 [2, 3, 64, 64], P('cascade'), may hold values from -0.4375 to 0.4375
- last_w: bfloat16 [2, 27, 64, 2], P('cascade'), may hold values from -0.15625 to 0.15625
Outputs:
- images: bfloat16 [2, 2, 4, 16, 128, 2, 128], P('cascade', None, None, 'readout', 'coil')
The draws below stay inside these ranges and needn't reach their ends.
Inputs may be any that keep to these rules, and one draw needn't show every extreme that they name: `sampled`: 1 where the sample at that phase, line and partition was acquired for that coil, else 0.
All inputs are finite; a program needn't handle non-finite values. No bound on the sum of `sampled` on one device may be relied on, other than what follows from the above.
Results may differ from the reference program's by a relative error of at most 0.024.
Values may be sent and summed in bfloat16 or wider, within the bound.
A program may use at most 128 MiB of HBM per device.

```python
import jax
import jax.numpy as jnp
from jax import lax

LINES = 128
PARTITIONS = 128
CHANNELS = 64
COILS = 16
PHASES = 4
MICRO = 2
CASCADES = 2
READOUT = 16


def set_ends(values, rng, smallest, top_value):
    index_at = [jax.random.randint(jax.random.fold_in(rng, axis), (), 0, length) for axis, length in enumerate(values.shape)]
    widest = values.shape.index(max(values.shape))
    beside = index_at[:widest] + [(index_at[widest] + 1) % values.shape[widest]] + index_at[widest + 1:]
    return values.at[tuple(index_at)].set(smallest).at[tuple(beside)].set(top_value)


def block_scale(rng, dims, pieces, low, largest):
    def one(dim, blocks):
        steps = jax.random.uniform(jax.random.fold_in(jax.random.fold_in(rng, 6), dim), (blocks,), jnp.float32, low / len(pieces), largest / len(pieces))
        return jnp.repeat(jnp.exp(steps), dims[dim] // blocks).reshape((-1,) + (1,) * (len(dims) - dim - 1))

    gain = one(*pieces[0])
    for cut in pieces[1:]:
        gain = gain * one(*cut)
    return gain


def centred(stream_key, extent, width, bound, shards=(), kind=jnp.bfloat16):
    factor_of = block_scale(stream_key, extent, shards, -0.22, 0.18) if shards else 1.0
    entries = jax.random.normal(stream_key, extent, jnp.float32) * width * factor_of
    return jnp.minimum(jnp.maximum(entries, -bound), bound).astype(kind)


def setup_inputs(seed: int = 0) -> dict:
    arg_keys = jax.random.split(jax.random.key(seed), 8)
    return {
        "initial": centred(arg_keys[0], (MICRO, PHASES, READOUT, LINES, 2, PARTITIONS), 1.0, 6.0, ((2, 8),)),
        "coil_maps": centred(arg_keys[1], (MICRO, COILS, READOUT, LINES, 2, PARTITIONS), 0.25, 1.5, ((1, 8), (2, 8))),
        "kspace": centred(arg_keys[2], (MICRO, COILS, PHASES, READOUT, LINES, 2, PARTITIONS), 1.0, 6.0, ((1, 8), (3, 8))),
        "sampled": set_ends((jax.random.randint(arg_keys[3], (COILS, PHASES, LINES, PARTITIONS), 0, 3) < 1).astype(jnp.int32), jax.random.fold_in(arg_keys[3], 1), 0, 1),
        "first_w": centred(arg_keys[4], (CASCADES, 27, 2, CHANNELS), 54 ** -0.5, 0.875, ((0, 2),)),
        "time_w": centred(arg_keys[5], (CASCADES, 3, CHANNELS, CHANNELS), (3 * CHANNELS) ** -0.5, 0.4375, ((0, 2),)),
        "last_w": centred(arg_keys[6], (CASCADES, 27, CHANNELS, 2), (27 * CHANNELS) ** -0.5, 0.15625, ((0, 2),)),
    }


def fourier_table(length, direction):
    positions = jnp.arange(length, dtype=jnp.int32)
    products = positions[:, None] * positions[None, :] % length
    angles = products.astype(jnp.float32) * (2.0 * jnp.pi / length)
    factor = 1.0 / jnp.sqrt(jnp.float32(length))
    return (jnp.cos(angles) * factor, direction * jnp.sin(angles) * factor)

def row_matrix(length, direction):
    cosine_part, sine_part = fourier_table(length, direction)
    blocks = jnp.stack([jnp.stack([cosine_part, -sine_part], -1), jnp.stack([sine_part, cosine_part], -1)], 1)
    return blocks.reshape(2 * length, 2 * length).astype(jnp.bfloat16)

def column_matrix(length, direction):
    cosine_part, sine_part = fourier_table(length, direction)
    blocks = jnp.stack([jnp.stack([cosine_part, sine_part], 1), jnp.stack([-sine_part, cosine_part], 1)], 0)
    return blocks.reshape(2 * length, 2 * length).astype(jnp.bfloat16)

def multiply(coil_map, values, conjugate):
    coil_map = coil_map.astype(jnp.float32)
    values = values.astype(jnp.float32)
    map_real, map_imag = (coil_map[..., 0, :], coil_map[..., 1, :])
    value_real, value_imag = (values[..., 0, :], values[..., 1, :])
    if conjugate:
        return jnp.stack([map_real * value_real + map_imag * value_imag, map_real * value_imag - map_imag * value_real], -2)
    return jnp.stack([map_real * value_real - map_imag * value_imag, map_real * value_imag + map_imag * value_real], -2)

def along_columns(fields, matrix):
    layout = fields.shape
    flattened = fields.reshape(-1, 2 * layout[-1])
    return jnp.dot(flattened, matrix, preferred_element_type=jnp.float32).reshape(layout)

def along_rows(fields, matrix):
    layout = fields.shape
    flattened = fields.reshape(-1, 2 * layout[-3], layout[-1]).astype(jnp.float32)
    result = jnp.einsum('ab,nbz->naz', matrix.astype(jnp.float32), flattened)
    return result.reshape(layout)

def coil_term(image, coil_map, coil_data, coil_mask, tables):
    forward_rows, forward_columns, inverse_rows, inverse_columns = tables
    coil_image = multiply(coil_map[None], image, False).astype(jnp.bfloat16)
    half_done = along_columns(coil_image, forward_columns).astype(jnp.bfloat16)
    spectrum = along_rows(half_done, forward_rows)
    weight = coil_mask.astype(jnp.float32)[:, None, :, None, :]
    mixed = (spectrum + weight * (coil_data.astype(jnp.float32) - spectrum)).astype(jnp.bfloat16)
    back_half = along_rows(mixed, inverse_rows).astype(jnp.bfloat16)
    restored = along_columns(back_half, inverse_columns)
    return multiply(coil_map[None], restored, True)

def lift(padded, weights):
    row_count = padded.shape[1] - 2
    line_count = padded.shape[2] - 2
    part_count = padded.shape[4] - 2
    tap_views = [padded[:, row_shift:row_shift + row_count, line_shift:line_shift + line_count, :, part_shift:part_shift + part_count] for row_shift in range(3) for line_shift in range(3) for part_shift in range(3)]
    stacked = jnp.stack(tap_views, 3)
    stacked = stacked.reshape(stacked.shape[0], row_count, line_count, -1, part_count)
    return jnp.einsum('prlie,io->prloe', stacked.astype(jnp.float32), weights.reshape(-1, weights.shape[-1]).astype(jnp.float32))

def temporal(hidden, weights):
    phase_count = hidden.shape[0]
    padded = jnp.pad(hidden, ((2, 2), (0, 0), (0, 0), (0, 0), (0, 0)))
    total = hidden.astype(jnp.float32)
    for tap_index in range(3):
        window = padded[2 * tap_index:2 * tap_index + phase_count].astype(jnp.float32)
        total = total + jnp.einsum('prlie,io->prloe', window, weights[tap_index].astype(jnp.float32))
    return jax.nn.relu(total).astype(jnp.bfloat16)

def project(edged, weights, base):
    row_count = edged.shape[1] - 2
    line_count = edged.shape[2] - 2
    part_count = edged.shape[4]
    per_tap = jnp.einsum('prlie,tio->prltoe', edged.astype(jnp.float32), weights.astype(jnp.float32))
    per_tap = jnp.pad(per_tap, ((0, 0), (0, 0), (0, 0), (0, 0), (0, 0), (1, 1)))
    total = base.astype(jnp.float32)
    for row_shift in range(3):
        for line_shift in range(3):
            for part_shift in range(3):
                tap_index = 9 * row_shift + 3 * line_shift + part_shift
                total = total + per_tap[:, row_shift:row_shift + row_count, line_shift:line_shift + line_count, tap_index, :, part_shift:part_shift + part_count]
    return total.astype(jnp.bfloat16)

def project_all(edged, weights, base):

    def one_phase(phase_pair):
        return project(phase_pair[0][None], weights, phase_pair[1][None])[0]
    return lax.map(one_phase, (edged, base))

def cascade(image, coil_maps, measured, sampled, first_w, time_w, last_w, tables):

    def add_coil(total, inputs):
        coil_map, coil_data, coil_mask = inputs
        return (total + coil_term(image, coil_map, coil_data, coil_mask, tables), None)
    combined, unused = lax.scan(add_coil, jnp.zeros(image.shape, jnp.float32), (coil_maps, measured, sampled))
    combined = combined.astype(jnp.bfloat16)
    padded = jnp.pad(combined, ((0, 0), (1, 1), (1, 1), (0, 0), (1, 1)))
    hidden = jax.nn.relu(lift(padded, first_w)).astype(jnp.bfloat16)
    mixed_time = temporal(hidden, time_w)
    edged = jnp.pad(mixed_time, ((0, 0), (1, 1), (1, 1), (0, 0), (0, 0)))
    return project_all(edged, last_w, combined)

def reference(initial, coil_maps, kspace, sampled, first_w, time_w, last_w):
    tables = (row_matrix(LINES, -1.0), column_matrix(PARTITIONS, -1.0), row_matrix(LINES, 1.0), column_matrix(PARTITIONS, 1.0))
    outputs_all = []
    for micro_index in range(MICRO):
        image = initial[micro_index]
        outputs_row = []
        for section_index in range(CASCADES):
            image = cascade(image, coil_maps[micro_index], kspace[micro_index], sampled, first_w[section_index], time_w[section_index], last_w[section_index], tables)
            outputs_row.append(image)
        outputs_all.append(jnp.stack(outputs_row))
    return jnp.stack(outputs_all, 1)
```

```python
import functools

import jax
import jax.numpy as jnp
import numpy as np
from jax import lax
from jax.experimental import pallas as pl
from jax.experimental.pallas import tpu as pltpu
from jax.sharding import PartitionSpec as P

MESH = pl.DeviceIdType.MESH
BF = jnp.bfloat16
F32 = jnp.float32
N = 128
ZS = 4
SHARE = N // ZS
WIN = 40
GROUPS = 9


def complex_blocks(direction):
    k = np.arange(N)
    angle = ((k[:, None] * k[None, :]) % N).astype(np.float32) * np.float32(2.0 * np.pi / N)
    factor = np.float32(1.0 / np.sqrt(N))
    cos, sin = np.cos(angle) * factor, direction * np.sin(angle) * factor
    return np.block([[cos, -sin], [sin, cos]]), np.block([[cos, sin], [-sin, cos]])


def constant_tables():
    rows_forward, cols_forward = complex_blocks(-1.0)
    rows_inverse, cols_inverse = complex_blocks(1.0)
    deint = np.zeros((256, 256))
    for c in range(2):
        for l in range(N):
            deint[c * N + l, 2 * l + c] = 1
    window = np.zeros((2 * ZS * WIN, 256))
    for c in range(2):
        for z in range(ZS):
            for w in range(SHARE + 4):
                l = SHARE * z - 2 + w
                if 0 <= l < N:
                    window[(c * ZS + z) * WIN + w, c * N + l] = 1
    shift = [np.zeros((256, 256)) for _ in range(2)]
    for q in range(2):
        for p in range(N):
            if p > 0:
                shift[0][q * N + p - 1, q * N + p] = 1
            if p < N - 1:
                shift[1][q * N + p + 1, q * N + p] = 1
    slabs = np.zeros((GROUPS * 16, 256))
    for g in range(GROUPS):
        for c in range(2):
            for l8 in range(8):
                slabs[g * 16 + c * 8 + l8, c * WIN + 4 * g + l8] = 1
    base = np.zeros((128, 256))
    gather = np.zeros((128, 256))
    final = np.zeros((128, 256))
    for l in range(SHARE):
        for r in range(2):
            for o in range(2):
                mine = 4 * l + 2 * r + o
                base[mine, r * 2 * WIN + o * WIN + 2 + l] = 1
                gather[(r * 2 + o) * SHARE + l, mine] = 1
                final[((l // 16) * 2 + r) * 32 + (l % 16) * 2 + o, mine] = 1
    return {
        "deint": deint,
        "deint_window": window @ deint,
        "rows_forward": rows_forward,
        "cols_forward": cols_forward,
        "cols_inverse": cols_inverse,
        "rows_inverse": window @ rows_inverse,
        "shift0": shift[0],
        "shift2": shift[1],
        "slabs": slabs,
        "base": base,
        "gather": gather,
        "final": final,
    }


def tables_array():
    tables = constant_tables()
    where, parts, at = {}, [], 0
    for name, table in tables.items():
        where[name] = (at, table.shape[0])
        parts.append(table)
        at += table.shape[0]
    return where, np.concatenate(parts, 0).astype(jnp.bfloat16)


WHERE, TABLES = tables_array()


def first_selection():
    pick = np.zeros((4, 144, 54))
    for j in range(4):
        for a in range(3):
            for e in range(3):
                for c in range(2):
                    for t in range(3):
                        pick[j, ((a * 3 + e) * 2 + c) * 8 + j + t, (9 * a + 3 * t + e) * 2 + c] = 1
    return pick


def last_selection():
    pick = np.zeros((24, 2, 4, 27))
    for delta in range(2):
        for e in range(3):
            for par in range(2):
                for row in range(2):
                    for jpar in range(2):
                        for r4 in range(4):
                            c, a = jpar + 2 * delta - par, r4 - row
                            if 0 <= c < 3 and 0 <= a < 3:
                                pick[((delta * 3 + e) * 2 + par) * 2 + row, jpar, r4, 9 * a + 3 * c + e] = 1
    return pick


def prepared(first_w, time_w, last_w):
    first = jnp.einsum(
        "jkx,xo->jok", jnp.asarray(first_selection(), BF), first_w.reshape(54, 64), preferred_element_type=F32
    )
    first = first.reshape(256, 144).astype(BF)
    turned = jnp.swapaxes(time_w, 1, 2)
    eye, none = jnp.eye(64, dtype=BF), jnp.zeros((64, 64), BF)
    time = jnp.concatenate(
        [
            jnp.concatenate([turned[1], turned[2], eye, none], 1),
            jnp.concatenate([turned[0], turned[1], none, eye], 1),
        ],
        0,
    )
    last = jnp.einsum("mjrt,tio->mojri", jnp.asarray(last_selection(), BF), last_w, preferred_element_type=F32)
    return first, time, last.reshape(48, 512).astype(BF)


def dot(a, b):
    return jnp.dot(a, b, preferred_element_type=F32)


def swap_blocks(x):
    return jnp.concatenate(
        [
            jnp.concatenate([x[:N, :N], x[N:, :N]], 1),
            jnp.concatenate([x[:N, N:], x[N:, N:]], 1),
        ],
        0,
    )


def twice(x):
    return jnp.concatenate([x, x], 1)


def kernel(
    tables_in, initial, coil_maps, kspace, sampled, first_in, time_in, last_in,
    out,
    tab, maps_raw, ksp_raw, img_raw, mask,
    first_s, time_s, last_s,
    maps_d, maps_w, ksp_d, img, acc, rs_send, rs_recv, halo, slab, total, outs,
    local_sem, core_send, core_recv, w_send, w_recv, rs_ssem, rs_rsem, h_ssem, h_rsem,
    ag_ssem, ag_rsem, o_ssem, o_rsem,
):
    cas, coil, ro = lax.axis_index("cascade"), lax.axis_index("coil"), lax.axis_index("readout")
    z, core = coil // 2, coil % 2
    hi = ro % 2
    block = 1 - (hi + cas - 2 * hi * cas)
    other_core = (cas, coil + 1 - 2 * core, ro)
    other_cas = (1 - cas, coil, ro)
    other_both = (1 - cas, coil + 1 - 2 * core, ro)
    peers = [(cas, 2 * ((z + d) % ZS) + core, ro) for d in (1, 2, 3)]
    before, after = (1 - cas, coil, ro - 1), (1 - cas, coil, ro + 1)
    has_before, has_after = ro > 0, ro < 7

    def table(name, columns=256):
        at, count = WHERE[name]
        return tab[at:at + count, :columns]

    def local(number, source, target):
        return pltpu.make_async_copy(source, target, local_sem.at[number])

    def remote(source, target, ssem, rsem, device):
        return pltpu.make_async_remote_copy(
            src_ref=source, dst_ref=target, send_sem=ssem, recv_sem=rsem, device_id=device, device_id_type=MESH
        )

    loads = [
        local(0, tables_in, tab),
        local(1, coil_maps.at[block], maps_raw.at[pl.ds(0, 2)]),
        local(2, kspace.at[block, :, :, core], ksp_raw.at[pl.ds(0, 2)]),
        local(3, sampled.at[:, :, core], mask.at[pl.ds(0, 2)]),
        local(4, initial.at[block, :, core], img_raw),
        local(5, first_in, first_s.at[cas]),
        local(6, time_in, time_s.at[cas]),
        local(7, last_in, last_s.at[cas]),
    ]
    for copy in loads:
        copy.start()

    barrier = pltpu.get_barrier_semaphore()
    for device in [other_core, other_cas, other_both, *peers]:
        pl.semaphore_signal(barrier, inc=1, device_id=device, device_id_type=MESH)

    @pl.when(has_before)
    def _():
        pl.semaphore_signal(barrier, inc=1, device_id=before, device_id_type=MESH)

    @pl.when(has_after)
    def _():
        pl.semaphore_signal(barrier, inc=1, device_id=after, device_id_type=MESH)

    pl.semaphore_wait(barrier, 6 + jnp.where(has_before, 1, 0) + jnp.where(has_after, 1, 0))

    exchange = [
        remote(coil_maps.at[block], maps_raw.at[pl.ds(2, 2)], core_send.at[0], core_recv.at[0], other_core),
        remote(kspace.at[block, :, :, 1 - core], ksp_raw.at[pl.ds(2, 2)], core_send.at[1], core_recv.at[1], other_core),
        remote(sampled.at[:, :, 1 - core], mask.at[pl.ds(2, 2)], core_send.at[2], core_recv.at[2], other_core),
    ]
    for copy in exchange:
        copy.start()
    weights = [
        remote(source, target.at[cas], w_send.at[n], w_recv.at[n], other_cas)
        for n, (source, target) in enumerate(((first_in, first_s), (time_in, time_s), (last_in, last_s)))
    ]
    for copy in weights:
        copy.start()
    weights_in = [
        remote(source, target.at[1 - cas], w_send.at[n], w_recv.at[n], other_cas)
        for n, (source, target) in enumerate(((first_in, first_s), (time_in, time_s), (last_in, last_s)))
    ]

    zero_rows = jnp.zeros((2 * WIN, 256), BF)
    for s in range(2):
        @pl.when(ro == 0)
        def _():
            halo[s, 0] = zero_rows
            halo[s, 1] = zero_rows

        @pl.when(ro == 7)
        def _():
            halo[s, 4] = zero_rows
            halo[s, 5] = zero_rows

    def prepare(j):
        both = jnp.concatenate([maps_raw[j, 0], maps_raw[j, 1]], 1)
        maps_d[j] = dot(table("deint"), both)
        maps_w[j] = dot(table("deint_window"), both)
        for r in range(2):
            pair = jnp.concatenate([ksp_raw[j, 0, r], ksp_raw[j, 1, r]], 1)
            ksp_d[j, r] = swap_blocks(dot(table("deint"), pair)).astype(BF)

    def consistency(s, r, j):
        image = img[s, :, r].astype(F32)
        real, imag = image[:, 0].reshape(N, 256), image[:, 1].reshape(N, 256)
        lanes = slice(r * N, r * N + N)
        map_r, map_i = twice(maps_d[j, :N, lanes]), twice(maps_d[j, N:, lanes])
        coil_image = jnp.concatenate([map_r * real - map_i * imag, map_r * imag + map_i * real], 0).astype(BF)
        half = swap_blocks(dot(table("rows_forward"), coil_image).astype(BF))
        spectrum = dot(half, table("cols_forward"))
        taken = twice(mask[j].reshape(256, N)) != 0
        mixed = jnp.where(taken, ksp_d[j, r].astype(F32), spectrum).astype(BF)
        back = swap_blocks(dot(mixed, table("cols_inverse")).astype(BF))
        restored = dot(table("rows_inverse"), back)
        rows = ZS * WIN
        value_r, value_i = restored[:rows], restored[rows:]
        win_r, win_i = twice(maps_w[j, :rows, lanes]), twice(maps_w[j, rows:, lanes])
        return win_r * value_r + win_i * value_i, win_r * value_i - win_i * value_r

    def reduce_copies(s, r):
        return [
            remote(
                rs_send.at[s, r, (z + d) % ZS], rs_recv.at[s, r, d - 1],
                rs_ssem.at[s, r, d - 1], rs_rsem.at[s, r, d - 1], peers[d - 1],
            )
            for d in (1, 2, 3)
        ]

    def data_consistency(s, r):
        rows = ZS * WIN

        def pair(jp, unused):
            if s == 0 and r == 0:
                @pl.when(jp == 1)
                def _():
                    for copy in exchange:
                        copy.wait_recv()
                    prepare(2)
                    prepare(3)
            first_r, first_i = consistency(s, r, 2 * jp)
            second_r, second_i = consistency(s, r, 2 * jp + 1)
            acc[:rows] += first_r + second_r
            acc[rows:] += first_i + second_i
            return unused

        acc[...] = jnp.zeros_like(acc)
        lax.fori_loop(0, 2, pair, 0)
        for share in range(ZS):
            at = share * WIN
            rs_send[s, r, share] = jnp.concatenate(
                [acc[at:at + WIN], acc[rows + at:rows + at + WIN]], 0
            ).astype(BF)
        for copy in reduce_copies(s, r):
            copy.start()

    def halo_copies(s, r):
        return (
            remote(halo.at[s, 2 + r], halo.at[s, 4 + r], h_ssem.at[s, r, 0], h_rsem.at[s, r, 0], before),
            remote(halo.at[s, 2 + r], halo.at[s, r], h_ssem.at[s, r, 1], h_rsem.at[s, r, 1], after),
        )

    def combine(s, r):
        for copy in reduce_copies(s, r):
            copy.wait_recv()
        summed = rs_send[s, r, z].astype(F32)
        for d in range(3):
            summed = summed + rs_recv[s, r, d].astype(F32)
        halo[s, 2 + r] = summed.astype(BF)
        to_before, to_after = halo_copies(s, r)

        @pl.when(has_before)
        def _():
            to_before.start()

        @pl.when(has_after)
        def _():
            to_after.start()

    def denoise(s):
        for r in range(2):
            to_before, to_after = halo_copies(s, r)

            @pl.when(has_after)
            def _():
                to_before.wait_recv()

            @pl.when(has_before)
            def _():
                to_after.wait_recv()

        cells = halo[s].reshape(6 * 2 * WIN, 256)
        for e in range(3):
            moved = cells if e == 1 else dot(cells, table(f"shift{e}")).astype(BF)
            for row in range(6):
                piece = moved[row * 2 * WIN:(row + 1) * 2 * WIN]
                parts = dot(table("slabs", 2 * WIN), piece).astype(BF)
                at = (row * 3 + e) * 16
                for g in range(GROUPS):
                    slab[g, at:at + 16] = parts[16 * g:16 * g + 16]

        if s == 0:
            @pl.when(cas == 1)
            def _():
                for copy in weights_in:
                    copy.wait_recv()
        else:
            @pl.when(cas == 0)
            def _():
                for copy in weights_in:
                    copy.wait_recv()

        row_of = (lax.broadcasted_iota(jnp.int32, (48, 512), 1) // 64) % 4
        dead = ((row_of == 0) & (ro == 0)) | ((row_of == 3) & (ro == 7))
        last = jnp.where(dead, 0.0, last_s[s].astype(F32))
        total[...] = jnp.zeros_like(total)

        def group(g, unused):
            features = []
            for row in range(4):
                hidden = dot(first_s[s], slab[g, 48 * row:48 * row + 144])
                hidden = jnp.maximum(hidden, 0.0).astype(BF)
                for u in range(2):
                    lines = []
                    for j in (2 * u, 2 * u + 1):
                        one = hidden[64 * j:64 * j + 64]
                        lines.append(jnp.concatenate([one[:, :N], one[:, N:]], 0))
                    lines = jnp.concatenate(lines, 1)
                    mixed = dot(time_s[s], jnp.concatenate([lines, lines], 0))
                    features.append(jnp.maximum(mixed, 0.0).astype(BF))
            for u in range(2):
                k = 2 * g + u
                stack = []
                for j in range(2):
                    for row in range(4):
                        one = features[2 * row + u][:, j * N:j * N + N]
                        stack.append(jnp.concatenate([one[:64], one[64:]], 1))
                stack = jnp.concatenate(stack, 0)
                keep0 = jnp.where((k == 0) & (z == 0), 0.0, 1.0)
                keep1 = jnp.where((k == 16) & (z == ZS - 1), 0.0, 1.0)
                weight = jnp.concatenate([last[:, :256] * keep0, last[:, 256:] * keep1], 1).astype(BF)
                result = dot(weight, stack)
                total[k + 1] += result[:24]
                total[k] += result[24:]
            return unused

        lax.fori_loop(0, GROUPS, group, 0)

        taps = [total[1:17, 8 * e:8 * e + 8].reshape(128, 256) for e in range(3)]
        lane = lax.broadcasted_iota(jnp.int32, (128, N), 1)
        halves = []
        for q in range(2):
            at = slice(q * N, q * N + N)
            low = jnp.where(lane == 0, 0.0, pltpu.roll(taps[0][:, at], 1, 1))
            high = jnp.where(lane == N - 1, 0.0, pltpu.roll(taps[2][:, at], N - 1, 1))
            halves.append(low + taps[1][:, at] + high)
        own = jnp.concatenate([halo[s, 2], halo[s, 3]], 0)
        return (dot(table("base", 4 * WIN), own) + jnp.concatenate(halves, 1)).astype(BF)

    def gather_copies(arriving):
        return [
            remote(
                img.at[1, z], img.at[1, (z + ZS - d) % ZS if arriving else z],
                ag_ssem.at[d - 1], ag_rsem.at[d - 1], peers[d - 1],
            )
            for d in (1, 2, 3)
        ]

    def keep_output(s, image):
        ordered = dot(table("final", 128), image).astype(BF)
        for half in range(2):
            for q in range(2):
                for r in range(2):
                    at = (half * 2 + r) * 32
                    outs[s, half, q, r] = ordered[at:at + 32, q * N:q * N + N]

    def near_copies(s):
        return (
            local(8, outs.at[s, core], out.at[block, :, core]),
            remote(outs.at[s, 1 - core], out.at[block, :, core], o_ssem.at[0], o_rsem.at[0], other_core),
        )

    def far_copies(s):
        return (
            remote(outs.at[s, core], out.at[block, :, core], o_ssem.at[1], o_rsem.at[1], other_cas),
            remote(outs.at[s, 1 - core], out.at[block, :, core], o_ssem.at[2], o_rsem.at[2], other_both),
        )

    def send_output(s):
        @pl.when(cas == s)
        def _():
            for copy in near_copies(s):
                copy.start()

        @pl.when(cas != s)
        def _():
            for copy in far_copies(s):
                copy.start()

    for copy in loads[:5]:
        copy.wait()
    for r in range(2):
        pair = jnp.concatenate([img_raw[0, r], img_raw[1, r]], 1)
        plain = dot(table("deint"), pair).astype(BF)
        for share in range(ZS):
            for c in range(2):
                at = c * N + share * SHARE
                img[0, share, r, c] = plain[at:at + SHARE]
    prepare(0)
    prepare(1)
    for copy in loads[5:]:
        copy.wait()

    for s in range(2):
        data_consistency(s, 0)
        data_consistency(s, 1)
        combine(s, 0)
        combine(s, 1)
        image = denoise(s)
        if s == 0:
            shares = dot(table("gather", 128), image).astype(BF)
            for r in range(2):
                for c in range(2):
                    at = (2 * r + c) * SHARE
                    img[1, z, r, c] = shares[at:at + SHARE]
            for copy in gather_copies(False):
                copy.start()
        keep_output(s, image)
        send_output(s)
        if s == 0:
            for copy in gather_copies(True):
                copy.wait_recv()

    for copy in exchange + weights + gather_copies(False):
        copy.wait_send()
    for s in range(2):
        for r in range(2):
            for copy in reduce_copies(s, r):
                copy.wait_send()
            to_before, to_after = halo_copies(s, r)

            @pl.when(has_before)
            def _():
                to_before.wait_send()

            @pl.when(has_after)
            def _():
                to_after.wait_send()

        @pl.when(cas == s)
        def _():
            keep, give = near_copies(s)
            keep.wait()
            give.wait_send()

        @pl.when(cas != s)
        def _():
            for copy in far_copies(s):
                copy.wait_send()

    arriving = (
        remote(outs.at[0, 0], out.at[block, :, 1 - core], o_ssem.at[0], o_rsem.at[0], other_core),
        remote(outs.at[0, 0], out.at[1 - block, :, core], o_ssem.at[1], o_rsem.at[1], other_cas),
        remote(outs.at[0, 0], out.at[1 - block, :, 1 - core], o_ssem.at[2], o_rsem.at[2], other_both),
    )
    for copy in arriving:
        copy.wait_recv()


def per_device(initial, coil_maps, kspace, sampled, first_w, time_w, last_w):
    first, time, last = prepared(first_w[0], time_w[0], last_w[0])
    dma = pltpu.SemaphoreType.DMA
    out = pl.pallas_call(
        kernel,
        out_shape=jax.ShapeDtypeStruct((2, 2, 2, 2, 32, N), BF),
        in_specs=[pl.BlockSpec(memory_space=pl.ANY)] * 8,
        out_specs=pl.BlockSpec(memory_space=pl.ANY),
        scratch_shapes=[
            pltpu.VMEM(TABLES.shape, BF),
            pltpu.VMEM((4, 2, 256, N), BF),
            pltpu.VMEM((4, 2, 2, 256, N), BF),
            pltpu.VMEM((2, 2, 256, N), BF),
            pltpu.VMEM((4, 2, N, N), jnp.int32),
            pltpu.VMEM((2, 256, 144), BF),
            pltpu.VMEM((2, 128, 256), BF),
            pltpu.VMEM((2, 48, 512), BF),
            pltpu.VMEM((4, 256, 256), F32),
            pltpu.VMEM((4, 2 * ZS * WIN, 256), F32),
            pltpu.VMEM((4, 2, 256, 256), BF),
            pltpu.VMEM((2, ZS, 2, 2, SHARE, 256), BF),
            pltpu.VMEM((2 * ZS * WIN, 256), F32),
            pltpu.VMEM((2, 2, ZS, 2 * WIN, 256), BF),
            pltpu.VMEM((2, 2, 3, 2 * WIN, 256), BF),
            pltpu.VMEM((2, 6, 2 * WIN, 256), BF),
            pltpu.VMEM((GROUPS, 288, 256), BF),
            pltpu.VMEM((20, 24, 256), F32),
            pltpu.VMEM((2, 2, 2, 2, 32, N), BF),
            dma((9,)),
            dma((3,)),
            dma((3,)),
            dma((3,)),
            dma((3,)),
            dma((2, 2, 3)),
            dma((2, 2, 3)),
            dma((2, 2, 2)),
            dma((2, 2, 2)),
            dma((3,)),
            dma((3,)),
            dma((3,)),
            dma((3,)),
        ],
        compiler_params=pltpu.CompilerParams(
            collective_id=0, has_side_effects=True, vmem_limit_bytes=48 * 1024 * 1024
        ),
    )(
        jnp.asarray(TABLES),
        initial.reshape(2, 2, 2, 2, 256, N),
        coil_maps.reshape(2, 2, 2, 256, N),
        kspace.reshape(2, 2, 2, 2, 2, 256, N),
        sampled.reshape(2, 2, 2, N, N),
        first,
        time,
        last,
    )
    return out.reshape(1, 2, 4, 2, 16, 2, N)


def solution(mesh):
    in_specs = (
        P(None, None, "readout", None, None, None),
        P(None, "coil", "readout", None, None, None),
        P(None, "coil", None, "readout", None, None, None),
        P("coil", None, None, None),
        P("cascade", None, None, None),
        P("cascade", None, None, None),
        P("cascade", None, None, None),
    )
    out_specs = P("cascade", None, None, "readout", "coil", None, None)
    return jax.shard_map(per_device, mesh=mesh, in_specs=in_specs, out_specs=out_specs, check_vma=False)
```

```python
import functools

import jax
import jax.numpy as jnp
import numpy as np
from jax import lax
from jax.experimental import pallas as pl
from jax.experimental.pallas import tpu as pltpu
from jax.sharding import PartitionSpec as P

MESH = pl.DeviceIdType.MESH
BF = jnp.bfloat16
F32 = jnp.float32
N = 128
ZS = 4
SHARE = N // ZS
WIN = 40
GROUPS = 9


def complex_blocks(direction):
    k = np.arange(N)
    angle = ((k[:, None] * k[None, :]) % N).astype(np.float32) * np.float32(2.0 * np.pi / N)
    factor = np.float32(1.0 / np.sqrt(N))
    cos, sin = np.cos(angle) * factor, direction * np.sin(angle) * factor
    return np.block([[cos, -sin], [sin, cos]]), np.block([[cos, sin], [-sin, cos]])


def first_selection():
    pick = np.zeros((4, 64, 144))
    for j in range(4):
        for a in range(3):
            for e in range(3):
                for c in range(2):
                    for t in range(3):
                        pick[j, (9 * a + 3 * t + e) * 2 + c, ((a * 3 + e) * 2 + c) * 8 + j + t] = 1
    return pick


def last_selection():
    pick = np.zeros((2, 2, 2, 3, 2, 2, 2, 2, 64))
    for delta in range(2):
        for e in range(3):
            for par in range(2):
                for row in range(2):
                    for jpar in range(2):
                        for r4 in range(4):
                            c, a = jpar + 2 * delta - par, r4 - row
                            if 0 <= c < 3 and 0 <= a < 3:
                                for o in range(2):
                                    x = (9 * a + 3 * c + e) * 2 + o
                                    pick[jpar, r4 // 2, delta, e, par, row, o, r4 % 2, x] = 1
    return pick


def constant_tables():
    rows_forward, cols_forward = complex_blocks(-1.0)
    rows_inverse, cols_inverse = complex_blocks(1.0)
    deint = np.zeros((256, 256))
    for c in range(2):
        for l in range(N):
            deint[c * N + l, 2 * l + c] = 1
    window = np.zeros((2 * ZS * WIN, 256))
    for c in range(2):
        for z in range(ZS):
            for w in range(SHARE + 4):
                l = SHARE * z - 2 + w
                if 0 <= l < N:
                    window[(c * ZS + z) * WIN + w, c * N + l] = 1
    shift = [np.zeros((256, 256)) for _ in range(2)]
    for q in range(2):
        for p in range(N):
            if p > 0:
                shift[0][q * N + p - 1, q * N + p] = 1
            if p < N - 1:
                shift[1][q * N + p + 1, q * N + p] = 1
    slabs = np.zeros((GROUPS * 16, 256))
    for g in range(GROUPS):
        for c in range(2):
            for l8 in range(8):
                slabs[g * 16 + c * 8 + l8, c * WIN + 4 * g + l8] = 1
    base = np.zeros((128, 256))
    gather = np.zeros((128, 256))
    final = np.zeros((128, 256))
    for l in range(SHARE):
        for r in range(2):
            for o in range(2):
                mine = 4 * l + 2 * r + o
                base[mine, r * 2 * WIN + o * WIN + 2 + l] = 1
                gather[(r * 2 + o) * SHARE + l, mine] = 1
                final[((l // 16) * 2 + r) * 32 + (l % 16) * 2 + o, mine] = 1
    return {
        "deint": deint,
        "deint_window": window @ deint,
        "rows_forward": rows_forward,
        "cols_forward": cols_forward,
        "cols_inverse": cols_inverse,
        "rows_inverse": window @ rows_inverse,
        "shift0": shift[0],
        "shift2": shift[1],
        "slabs": slabs,
        "base": base,
        "gather": gather,
        "final": final,
        "eye": np.eye(128),
        "first": first_selection().reshape(4 * 64, 144),
        "last": last_selection().reshape(4 * 48, 128),
    }


def tables_array():
    tables = constant_tables()
    where, parts, at = {}, [], 0
    for name, table in tables.items():
        where[name] = (at, table.shape[0])
        parts.append(np.pad(table, ((0, 0), (0, 256 - table.shape[1]))))
        at += table.shape[0]
    return where, np.concatenate(parts, 0).astype(jnp.bfloat16)


WHERE, TABLES = tables_array()


def dot(a, b):
    return jnp.dot(a, b, preferred_element_type=F32)


def dot_turned(a, b):
    return lax.dot_general(a, b, (((1,), (1,)), ((), ())), preferred_element_type=F32)


def swap_blocks(x):
    return jnp.concatenate(
        [
            jnp.concatenate([x[:N, :N], x[N:, :N]], 1),
            jnp.concatenate([x[:N, N:], x[N:, N:]], 1),
        ],
        0,
    )


def twice(x):
    return jnp.concatenate([x, x], 1)


def kernel(
    tables_in, initial, coil_maps, kspace, sampled, first_in, time_in, last_in,
    out,
    tab, maps_raw, ksp_raw, img_raw, mask,
    first_r, time_r, last_r, first_s, time_s, last_s,
    maps_d, maps_w, ksp_d, img, acc, rs_send, rs_recv, halo, slab, total, outs,
    local_sem, core_send, core_recv, w_send, w_recv, rs_ssem, rs_rsem, h_ssem, h_rsem,
    ag_ssem, ag_rsem, o_ssem, o_rsem,
):
    cas, coil, ro = lax.axis_index("cascade"), lax.axis_index("coil"), lax.axis_index("readout")
    z, core = coil // 2, coil % 2
    hi = ro % 2
    block = 1 - (hi + cas - 2 * hi * cas)
    other_core = (cas, coil + 1 - 2 * core, ro)
    other_cas = (1 - cas, coil, ro)
    other_both = (1 - cas, coil + 1 - 2 * core, ro)
    peers = [(cas, 2 * ((z + d) % ZS) + core, ro) for d in (1, 2, 3)]
    before, after = (1 - cas, coil, ro - 1), (1 - cas, coil, ro + 1)
    has_before, has_after = ro > 0, ro < 7

    def table(name, columns=256):
        at, count = WHERE[name]
        return tab[at:at + count, :columns]

    def local(number, source, target):
        return pltpu.make_async_copy(source, target, local_sem.at[number])

    def remote(source, target, ssem, rsem, device):
        return pltpu.make_async_remote_copy(
            src_ref=source, dst_ref=target, send_sem=ssem, recv_sem=rsem, device_id=device, device_id_type=MESH
        )

    loads = [
        local(0, tables_in, tab),
        local(1, coil_maps.at[block], maps_raw.at[pl.ds(0, 2)]),
        local(2, kspace.at[block, :, :, core], ksp_raw.at[pl.ds(0, 2)]),
        local(3, sampled.at[:, :, core], mask.at[pl.ds(0, 2)]),
        local(4, initial.at[block, :, core], img_raw),
        local(5, first_in, first_r.at[cas]),
        local(6, time_in, time_r.at[cas]),
        local(7, last_in, last_r.at[cas]),
    ]
    for copy in loads:
        copy.start()

    barrier = pltpu.get_barrier_semaphore()
    for device in [other_core, other_cas, other_both, *peers]:
        pl.semaphore_signal(barrier, inc=1, device_id=device, device_id_type=MESH)

    @pl.when(has_before)
    def _():
        pl.semaphore_signal(barrier, inc=1, device_id=before, device_id_type=MESH)

    @pl.when(has_after)
    def _():
        pl.semaphore_signal(barrier, inc=1, device_id=after, device_id_type=MESH)

    pl.semaphore_wait(barrier, 6 + jnp.where(has_before, 1, 0) + jnp.where(has_after, 1, 0))

    exchange = [
        remote(coil_maps.at[block], maps_raw.at[pl.ds(2, 2)], core_send.at[0], core_recv.at[0], other_core),
        remote(kspace.at[block, :, :, 1 - core], ksp_raw.at[pl.ds(2, 2)], core_send.at[1], core_recv.at[1], other_core),
        remote(sampled.at[:, :, 1 - core], mask.at[pl.ds(2, 2)], core_send.at[2], core_recv.at[2], other_core),
    ]
    for copy in exchange:
        copy.start()
    weights = [
        remote(source, target.at[cas], w_send.at[n], w_recv.at[n], other_cas)
        for n, (source, target) in enumerate(((first_in, first_r), (time_in, time_r), (last_in, last_r)))
    ]
    for copy in weights:
        copy.start()
    weights_in = [
        remote(source, target.at[1 - cas], w_send.at[n], w_recv.at[n], other_cas)
        for n, (source, target) in enumerate(((first_in, first_r), (time_in, time_r), (last_in, last_r)))
    ]

    zero_rows = jnp.zeros((2 * WIN, 256), BF)
    for s in range(2):
        @pl.when(ro == 0)
        def _():
            halo[s, 0] = zero_rows
            halo[s, 1] = zero_rows

        @pl.when(ro == 7)
        def _():
            halo[s, 4] = zero_rows
            halo[s, 5] = zero_rows

    def prepare(j):
        both = jnp.concatenate([maps_raw[j, 0], maps_raw[j, 1]], 1)
        maps_d[j] = dot(table("deint"), both)
        maps_w[j] = dot(table("deint_window"), both)
        for r in range(2):
            pair = jnp.concatenate([ksp_raw[j, 0, r], ksp_raw[j, 1, r]], 1)
            ksp_d[j, r] = swap_blocks(dot(table("deint"), pair)).astype(BF)

    def consistency(s, r, j):
        image = img[s, :, r].astype(F32)
        real, imag = image[:, 0].reshape(N, 256), image[:, 1].reshape(N, 256)
        lanes = slice(r * N, r * N + N)
        map_r, map_i = twice(maps_d[j, :N, lanes]), twice(maps_d[j, N:, lanes])
        coil_image = jnp.concatenate([map_r * real - map_i * imag, map_r * imag + map_i * real], 0).astype(BF)
        half = swap_blocks(dot(table("rows_forward"), coil_image).astype(BF))
        spectrum = dot(half, table("cols_forward"))
        taken = twice(mask[j].reshape(256, N)) != 0
        mixed = jnp.where(taken, ksp_d[j, r].astype(F32), spectrum).astype(BF)
        back = swap_blocks(dot(mixed, table("cols_inverse")).astype(BF))
        restored = dot(table("rows_inverse"), back)
        rows = ZS * WIN
        value_r, value_i = restored[:rows], restored[rows:]
        win_r, win_i = twice(maps_w[j, :rows, lanes]), twice(maps_w[j, rows:, lanes])
        return win_r * value_r + win_i * value_i, win_r * value_i - win_i * value_r

    def reduce_copies(s, r):
        return [
            remote(
                rs_send.at[s, r, (z + d) % ZS], rs_recv.at[s, r, d - 1],
                rs_ssem.at[s, r, d - 1], rs_rsem.at[s, r, d - 1], peers[d - 1],
            )
            for d in (1, 2, 3)
        ]

    def data_consistency(s, r):
        rows = ZS * WIN

        def pair(jp, unused):
            if s == 0 and r == 0:
                @pl.when(jp == 1)
                def _():
                    for copy in exchange:
                        copy.wait_recv()
                    prepare(2)
                    prepare(3)
            first_r, first_i = consistency(s, r, 2 * jp)
            second_r, second_i = consistency(s, r, 2 * jp + 1)
            acc[:rows] += first_r + second_r
            acc[rows:] += first_i + second_i
            return unused

        acc[...] = jnp.zeros_like(acc)
        lax.fori_loop(0, 2, pair, 0)
        for share in range(ZS):
            at = share * WIN
            rs_send[s, r, share] = jnp.concatenate(
                [acc[at:at + WIN], acc[rows + at:rows + at + WIN]], 0
            ).astype(BF)
        for copy in reduce_copies(s, r):
            copy.start()

    def halo_copies(s, r):
        return (
            remote(halo.at[s, 2 + r], halo.at[s, 4 + r], h_ssem.at[s, r, 0], h_rsem.at[s, r, 0], before),
            remote(halo.at[s, 2 + r], halo.at[s, r], h_ssem.at[s, r, 1], h_rsem.at[s, r, 1], after),
        )

    def combine(s, r):
        for copy in reduce_copies(s, r):
            copy.wait_recv()
        summed = rs_send[s, r, z].astype(F32)
        for d in range(3):
            summed = summed + rs_recv[s, r, d].astype(F32)
        halo[s, 2 + r] = summed.astype(BF)
        to_before, to_after = halo_copies(s, r)

        @pl.when(has_before)
        def _():
            to_before.start()

        @pl.when(has_after)
        def _():
            to_after.start()

    def weights_of(s):
        @pl.when(cas != s)
        def _():
            for copy in weights_in:
                copy.wait_recv()

        eye = table("eye", 128)
        small = table("eye", 64)[:64]
        rows = dot_turned(small, first_r[s].reshape(54, 64)).astype(BF)
        for j in range(4):
            at = WHERE["first"][0] + 64 * j
            first_s[64 * j:64 * j + 64] = dot(rows, tab[at:at + 54, :144]).astype(BF)
        steps = time_r[s]
        time_s[:64, :N] = dot_turned(small, steps[64:]).astype(BF)
        time_s[64:, :N] = dot_turned(small, steps[:128]).astype(BF)
        time_s[:, N:] = eye
        taps = last_r[s].reshape(54, 64)
        low, high = dot(taps, eye[:64]).astype(BF), dot(taps, eye[64:]).astype(BF)
        lane = lax.broadcasted_iota(jnp.int32, (48, N), 1)
        for n in range(4):
            at = WHERE["last"][0] + 48 * n
            part = dot(tab[at:at + 48, :54], low) + dot(tab[at:at + 48, 64:118], high)
            edge = (lane < 64) & (ro == 0) if n % 2 == 0 else (lane >= 64) & (ro == 7)
            last_s[:, N * n:N * n + N] = jnp.where(edge, 0.0, part)

    def denoise(s):
        for r in range(2):
            to_before, to_after = halo_copies(s, r)

            @pl.when(has_after)
            def _():
                to_before.wait_recv()

            @pl.when(has_before)
            def _():
                to_after.wait_recv()

        cells = halo[s].reshape(6 * 2 * WIN, 256)
        for e in range(3):
            moved = cells if e == 1 else dot(cells, table(f"shift{e}")).astype(BF)
            for row in range(6):
                piece = moved[row * 2 * WIN:(row + 1) * 2 * WIN]
                parts = dot(table("slabs", 2 * WIN), piece).astype(BF)
                at = (row * 3 + e) * 16
                for g in range(GROUPS):
                    slab[g, at:at + 16] = parts[16 * g:16 * g + 16]

        total[...] = jnp.zeros_like(total)

        def group(g, unused):
            last = last_s[...]
            features = []
            for row in range(4):
                hidden = dot(first_s[...], slab[g, 48 * row:48 * row + 144])
                hidden = jnp.maximum(hidden, 0.0).astype(BF)
                for u in range(2):
                    lines = []
                    for j in (2 * u, 2 * u + 1):
                        one = hidden[64 * j:64 * j + 64]
                        lines.append(jnp.concatenate([one[:, :N], one[:, N:]], 0))
                    lines = jnp.concatenate(lines, 1)
                    mixed = dot(time_s[...], jnp.concatenate([lines, lines], 0))
                    features.append(jnp.maximum(mixed, 0.0).astype(BF))
            for u in range(2):
                k = 2 * g + u
                stack = []
                for j in range(2):
                    for row in range(4):
                        one = features[2 * row + u][:, j * N:j * N + N]
                        stack.append(jnp.concatenate([one[:64], one[64:]], 1))
                stack = jnp.concatenate(stack, 0)
                keep0 = jnp.where((k == 0) & (z == 0), 0.0, 1.0)
                keep1 = jnp.where((k == 16) & (z == ZS - 1), 0.0, 1.0)
                weight = jnp.concatenate([last[:, :256] * keep0, last[:, 256:] * keep1], 1).astype(BF)
                result = dot(weight, stack)
                total[k + 1] += result[:24]
                total[k] += result[24:]
            return unused

        lax.fori_loop(0, GROUPS, group, 0)

        taps = [total[1:17, 8 * e:8 * e + 8].reshape(128, 256) for e in range(3)]
        lane = lax.broadcasted_iota(jnp.int32, (128, N), 1)
        halves = []
        for q in range(2):
            at = slice(q * N, q * N + N)
            low = jnp.where(lane == 0, 0.0, pltpu.roll(taps[0][:, at], 1, 1))
            high = jnp.where(lane == N - 1, 0.0, pltpu.roll(taps[2][:, at], N - 1, 1))
            halves.append(low + taps[1][:, at] + high)
        own = jnp.concatenate([halo[s, 2], halo[s, 3]], 0)
        return (dot(table("base", 4 * WIN), own) + jnp.concatenate(halves, 1)).astype(BF)

    def gather_copies(arriving):
        return [
            remote(
                img.at[1, z], img.at[1, (z + ZS - d) % ZS if arriving else z],
                ag_ssem.at[d - 1], ag_rsem.at[d - 1], peers[d - 1],
            )
            for d in (1, 2, 3)
        ]

    def keep_output(s, image):
        ordered = dot(table("final", 128), image).astype(BF)
        for half in range(2):
            for q in range(2):
                for r in range(2):
                    at = (half * 2 + r) * 32
                    outs[s, half, q, r] = ordered[at:at + 32, q * N:q * N + N]

    def near_copies(s):
        return (
            local(8, outs.at[s, core], out.at[block, :, core]),
            remote(outs.at[s, 1 - core], out.at[block, :, core], o_ssem.at[0], o_rsem.at[0], other_core),
        )

    def far_copies(s):
        return (
            remote(outs.at[s, core], out.at[block, :, core], o_ssem.at[1], o_rsem.at[1], other_cas),
            remote(outs.at[s, 1 - core], out.at[block, :, core], o_ssem.at[2], o_rsem.at[2], other_both),
        )

    def send_output(s):
        @pl.when(cas == s)
        def _():
            for copy in near_copies(s):
                copy.start()

        @pl.when(cas != s)
        def _():
            for copy in far_copies(s):
                copy.start()

    for copy in loads[:5]:
        copy.wait()
    for r in range(2):
        pair = jnp.concatenate([img_raw[0, r], img_raw[1, r]], 1)
        plain = dot(table("deint"), pair).astype(BF)
        for share in range(ZS):
            for c in range(2):
                at = c * N + share * SHARE
                img[0, share, r, c] = plain[at:at + SHARE]
    prepare(0)
    prepare(1)
    for copy in loads[5:]:
        copy.wait()

    for s in range(2):
        data_consistency(s, 0)
        data_consistency(s, 1)
        weights_of(s)
        combine(s, 0)
        combine(s, 1)
        image = denoise(s)
        if s == 0:
            shares = dot(table("gather", 128), image).astype(BF)
            for r in range(2):
                for c in range(2):
                    at = (2 * r + c) * SHARE
                    img[1, z, r, c] = shares[at:at + SHARE]
            for copy in gather_copies(False):
                copy.start()
        keep_output(s, image)
        send_output(s)
        if s == 0:
            for copy in gather_copies(True):
                copy.wait_recv()

    for copy in exchange + weights + gather_copies(False):
        copy.wait_send()
    for s in range(2):
        for r in range(2):
            for copy in reduce_copies(s, r):
                copy.wait_send()
            to_before, to_after = halo_copies(s, r)

            @pl.when(has_before)
            def _():
                to_before.wait_send()

            @pl.when(has_after)
            def _():
                to_after.wait_send()

        @pl.when(cas == s)
        def _():
            keep, give = near_copies(s)
            keep.wait()
            give.wait_send()

        @pl.when(cas != s)
        def _():
            for copy in far_copies(s):
                copy.wait_send()

    arriving = (
        remote(outs.at[0, 0], out.at[block, :, 1 - core], o_ssem.at[0], o_rsem.at[0], other_core),
        remote(outs.at[0, 0], out.at[1 - block, :, core], o_ssem.at[1], o_rsem.at[1], other_cas),
        remote(outs.at[0, 0], out.at[1 - block, :, 1 - core], o_ssem.at[2], o_rsem.at[2], other_both),
    )
    for copy in arriving:
        copy.wait_recv()


def per_device(initial, coil_maps, kspace, sampled, first_w, time_w, last_w):
    dma = pltpu.SemaphoreType.DMA
    out = pl.pallas_call(
        kernel,
        out_shape=jax.ShapeDtypeStruct((2, 2, 2, 2, 32, N), BF),
        in_specs=[pl.BlockSpec(memory_space=pl.ANY)] * 8,
        out_specs=pl.BlockSpec(memory_space=pl.ANY),
        scratch_shapes=[
            pltpu.VMEM(TABLES.shape, BF),
            pltpu.VMEM((4, 2, 256, N), BF),
            pltpu.VMEM((4, 2, 2, 256, N), BF),
            pltpu.VMEM((2, 2, 256, N), BF),
            pltpu.VMEM((4, 2, N, N), jnp.int32),
            pltpu.VMEM((2, 27, 2, 64), BF),
            pltpu.VMEM((2, 192, 64), BF),
            pltpu.VMEM((2, 27, 2, 64), BF),
            pltpu.VMEM((256, 144), BF),
            pltpu.VMEM((128, 256), BF),
            pltpu.VMEM((48, 512), F32),
            pltpu.VMEM((4, 256, 256), F32),
            pltpu.VMEM((4, 2 * ZS * WIN, 256), F32),
            pltpu.VMEM((4, 2, 256, 256), BF),
            pltpu.VMEM((2, ZS, 2, 2, SHARE, 256), BF),
            pltpu.VMEM((2 * ZS * WIN, 256), F32),
            pltpu.VMEM((2, 2, ZS, 2 * WIN, 256), BF),
            pltpu.VMEM((2, 2, 3, 2 * WIN, 256), BF),
            pltpu.VMEM((2, 6, 2 * WIN, 256), BF),
            pltpu.VMEM((GROUPS, 288, 256), BF),
            pltpu.VMEM((20, 24, 256), F32),
            pltpu.VMEM((2, 2, 2, 2, 32, N), BF),
            dma((9,)),
            dma((3,)),
            dma((3,)),
            dma((3,)),
            dma((3,)),
            dma((2, 2, 3)),
            dma((2, 2, 3)),
            dma((2, 2, 2)),
            dma((2, 2, 2)),
            dma((3,)),
            dma((3,)),
            dma((3,)),
            dma((3,)),
        ],
        compiler_params=pltpu.CompilerParams(
            collective_id=0, has_side_effects=True, vmem_limit_bytes=60_000_000
        ),
    )(
        jnp.asarray(TABLES),
        initial.reshape(2, 2, 2, 2, 256, N),
        coil_maps.reshape(2, 2, 2, 256, N),
        kspace.reshape(2, 2, 2, 2, 2, 256, N),
        sampled.reshape(2, 2, 2, N, N),
        first_w[0],
        time_w[0].reshape(192, 64),
        jnp.swapaxes(last_w[0], 1, 2),
    )
    return out.reshape(1, 2, 4, 2, 16, 2, N)


def solution(mesh):
    in_specs = (
        P(None, None, "readout", None, None, None),
        P(None, "coil", "readout", None, None, None),
        P(None, "coil", None, "readout", None, None, None),
        P("coil", None, None, None),
        P("cascade", None, None, None),
        P("cascade", None, None, None),
        P("cascade", None, None, None),
    )
    out_specs = P("cascade", None, None, "readout", "coil", None, None)
    return jax.shard_map(per_device, mesh=mesh, in_specs=in_specs, out_specs=out_specs, check_vma=False)
```

```python
import functools

import jax
import jax.numpy as jnp
import numpy as np
from jax import lax
from jax.experimental import pallas as pl
from jax.experimental.pallas import tpu as pltpu
from jax.sharding import PartitionSpec as P

MESH = pl.DeviceIdType.MESH
BF = jnp.bfloat16
F32 = jnp.float32
N = 128
ZS = 4
SHARE = N // ZS
WIN = 40
GROUPS = 9


def complex_blocks(direction):
    k = np.arange(N)
    angle = ((k[:, None] * k[None, :]) % N).astype(np.float32) * np.float32(2.0 * np.pi / N)
    factor = np.float32(1.0 / np.sqrt(N))
    cos, sin = np.cos(angle) * factor, direction * np.sin(angle) * factor
    return np.block([[cos, -sin], [sin, cos]]), np.block([[cos, sin], [-sin, cos]])


def first_selection():
    pick = np.zeros((4, 64, 144))
    for j in range(4):
        for a in range(3):
            for e in range(3):
                for c in range(2):
                    for t in range(3):
                        pick[j, (9 * a + 3 * t + e) * 2 + c, ((a * 3 + e) * 2 + c) * 8 + j + t] = 1
    return pick


def last_selection():
    pick = np.zeros((2, 3, 2, 3, 4, 2, 2, 64))
    for a in range(3):
        for delta in range(2):
            for e in range(3):
                for line in range(4):
                    for j in range(4):
                        c = j + 4 * delta - line
                        if 0 <= c < 3:
                            for o in range(2):
                                pick[j // 2, 2 - a, delta, e, line, o, j % 2, (9 * a + 3 * c + e) * 2 + o] = 1
    return pick


def constant_tables():
    rows_forward, cols_forward = complex_blocks(-1.0)
    rows_inverse, cols_inverse = complex_blocks(1.0)
    deint = np.zeros((256, 256))
    for c in range(2):
        for l in range(N):
            deint[c * N + l, 2 * l + c] = 1
    window = np.zeros((2 * ZS * WIN, 256))
    for c in range(2):
        for z in range(ZS):
            for w in range(SHARE + 4):
                l = SHARE * z - 2 + w
                if 0 <= l < N:
                    window[(c * ZS + z) * WIN + w, c * N + l] = 1
    shift = [np.zeros((256, 256)) for _ in range(2)]
    for q in range(2):
        for p in range(N):
            if p > 0:
                shift[0][q * N + p - 1, q * N + p] = 1
            if p < N - 1:
                shift[1][q * N + p + 1, q * N + p] = 1
    slabs = np.zeros((GROUPS * 16, 256))
    for g in range(GROUPS):
        for c in range(2):
            for l8 in range(8):
                slabs[g * 16 + c * 8 + l8, c * WIN + 4 * g + l8] = 1
    base = np.zeros((64, 256))
    gather = np.zeros((64, 256))
    for l in range(SHARE):
        for o in range(2):
            base[2 * l + o, o * WIN + 2 + l] = 1
            gather[o * SHARE + l, 2 * l + o] = 1
    return {
        "deint": deint,
        "deint_window": window @ deint,
        "rows_forward": rows_forward,
        "cols_forward": cols_forward,
        "cols_inverse": cols_inverse,
        "rows_inverse": window @ rows_inverse,
        "shift0": shift[0],
        "shift2": shift[1],
        "slabs": slabs,
        "base": base,
        "gather": gather,
        "eye": np.eye(128),
        "first": first_selection().reshape(4 * 64, 144),
        "last": last_selection().reshape(2 * 144, 128),
    }


def tables_array():
    tables = constant_tables()
    where, parts, at = {}, [], 0
    for name, table in tables.items():
        where[name] = (at, table.shape[0])
        parts.append(np.pad(table, ((0, 0), (0, 256 - table.shape[1]))))
        at += table.shape[0]
    return where, np.concatenate(parts, 0).astype(jnp.bfloat16)


WHERE, TABLES = tables_array()


def dot(a, b):
    return jnp.dot(a, b, preferred_element_type=F32)


def dot_turned(a, b):
    return lax.dot_general(a, b, (((1,), (1,)), ((), ())), preferred_element_type=F32)


def swap_blocks(x):
    return jnp.concatenate(
        [
            jnp.concatenate([x[:N, :N], x[N:, :N]], 1),
            jnp.concatenate([x[:N, N:], x[N:, N:]], 1),
        ],
        0,
    )


def twice(x):
    return jnp.concatenate([x, x], 1)


def kernel(
    tables_in, initial, coil_maps, kspace, sampled, first_in, time_in, last_in,
    out,
    tab, maps_raw, ksp_raw, img_raw, mask,
    first_r, time_r, last_r, first_s, time_s, last_s,
    maps_d, maps_w, ksp_d, img, acc, rs_send, rs_recv, halo, slab, total, outs,
    local_sem, core_send, core_recv, w_send, w_recv, rs_ssem, rs_rsem, h_ssem, h_rsem,
    ag_ssem, ag_rsem, o_ssem, o_rsem,
):
    cas, coil, ro = lax.axis_index("cascade"), lax.axis_index("coil"), lax.axis_index("readout")
    z, core = coil // 2, coil % 2
    hi = ro % 2
    block = 1 - (hi + cas - 2 * hi * cas)
    other_core = (cas, coil + 1 - 2 * core, ro)
    other_cas = (1 - cas, coil, ro)
    other_both = (1 - cas, coil + 1 - 2 * core, ro)
    peers = [(cas, 2 * ((z + d) % ZS) + core, ro) for d in (1, 2, 3)]
    before, after = (1 - cas, coil, ro - 1), (1 - cas, coil, ro + 1)
    has_before, has_after = ro > 0, ro < 7

    def table(name, columns=256):
        at, count = WHERE[name]
        return tab[at:at + count, :columns]

    def local(number, source, target):
        return pltpu.make_async_copy(source, target, local_sem.at[number])

    def remote(source, target, ssem, rsem, device):
        return pltpu.make_async_remote_copy(
            src_ref=source, dst_ref=target, send_sem=ssem, recv_sem=rsem, device_id=device, device_id_type=MESH
        )

    loads = [
        local(0, tables_in, tab),
        local(1, coil_maps.at[block], maps_raw.at[pl.ds(0, 2)]),
        local(2, kspace.at[block, :, :, core], ksp_raw.at[pl.ds(0, 2)]),
        local(3, sampled.at[:, :, core], mask.at[pl.ds(0, 2)]),
        local(4, initial.at[block, :, core], img_raw),
        local(5, first_in, first_r.at[cas]),
        local(6, time_in, time_r.at[cas]),
        local(7, last_in, last_r.at[cas]),
    ]
    for copy in loads:
        copy.start()

    barrier = pltpu.get_barrier_semaphore()
    for device in [other_core, other_cas, other_both, *peers]:
        pl.semaphore_signal(barrier, inc=1, device_id=device, device_id_type=MESH)

    @pl.when(has_before)
    def _():
        pl.semaphore_signal(barrier, inc=1, device_id=before, device_id_type=MESH)

    @pl.when(has_after)
    def _():
        pl.semaphore_signal(barrier, inc=1, device_id=after, device_id_type=MESH)

    exchange = [remote(sampled.at[:, :, 1 - core], mask.at[pl.ds(2, 2)], core_send.at[4], core_recv.at[4], other_core)]
    for r in range(2):
        exchange += [
            remote(
                kspace.at[block, :, :, 1 - core, r], ksp_raw.at[pl.ds(2, 2), :, r],
                core_send.at[2 * r], core_recv.at[2 * r], other_core,
            ),
            remote(
                coil_maps.at[block, :, r], maps_raw.at[pl.ds(2, 2), r],
                core_send.at[2 * r + 1], core_recv.at[2 * r + 1], other_core,
            ),
        ]
    weights = [
        remote(source, target.at[cas], w_send.at[n], w_recv.at[n], other_cas)
        for n, (source, target) in enumerate(((first_in, first_r), (time_in, time_r), (last_in, last_r)))
    ]
    weights_in = [
        remote(source, target.at[1 - cas], w_send.at[n], w_recv.at[n], other_cas)
        for n, (source, target) in enumerate(((first_in, first_r), (time_in, time_r), (last_in, last_r)))
    ]

    zero_rows = jnp.zeros((2 * WIN, 256), BF)
    for s in range(2):
        @pl.when(ro == 0)
        def _():
            halo[s, 0] = zero_rows
            halo[s, 1] = zero_rows

        @pl.when(ro == 7)
        def _():
            halo[s, 4] = zero_rows
            halo[s, 5] = zero_rows

    def prepare(pair, r):
        both = jnp.concatenate([maps_raw[2 * pair, r], maps_raw[2 * pair + 1, r]], 1)
        maps_d[pair, r] = dot(table("deint"), both)
        maps_w[pair, r] = dot(table("deint_window"), both)
        for j in (2 * pair, 2 * pair + 1):
            phases = jnp.concatenate([ksp_raw[j, 0, r], ksp_raw[j, 1, r]], 1)
            ksp_d[j, r] = swap_blocks(dot(table("deint"), phases)).astype(BF)

    def consistency(s, r, coils):
        image = img[s, r].astype(F32)
        real, imag = image[:, 0].reshape(N, 256), image[:, 1].reshape(N, 256)
        stage = []
        for j in coils:
            lanes = slice(j % 2 * N, j % 2 * N + N)
            map_r, map_i = twice(maps_d[j // 2, r, :N, lanes]), twice(maps_d[j // 2, r, N:, lanes])
            stage.append(jnp.concatenate([map_r * real - map_i * imag, map_r * imag + map_i * real], 0).astype(BF))
        forward = table("rows_forward")
        stage = [swap_blocks(dot(forward, x).astype(BF)) for x in stage]
        forward = table("cols_forward")
        stage = [dot(x, forward) for x in stage]
        stage = [
            jnp.where(twice(mask[j].reshape(256, N)) != 0, ksp_d[j, r].astype(F32), x).astype(BF)
            for j, x in zip(coils, stage)
        ]
        inverse = table("cols_inverse")
        stage = [swap_blocks(dot(x, inverse).astype(BF)) for x in stage]
        inverse = table("rows_inverse")
        stage = [dot(inverse, x) for x in stage]
        rows = ZS * WIN
        sum_r, sum_i = 0.0, 0.0
        for j, x in zip(coils, stage):
            value_r, value_i = x[:rows], x[rows:]
            lanes = slice(j % 2 * N, j % 2 * N + N)
            win_r, win_i = twice(maps_w[j // 2, r, :rows, lanes]), twice(maps_w[j // 2, r, rows:, lanes])
            sum_r = sum_r + win_r * value_r + win_i * value_i
            sum_i = sum_i + win_r * value_i - win_i * value_r
        return sum_r, sum_i

    def reduce_copies(s, r):
        return [
            remote(
                rs_send.at[s, r, (z + d) % ZS], rs_recv.at[s, r, d - 1],
                rs_ssem.at[s, r, d - 1], rs_rsem.at[s, r, d - 1], peers[d - 1],
            )
            for d in (1, 2, 3)
        ]

    def reduce_send(s, r, sum_r, sum_i):
        for share in range(ZS):
            at = share * WIN
            rs_send[s, r, share] = jnp.concatenate([sum_r[at:at + WIN], sum_i[at:at + WIN]], 0).astype(BF)
        for copy in reduce_copies(s, r):
            copy.start()

    def halo_copies(s, r):
        return (
            remote(halo.at[s, 2 + r], halo.at[s, 4 + r], h_ssem.at[s, r, 0], h_rsem.at[s, r, 0], before),
            remote(halo.at[s, 2 + r], halo.at[s, r], h_ssem.at[s, r, 1], h_rsem.at[s, r, 1], after),
        )

    def combine(s, r):
        for copy in reduce_copies(s, r):
            copy.wait_recv()
        summed = rs_send[s, r, z].astype(F32)
        for d in range(3):
            summed = summed + rs_recv[s, r, d].astype(F32)
        halo[s, 2 + r] = summed.astype(BF)
        to_before, to_after = halo_copies(s, r)

        @pl.when(has_before)
        def _():
            to_before.start()

        @pl.when(has_after)
        def _():
            to_after.start()

    def weights_of(s):
        @pl.when(cas != s)
        def _():
            for copy in weights_in:
                copy.wait_recv()

        eye = table("eye", 128)
        small = table("eye", 64)[:64]
        rows = dot_turned(small, first_r[s].reshape(54, 64)).astype(BF)
        for j in range(4):
            at = WHERE["first"][0] + 64 * j
            first_s[64 * j:64 * j + 64] = dot(rows, tab[at:at + 54, :144]).astype(BF)
        steps = time_r[s]
        time_s[:64, :N] = dot_turned(small, steps[64:]).astype(BF)
        time_s[64:, :N] = dot_turned(small, steps[:128]).astype(BF)
        time_s[:, N:] = eye
        taps = last_r[s].reshape(54, 64)
        low, high = dot(taps, eye[:64]).astype(BF), dot(taps, eye[64:]).astype(BF)
        parts = []
        for n in range(2):
            at = WHERE["last"][0] + 144 * n
            parts.append(dot(tab[at:at + 144, :54], low) + dot(tab[at:at + 144, 64:118], high))
        last = jnp.concatenate(parts, 1)
        line = lax.broadcasted_iota(jnp.int32, (144, 256), 1) // 64
        for place in range(3):
            mine = last
            if place == 0:
                mine = jnp.where((line == 0) & (z == 0), 0.0, last)
            if place == 2:
                mine = jnp.where((line > 0) & (z == ZS - 1), 0.0, last)
            last_s[place, :144] = mine.astype(BF)
            last_s[place, 144:192] = (mine[96:] * jnp.where(ro == 0, 0.0, 1.0)).astype(BF)
            last_s[place, 192:] = (mine[:48] * jnp.where(ro == 7, 0.0, 1.0)).astype(BF)

    def spread(s, rows):
        cells = [halo[s, row] for row in rows]
        for e in range(3):
            moved = cells if e == 1 else [dot(x, table(f"shift{e}")).astype(BF) for x in cells]
            for row, x in zip(rows, moved):
                parts = dot(table("slabs", 2 * WIN), x).astype(BF)
                at = (row * 3 + e) * 16
                for g in range(GROUPS):
                    slab[g, at:at + 16] = parts[16 * g:16 * g + 16]

    def features(row, groups):
        weight = first_s[...]
        stage = [jnp.maximum(dot(weight, slab[g, 48 * row:48 * row + 144]), 0.0).astype(BF) for g in groups]
        columns = []
        for hidden in stage:
            for u in range(2):
                lines = []
                for j in (2 * u, 2 * u + 1):
                    one = hidden[64 * j:64 * j + 64]
                    lines.append(jnp.concatenate([one[:, :N], one[:, N:]], 0))
                lines = jnp.concatenate(lines, 1)
                columns.append(jnp.concatenate([lines, lines], 0))
        weight = time_s[...]
        columns = [jnp.maximum(dot(weight, x), 0.0).astype(BF) for x in columns]
        low, high = {0: (144, 192), 1: (48, 144), 2: (0, 96), 3: (192, 240)}[row]
        results = []
        for n, g in enumerate(groups):
            stack = []
            for u in range(2):
                for j in range(2):
                    one = columns[2 * n + u][:, j * N:j * N + N]
                    stack.append(jnp.concatenate([one[:64], one[64:]], 1))
            place = jnp.where(g == 0, 0, jnp.where(g == GROUPS - 1, 2, 1))
            results.append(dot(last_s[place, low:high], jnp.concatenate(stack, 0)))
        for n, target in enumerate({0: (0,), 1: (0, 1), 2: (0, 1), 3: (1,)}[row]):
            here = [x[48 * n:48 * n + 24] for x in results]
            left = [x[48 * n + 24:48 * n + 48] for x in results]
            total[target, groups[0]] += left[0]
            total[target, groups[1]] += here[0] + left[1]
            total[target, groups[2]] += here[1] + left[2]
            total[target, groups[2] + 1] += here[2]

    def sweep(rows):
        def some(it, unused):
            for row in rows:
                features(row, [3 * it, 3 * it + 1, 3 * it + 2])
            return unused

        lax.fori_loop(0, GROUPS // 3, some, 0)

    def halo_wait(s, r):
        to_before, to_after = halo_copies(s, r)

        @pl.when(has_after)
        def _():
            to_before.wait_recv()

        @pl.when(has_before)
        def _():
            to_after.wait_recv()

    def finish(s, r):
        taps = [total[r, 1:9, 8 * e:8 * e + 8].reshape(64, 256) for e in range(3)]
        lane = lax.broadcasted_iota(jnp.int32, (64, N), 1)
        halves = []
        for q in range(2):
            at = slice(q * N, q * N + N)
            low = jnp.where(lane == 0, 0.0, pltpu.roll(taps[0][:, at], 1, 1))
            high = jnp.where(lane == N - 1, 0.0, pltpu.roll(taps[2][:, at], N - 1, 1))
            halves.append(low + taps[1][:, at] + high)
        image = (dot(table("base", 2 * WIN), halo[s, 2 + r]) + jnp.concatenate(halves, 1)).astype(BF)
        if s == 0:
            share = dot(table("gather", 64), image).astype(BF)
            for c in range(2):
                img[1, r, z, c] = share[c * SHARE:c * SHARE + SHARE]
            for copy in gather_copies(r, False):
                copy.start()
        for half in range(2):
            for q in range(2):
                outs[s, r, half, q] = image[32 * half:32 * half + 32, q * N:q * N + N]
        send_output(s, r)

    def gather_copies(r, arriving):
        return [
            remote(
                img.at[1, r, z], img.at[1, r, (z + ZS - d) % ZS if arriving else z],
                ag_ssem.at[r, d - 1], ag_rsem.at[r, d - 1], peers[d - 1],
            )
            for d in (1, 2, 3)
        ]

    def near_copies(s, r):
        return (
            local(8 + r, outs.at[s, r, core], out.at[block, :, core, r]),
            remote(outs.at[s, r, 1 - core], out.at[block, :, core, r], o_ssem.at[r, 0], o_rsem.at[r, 0], other_core),
        )

    def far_copies(s, r):
        return (
            remote(outs.at[s, r, core], out.at[block, :, core, r], o_ssem.at[r, 1], o_rsem.at[r, 1], other_cas),
            remote(outs.at[s, r, 1 - core], out.at[block, :, core, r], o_ssem.at[r, 2], o_rsem.at[r, 2], other_both),
        )

    def send_output(s, r):
        @pl.when(cas == s)
        def _():
            for copy in near_copies(s, r):
                copy.start()

        @pl.when(cas != s)
        def _():
            for copy in far_copies(s, r):
                copy.start()

    for copy in loads[:5]:
        copy.wait()
    for r in range(2):
        phases = jnp.concatenate([img_raw[0, r], img_raw[1, r]], 1)
        plain = dot(table("deint"), phases).astype(BF)
        for share in range(ZS):
            for c in range(2):
                at = c * N + share * SHARE
                img[0, r, share, c] = plain[at:at + SHARE]
        prepare(0, r)
    for copy in loads[5:]:
        copy.wait()
    acc[0, 0], acc[0, 1] = consistency(0, 0, (0, 1))

    pl.semaphore_wait(barrier, 6 + jnp.where(has_before, 1, 0) + jnp.where(has_after, 1, 0))
    for copy in exchange + weights:
        copy.start()
    acc[1, 0], acc[1, 1] = consistency(0, 1, (0, 1))
    exchange[0].wait_recv()
    for r in range(2):
        for copy in exchange[1 + 2 * r:3 + 2 * r]:
            copy.wait_recv()
        prepare(1, r)
        sum_r, sum_i = consistency(0, r, (2, 3))
        reduce_send(0, r, acc[r, 0] + sum_r, acc[r, 1] + sum_i)

    for s in range(2):
        if s == 1:
            for r in range(2):
                for copy in gather_copies(r, True):
                    copy.wait_recv()
                reduce_send(1, r, *consistency(1, r, (0, 1, 2, 3)))
        weights_of(s)
        total[...] = jnp.zeros_like(total)
        combine(s, 0)
        spread(s, (2,))
        combine(s, 1)
        spread(s, (3,))
        halo_wait(s, 0)
        spread(s, (0, 4))
        sweep((2,))
        halo_wait(s, 1)
        spread(s, (1, 5))
        sweep((1, 0))
        finish(s, 0)
        sweep((3,))
        finish(s, 1)

    for copy in exchange + weights + gather_copies(0, False) + gather_copies(1, False):
        copy.wait_send()
    for s in range(2):
        for r in range(2):
            for copy in reduce_copies(s, r):
                copy.wait_send()
            to_before, to_after = halo_copies(s, r)

            @pl.when(has_before)
            def _():
                to_before.wait_send()

            @pl.when(has_after)
            def _():
                to_after.wait_send()

            @pl.when(cas == s)
            def _():
                keep, give = near_copies(s, r)
                keep.wait()
                give.wait_send()

            @pl.when(cas != s)
            def _():
                for copy in far_copies(s, r):
                    copy.wait_send()

    for r in range(2):
        source = outs.at[0, r, 0]
        arriving = (
            remote(source, out.at[block, :, 1 - core, r], o_ssem.at[r, 0], o_rsem.at[r, 0], other_core),
            remote(source, out.at[1 - block, :, core, r], o_ssem.at[r, 1], o_rsem.at[r, 1], other_cas),
            remote(source, out.at[1 - block, :, 1 - core, r], o_ssem.at[r, 2], o_rsem.at[r, 2], other_both),
        )
        for copy in arriving:
            copy.wait_recv()


def per_device(initial, coil_maps, kspace, sampled, first_w, time_w, last_w):
    dma = pltpu.SemaphoreType.DMA
    out = pl.pallas_call(
        kernel,
        out_shape=jax.ShapeDtypeStruct((2, 2, 2, 2, 32, N), BF),
        in_specs=[pl.BlockSpec(memory_space=pl.ANY)] * 8,
        out_specs=pl.BlockSpec(memory_space=pl.ANY),
        scratch_shapes=[
            pltpu.VMEM(TABLES.shape, BF),
            pltpu.VMEM((4, 2, 256, N), BF),
            pltpu.VMEM((4, 2, 2, 256, N), BF),
            pltpu.VMEM((2, 2, 256, N), BF),
            pltpu.VMEM((4, 2, N, N), jnp.int32),
            pltpu.VMEM((2, 27, 2, 64), BF),
            pltpu.VMEM((2, 192, 64), BF),
            pltpu.VMEM((2, 27, 2, 64), BF),
            pltpu.VMEM((256, 144), BF),
            pltpu.VMEM((128, 256), BF),
            pltpu.VMEM((3, 240, 256), BF),
            pltpu.VMEM((2, 2, 256, 256), F32),
            pltpu.VMEM((2, 2, 2 * ZS * WIN, 256), F32),
            pltpu.VMEM((4, 2, 256, 256), BF),
            pltpu.VMEM((2, 2, ZS, 2, SHARE, 256), BF),
            pltpu.VMEM((2, 2, ZS * WIN, 256), F32),
            pltpu.VMEM((2, 2, ZS, 2 * WIN, 256), BF),
            pltpu.VMEM((2, 2, 3, 2 * WIN, 256), BF),
            pltpu.VMEM((2, 6, 2 * WIN, 256), BF),
            pltpu.VMEM((GROUPS, 288, 256), BF),
            pltpu.VMEM((2, 10, 24, 256), F32),
            pltpu.VMEM((2, 2, 2, 2, 32, N), BF),
            dma((10,)),
            dma((5,)),
            dma((5,)),
            dma((3,)),
            dma((3,)),
            dma((2, 2, 3)),
            dma((2, 2, 3)),
            dma((2, 2, 2)),
            dma((2, 2, 2)),
            dma((2, 3)),
            dma((2, 3)),
            dma((2, 3)),
            dma((2, 3)),
        ],
        compiler_params=pltpu.CompilerParams(
            collective_id=0, has_side_effects=True, vmem_limit_bytes=60_000_000
        ),
    )(
        jnp.asarray(TABLES),
        initial.reshape(2, 2, 2, 2, 256, N),
        coil_maps.reshape(2, 2, 2, 256, N),
        kspace.reshape(2, 2, 2, 2, 2, 256, N),
        sampled.reshape(2, 2, 2, N, N),
        first_w[0],
        time_w[0].reshape(192, 64),
        jnp.swapaxes(last_w[0], 1, 2),
    )
    return out.reshape(1, 2, 4, 2, 16, 2, N)


def solution(mesh):
    in_specs = (
        P(None, None, "readout", None, None, None),
        P(None, "coil", "readout", None, None, None),
        P(None, "coil", None, "readout", None, None, None),
        P("coil", None, None, None),
        P("cascade", None, None, None),
        P("cascade", None, None, None),
        P("cascade", None, None, None),
    )
    out_specs = P("cascade", None, None, "readout", "coil", None, None)
    return jax.shard_map(per_device, mesh=mesh, in_specs=in_specs, out_specs=out_specs, check_vma=False)
```

```python
import functools

import jax
import jax.numpy as jnp
import numpy as np
from jax import lax
from jax.experimental import pallas as pl
from jax.experimental.pallas import tpu as pltpu
from jax.sharding import PartitionSpec as P

MESH = pl.DeviceIdType.MESH
BF = jnp.bfloat16
F32 = jnp.float32
N = 128
ZS = 4
SHARE = N // ZS
WIN = 40
LAG = 3
GROUPS = 9


def complex_blocks(direction):
    k = np.arange(N)
    angle = ((k[:, None] * k[None, :]) % N).astype(np.float32) * np.float32(2.0 * np.pi / N)
    factor = np.float32(1.0 / np.sqrt(N))
    cos, sin = np.cos(angle) * factor, direction * np.sin(angle) * factor
    return np.block([[cos, -sin], [sin, cos]]), np.block([[cos, sin], [-sin, cos]])


def first_selection():
    pick = np.zeros((4, 64, 144))
    for j in range(4):
        for a in range(3):
            for e in range(3):
                for c in range(2):
                    for t in range(3):
                        pick[j, (9 * a + 3 * t + e) * 2 + c, ((a * 3 + e) * 2 + c) * 8 + j + t] = 1
    return pick


def last_selection():
    pick = np.zeros((2, 3, 2, 3, 4, 2, 2, 64))
    for a in range(3):
        for delta in range(2):
            for e in range(3):
                for line in range(4):
                    for j in range(4):
                        c = j + 4 * delta - line
                        if 0 <= c < 3:
                            for o in range(2):
                                pick[j // 2, 2 - a, delta, e, line, o, j % 2, (9 * a + 3 * c + e) * 2 + o] = 1
    return pick


def constant_tables():
    rows_forward, cols_forward = complex_blocks(-1.0)
    rows_inverse, cols_inverse = complex_blocks(1.0)
    deint = np.zeros((256, 256))
    for c in range(2):
        for l in range(N):
            deint[c * N + l, 2 * l + c] = 1
    window = np.zeros((2 * ZS * WIN, 256))
    for c in range(2):
        for z in range(ZS):
            for w in range(SHARE + 4):
                l = SHARE * z - 2 + w
                if 0 <= l < N:
                    window[(c * ZS + z) * WIN + w, c * N + l] = 1
    shift = [np.zeros((256, 256)) for _ in range(2)]
    for q in range(2):
        for p in range(N):
            if p > 0:
                shift[0][q * N + p - 1, q * N + p] = 1
            if p < N - 1:
                shift[1][q * N + p + 1, q * N + p] = 1
    slabs = np.zeros((GROUPS * 16, 256))
    for g in range(GROUPS):
        for c in range(2):
            for l8 in range(8):
                slabs[g * 16 + c * 8 + l8, c * WIN + 4 * g + l8] = 1
    base = np.zeros((64, 256))
    gather = np.zeros((64, 256))
    for l in range(SHARE):
        for o in range(2):
            base[2 * l + o, o * WIN + 2 + l] = 1
            gather[o * SHARE + l, 2 * l + o] = 1
    return {
        "deint": deint,
        "deint_window": window @ deint,
        "rows_forward": rows_forward,
        "cols_forward": cols_forward,
        "cols_inverse": cols_inverse,
        "rows_inverse": window @ rows_inverse,
        "shift0": shift[0],
        "shift2": shift[1],
        "slabs": slabs,
        "base": base,
        "gather": gather,
        "eye": np.eye(128),
        "first": first_selection().reshape(4 * 64, 144),
        "last": last_selection().reshape(2 * 144, 128),
    }


def tables_array():
    tables = constant_tables()
    where, parts, at = {}, [], 0
    for name, table in tables.items():
        where[name] = (at, table.shape[0])
        parts.append(np.pad(table, ((0, 0), (0, 256 - table.shape[1]))))
        at += table.shape[0]
    return where, np.concatenate(parts, 0).astype(jnp.bfloat16)


WHERE, TABLES = tables_array()
EARLY = sum(WHERE[name][1] for name in ("deint", "deint_window"))
LATE = TABLES.shape[0] - EARLY


def dot(a, b):
    return jnp.dot(a, b, preferred_element_type=F32)


def dot_turned(a, b):
    return lax.dot_general(a, b, (((1,), (1,)), ((), ())), preferred_element_type=F32)


def swap_blocks(x):
    return jnp.concatenate(
        [
            jnp.concatenate([x[:N, :N], x[N:, :N]], 1),
            jnp.concatenate([x[:N, N:], x[N:, N:]], 1),
        ],
        0,
    )


def twice(x):
    return jnp.concatenate([x, x], 1)


def kernel(
    tables_in, initial, coil_maps, kspace, sampled, first_in, time_in, last_in,
    out,
    tab, maps_raw, ksp_raw, img_raw, mask,
    first_r, time_r, last_r, first_s, time_s, last_s,
    maps_d, maps_w, ksp_d, img, acc, rs_send, rs_recv, halo, slab, total, outs,
    local_sem, core_send, core_recv, w_send, w_recv, rs_ssem, rs_rsem, h_ssem, h_rsem,
    ag_ssem, ag_rsem, o_ssem, o_rsem,
):
    cas, coil, ro = lax.axis_index("cascade"), lax.axis_index("coil"), lax.axis_index("readout")
    z, core = coil // 2, coil % 2
    hi = ro % 2
    block = 1 - (hi + cas - 2 * hi * cas)
    other_core = (cas, coil + 1 - 2 * core, ro)
    other_cas = (1 - cas, coil, ro)
    other_both = (1 - cas, coil + 1 - 2 * core, ro)
    peers = [(cas, 2 * ((z + d) % ZS) + core, ro) for d in (1, 2, 3)]
    before, after = (1 - cas, coil, ro - 1), (1 - cas, coil, ro + 1)
    has_before, has_after = ro > 0, ro < 7

    def table(name, columns=256):
        at, count = WHERE[name]
        return tab[at:at + count, :columns]

    def local(number, source, target):
        return pltpu.make_async_copy(source, target, local_sem.at[number])

    def remote(source, target, ssem, rsem, device):
        return pltpu.make_async_remote_copy(
            src_ref=source, dst_ref=target, send_sem=ssem, recv_sem=rsem, device_id=device, device_id_type=MESH
        )

    loads = [
        local(0, tables_in.at[pl.ds(0, EARLY)], tab.at[pl.ds(0, EARLY)]),
        local(1, coil_maps.at[block], maps_raw.at[pl.ds(0, 2)]),
        local(2, kspace.at[block, :, :, core], ksp_raw.at[pl.ds(0, 2)]),
        local(4, initial.at[block, :, core], img_raw),
        local(3, sampled.at[:, :, core], mask.at[pl.ds(0, 2)]),
        local(10, tables_in.at[pl.ds(EARLY, LATE)], tab.at[pl.ds(EARLY, LATE)]),
        local(5, first_in, first_r.at[cas]),
        local(6, time_in, time_r.at[cas]),
        local(7, last_in, last_r.at[cas]),
    ]
    for copy in loads:
        copy.start()

    barrier = pltpu.get_barrier_semaphore()
    for device in [other_core, other_cas, other_both, *peers]:
        pl.semaphore_signal(barrier, inc=1, device_id=device, device_id_type=MESH)

    @pl.when(has_before)
    def _():
        pl.semaphore_signal(barrier, inc=1, device_id=before, device_id_type=MESH)

    @pl.when(has_after)
    def _():
        pl.semaphore_signal(barrier, inc=1, device_id=after, device_id_type=MESH)

    exchange = [remote(sampled.at[:, :, 1 - core], mask.at[pl.ds(2, 2)], core_send.at[4], core_recv.at[4], other_core)]
    for r in range(2):
        exchange += [
            remote(
                kspace.at[block, :, :, 1 - core, r], ksp_raw.at[pl.ds(2, 2), :, r],
                core_send.at[2 * r], core_recv.at[2 * r], other_core,
            ),
            remote(
                coil_maps.at[block, :, r], maps_raw.at[pl.ds(2, 2), r],
                core_send.at[2 * r + 1], core_recv.at[2 * r + 1], other_core,
            ),
        ]
    weights = [
        remote(source, target.at[cas], w_send.at[n], w_recv.at[n], other_cas)
        for n, (source, target) in enumerate(((first_in, first_r), (time_in, time_r), (last_in, last_r)))
    ]
    weights_in = [
        remote(source, target.at[1 - cas], w_send.at[n], w_recv.at[n], other_cas)
        for n, (source, target) in enumerate(((first_in, first_r), (time_in, time_r), (last_in, last_r)))
    ]

    zero_rows = jnp.zeros((2 * WIN, 256), BF)
    for s in range(2):
        @pl.when(ro == 0)
        def _():
            halo[s, 0] = zero_rows
            halo[s, 1] = zero_rows

        @pl.when(ro == 7)
        def _():
            halo[s, 4] = zero_rows
            halo[s, 5] = zero_rows

    def prepare(pair, r):
        both = jnp.concatenate([maps_raw[2 * pair, r], maps_raw[2 * pair + 1, r]], 1)
        maps_d[pair, r] = dot(table("deint"), both)
        maps_w[pair, r] = dot(table("deint_window"), both)
        for j in (2 * pair, 2 * pair + 1):
            phases = jnp.concatenate([ksp_raw[j, 0, r], ksp_raw[j, 1, r]], 1)
            ksp_d[j, r] = swap_blocks(dot(table("deint"), phases)).astype(BF)

    def consistency(s, r, coils):
        image = img[s, r].astype(F32)
        real, imag = image[:, 0].reshape(N, 256), image[:, 1].reshape(N, 256)
        stage = []
        for j in coils:
            lanes = slice(j % 2 * N, j % 2 * N + N)
            map_r, map_i = twice(maps_d[j // 2, r, :N, lanes]), twice(maps_d[j // 2, r, N:, lanes])
            stage.append(jnp.concatenate([map_r * real - map_i * imag, map_r * imag + map_i * real], 0).astype(BF))
        forward = table("rows_forward")
        stage = [swap_blocks(dot(forward, x).astype(BF)) for x in stage]
        forward = table("cols_forward")
        stage = [dot(x, forward) for x in stage]
        stage = [
            jnp.where(twice(mask[j].reshape(256, N)) != 0, ksp_d[j, r].astype(F32), x).astype(BF)
            for j, x in zip(coils, stage)
        ]
        inverse = table("cols_inverse")
        stage = [swap_blocks(dot(x, inverse).astype(BF)) for x in stage]
        inverse = table("rows_inverse")
        stage = [dot(inverse, x) for x in stage]
        rows = ZS * WIN
        sum_r, sum_i = 0.0, 0.0
        for j, x in zip(coils, stage):
            value_r, value_i = x[:rows], x[rows:]
            lanes = slice(j % 2 * N, j % 2 * N + N)
            win_r, win_i = twice(maps_w[j // 2, r, :rows, lanes]), twice(maps_w[j // 2, r, rows:, lanes])
            sum_r = sum_r + win_r * value_r + win_i * value_i
            sum_i = sum_i + win_r * value_i - win_i * value_r
        return sum_r, sum_i

    def reduce_copies(s, r):
        return [
            remote(
                rs_send.at[s, r, (z + d) % ZS], rs_recv.at[s, r, d - 1],
                rs_ssem.at[s, r, d - 1], rs_rsem.at[s, r, d - 1], peers[d - 1],
            )
            for d in (1, 2, 3)
        ]

    def reduce_send(s, r, sum_r, sum_i):
        for share in range(ZS):
            at = share * WIN
            rs_send[s, r, share] = jnp.concatenate([sum_r[at:at + WIN], sum_i[at:at + WIN]], 0).astype(BF)
        for copy in reduce_copies(s, r):
            copy.start()

    def halo_copies(s, r):
        return (
            remote(halo.at[s, 2 + r], halo.at[s, 4 + r], h_ssem.at[s, r, 0], h_rsem.at[s, r, 0], before),
            remote(halo.at[s, 2 + r], halo.at[s, r], h_ssem.at[s, r, 1], h_rsem.at[s, r, 1], after),
        )

    def combine(s, r):
        for copy in reduce_copies(s, r):
            copy.wait_recv()
        summed = rs_send[s, r, z].astype(F32)
        for d in range(3):
            summed = summed + rs_recv[s, r, d].astype(F32)
        halo[s, 2 + r] = summed.astype(BF)
        to_before, to_after = halo_copies(s, r)

        @pl.when(has_before)
        def _():
            to_before.start()

        @pl.when(has_after)
        def _():
            to_after.start()

    def weights_of(s):
        @pl.when(cas != s)
        def _():
            for copy in weights_in:
                copy.wait_recv()

        eye = table("eye", 128)
        small = table("eye", 64)[:64]
        rows = dot_turned(small, first_r[s].reshape(54, 64)).astype(BF)
        for j in range(4):
            at = WHERE["first"][0] + 64 * j
            first_s[64 * j:64 * j + 64] = dot(rows, tab[at:at + 54, :144]).astype(BF)
        steps = time_r[s]
        time_s[:64, :N] = dot_turned(small, steps[64:]).astype(BF)
        time_s[64:, :N] = dot_turned(small, steps[:128]).astype(BF)
        time_s[:, N:] = eye
        taps = last_r[s].reshape(54, 64)
        low, high = dot(taps, eye[:64]).astype(BF), dot(taps, eye[64:]).astype(BF)
        parts = []
        for n in range(2):
            at = WHERE["last"][0] + 144 * n
            parts.append(dot(tab[at:at + 144, :54], low) + dot(tab[at:at + 144, 64:118], high))
        last = jnp.concatenate(parts, 1)
        line = lax.broadcasted_iota(jnp.int32, (144, 256), 1) // 64
        for place in range(3):
            mine = last
            if place == 0:
                mine = jnp.where((line == 0) & (z == 0), 0.0, last)
            if place == 2:
                mine = jnp.where((line > 0) & (z == ZS - 1), 0.0, last)
            last_s[place, :144] = mine.astype(BF)
            last_s[place, 144:192] = (mine[96:] * jnp.where(ro == 0, 0.0, 1.0)).astype(BF)
            last_s[place, 192:] = (mine[:48] * jnp.where(ro == 7, 0.0, 1.0)).astype(BF)

    def spread(s, rows):
        cells = [halo[s, row] for row in rows]
        for e in range(3):
            moved = cells if e == 1 else [dot(x, table(f"shift{e}")).astype(BF) for x in cells]
            for row, x in zip(rows, moved):
                parts = dot(table("slabs", 2 * WIN), x).astype(BF)
                at = (row * 3 + e) * 16
                for g in range(GROUPS):
                    slab[g, at:at + 16] = parts[16 * g:16 * g + 16]

    def lifted(row, g):
        return jnp.maximum(dot(first_s[...], slab[g, 48 * row:48 * row + 144]), 0.0).astype(BF)

    def in_time(hidden):
        columns = []
        for u in range(2):
            lines = []
            for j in (2 * u, 2 * u + 1):
                one = hidden[64 * j:64 * j + 64]
                lines.append(jnp.concatenate([one[:, :N], one[:, N:]], 0))
            lines = jnp.concatenate(lines, 1)
            columns.append(lines)
        weight = time_s[:, :N]
        columns = [jnp.maximum(dot(weight, x) + x.astype(F32), 0.0).astype(BF) for x in columns]
        stack = []
        for u in range(2):
            for j in range(2):
                one = columns[u][:, j * N:j * N + N]
                stack.append(jnp.concatenate([one[:64], one[64:]], 1))
        return jnp.concatenate(stack, 0)

    def projected(row, g, stack):
        low, high = {0: (144, 192), 1: (48, 144), 2: (0, 96), 3: (192, 240)}[row]
        result = dot(last_s[0 if g == 0 else 2 if g == GROUPS - 1 else 1, low:high], stack)
        for n, target in enumerate({0: (0,), 1: (0, 1), 2: (0, 1), 3: (1,)}[row]):
            total[target, g + 1] += result[48 * n:48 * n + 24]
            total[target, g] += result[48 * n + 24:48 * n + 48]

    def sweep(rows):
        units = [(row, g) for g in range(GROUPS) for row in rows]
        hidden, stacks = {}, {}
        for n in range(len(units) + 2 * LAG):
            if n < len(units):
                hidden[n] = lifted(*units[n])
            if 0 <= n - LAG < len(units):
                stacks[n - LAG] = in_time(hidden.pop(n - LAG))
            if 0 <= n - 2 * LAG:
                projected(*units[n - 2 * LAG], stacks.pop(n - 2 * LAG))

    def halo_wait(s, r):
        to_before, to_after = halo_copies(s, r)

        @pl.when(has_after)
        def _():
            to_before.wait_recv()

        @pl.when(has_before)
        def _():
            to_after.wait_recv()

    def finish(s, r):
        taps = [total[r, 1:9, 8 * e:8 * e + 8].reshape(64, 256) for e in range(3)]
        lane = lax.broadcasted_iota(jnp.int32, (64, N), 1)
        halves = []
        for q in range(2):
            at = slice(q * N, q * N + N)
            low = jnp.where(lane == 0, 0.0, pltpu.roll(taps[0][:, at], 1, 1))
            high = jnp.where(lane == N - 1, 0.0, pltpu.roll(taps[2][:, at], N - 1, 1))
            halves.append(low + taps[1][:, at] + high)
        image = (dot(table("base", 2 * WIN), halo[s, 2 + r]) + jnp.concatenate(halves, 1)).astype(BF)
        if s == 0:
            share = dot(table("gather", 64), image).astype(BF)
            for c in range(2):
                img[1, r, z, c] = share[c * SHARE:c * SHARE + SHARE]
            for copy in gather_copies(r, False):
                copy.start()
        for half in range(2):
            for q in range(2):
                outs[s, r, half, q] = image[32 * half:32 * half + 32, q * N:q * N + N]
        send_output(s, r)

    def gather_copies(r, arriving):
        return [
            remote(
                img.at[1, r, z], img.at[1, r, (z + ZS - d) % ZS if arriving else z],
                ag_ssem.at[r, d - 1], ag_rsem.at[r, d - 1], peers[d - 1],
            )
            for d in (1, 2, 3)
        ]

    def near_copies(s, r):
        return (
            local(8 + r, outs.at[s, r, core], out.at[block, :, core, r]),
            remote(outs.at[s, r, 1 - core], out.at[block, :, core, r], o_ssem.at[r, 0], o_rsem.at[r, 0], other_core),
        )

    def far_copies(s, r):
        return (
            remote(outs.at[s, r, core], out.at[block, :, core, r], o_ssem.at[r, 1], o_rsem.at[r, 1], other_cas),
            remote(outs.at[s, r, 1 - core], out.at[block, :, core, r], o_ssem.at[r, 2], o_rsem.at[r, 2], other_both),
        )

    def send_output(s, r):
        @pl.when(cas == s)
        def _():
            for copy in near_copies(s, r):
                copy.start()

        @pl.when(cas != s)
        def _():
            for copy in far_copies(s, r):
                copy.start()

    pl.semaphore_wait(barrier, 6 + jnp.where(has_before, 1, 0) + jnp.where(has_after, 1, 0))
    for copy in exchange + weights:
        copy.start()
    for copy in loads[:4]:
        copy.wait()
    for r in range(2):
        phases = jnp.concatenate([img_raw[0, r], img_raw[1, r]], 1)
        plain = dot(table("deint"), phases).astype(BF)
        for share in range(ZS):
            for c in range(2):
                at = c * N + share * SHARE
                img[0, r, share, c] = plain[at:at + SHARE]
        prepare(0, r)
    for copy in loads[4:]:
        copy.wait()
    acc[0, 0], acc[0, 1] = consistency(0, 0, (0, 1))

    acc[1, 0], acc[1, 1] = consistency(0, 1, (0, 1))
    exchange[0].wait_recv()
    for r in range(2):
        for copy in exchange[1 + 2 * r:3 + 2 * r]:
            copy.wait_recv()
        prepare(1, r)
        sum_r, sum_i = consistency(0, r, (2, 3))
        reduce_send(0, r, acc[r, 0] + sum_r, acc[r, 1] + sum_i)

    for s in range(2):
        if s == 1:
            for r in range(2):
                for copy in gather_copies(r, True):
                    copy.wait_recv()
                reduce_send(1, r, *consistency(1, r, (0, 1, 2, 3)))
        weights_of(s)
        total[...] = jnp.zeros_like(total)
        combine(s, 0)
        spread(s, (2,))
        combine(s, 1)
        spread(s, (3,))
        halo_wait(s, 0)
        spread(s, (0, 4))
        sweep((2,))
        halo_wait(s, 1)
        spread(s, (1, 5))
        sweep((1, 0))
        finish(s, 0)
        sweep((3,))
        finish(s, 1)

    for copy in exchange + weights + gather_copies(0, False) + gather_copies(1, False):
        copy.wait_send()
    for s in range(2):
        for r in range(2):
            for copy in reduce_copies(s, r):
                copy.wait_send()
            to_before, to_after = halo_copies(s, r)

            @pl.when(has_before)
            def _():
                to_before.wait_send()

            @pl.when(has_after)
            def _():
                to_after.wait_send()

            @pl.when(cas == s)
            def _():
                keep, give = near_copies(s, r)
                keep.wait()
                give.wait_send()

            @pl.when(cas != s)
            def _():
                for copy in far_copies(s, r):
                    copy.wait_send()

    for r in range(2):
        source = outs.at[0, r, 0]
        arriving = (
            remote(source, out.at[block, :, 1 - core, r], o_ssem.at[r, 0], o_rsem.at[r, 0], other_core),
            remote(source, out.at[1 - block, :, core, r], o_ssem.at[r, 1], o_rsem.at[r, 1], other_cas),
            remote(source, out.at[1 - block, :, 1 - core, r], o_ssem.at[r, 2], o_rsem.at[r, 2], other_both),
        )
        for copy in arriving:
            copy.wait_recv()


def per_device(initial, coil_maps, kspace, sampled, first_w, time_w, last_w):
    dma = pltpu.SemaphoreType.DMA
    out = pl.pallas_call(
        kernel,
        out_shape=jax.ShapeDtypeStruct((2, 2, 2, 2, 32, N), BF),
        in_specs=[pl.BlockSpec(memory_space=pl.ANY)] * 8,
        out_specs=pl.BlockSpec(memory_space=pl.ANY),
        scratch_shapes=[
            pltpu.VMEM(TABLES.shape, BF),
            pltpu.VMEM((4, 2, 256, N), BF),
            pltpu.VMEM((4, 2, 2, 256, N), BF),
            pltpu.VMEM((2, 2, 256, N), BF),
            pltpu.VMEM((4, 2, N, N), jnp.int32),
            pltpu.VMEM((2, 27, 2, 64), BF),
            pltpu.VMEM((2, 192, 64), BF),
            pltpu.VMEM((2, 27, 2, 64), BF),
            pltpu.VMEM((256, 144), BF),
            pltpu.VMEM((128, 256), BF),
            pltpu.VMEM((3, 240, 256), BF),
            pltpu.VMEM((2, 2, 256, 256), F32),
            pltpu.VMEM((2, 2, 2 * ZS * WIN, 256), F32),
            pltpu.VMEM((4, 2, 256, 256), BF),
            pltpu.VMEM((2, 2, ZS, 2, SHARE, 256), BF),
            pltpu.VMEM((2, 2, ZS * WIN, 256), F32),
            pltpu.VMEM((2, 2, ZS, 2 * WIN, 256), BF),
            pltpu.VMEM((2, 2, 3, 2 * WIN, 256), BF),
            pltpu.VMEM((2, 6, 2 * WIN, 256), BF),
            pltpu.VMEM((GROUPS, 288, 256), BF),
            pltpu.VMEM((2, 10, 24, 256), F32),
            pltpu.VMEM((2, 2, 2, 2, 32, N), BF),
            dma((11,)),
            dma((5,)),
            dma((5,)),
            dma((3,)),
            dma((3,)),
            dma((2, 2, 3)),
            dma((2, 2, 3)),
            dma((2, 2, 2)),
            dma((2, 2, 2)),
            dma((2, 3)),
            dma((2, 3)),
            dma((2, 3)),
            dma((2, 3)),
        ],
        compiler_params=pltpu.CompilerParams(
            collective_id=0, has_side_effects=True, vmem_limit_bytes=60_000_000
        ),
    )(
        jnp.asarray(TABLES),
        initial.reshape(2, 2, 2, 2, 256, N),
        coil_maps.reshape(2, 2, 2, 256, N),
        kspace.reshape(2, 2, 2, 2, 2, 256, N),
        sampled.reshape(2, 2, 2, N, N),
        first_w[0],
        time_w[0].reshape(192, 64),
        jnp.swapaxes(last_w[0], 1, 2),
    )
    return out.reshape(1, 2, 4, 2, 16, 2, N)


def solution(mesh):
    in_specs = (
        P(None, None, "readout", None, None, None),
        P(None, "coil", "readout", None, None, None),
        P(None, "coil", None, "readout", None, None, None),
        P("coil", None, None, None),
        P("cascade", None, None, None),
        P("cascade", None, None, None),
        P("cascade", None, None, None),
    )
    out_specs = P("cascade", None, None, "readout", "coil", None, None)
    return jax.shard_map(per_device, mesh=mesh, in_specs=in_specs, out_specs=out_specs, check_vma=False)
```

```python
import functools

import jax
import jax.numpy as jnp
import numpy as np
from jax import lax
from jax.experimental import pallas as pl
from jax.experimental.pallas import tpu as pltpu
from jax.sharding import PartitionSpec as P

MESH = pl.DeviceIdType.MESH
BF = jnp.bfloat16
F32 = jnp.float32
N = 128
ZS = 4
SHARE = N // ZS
WIN = 40
LAG = 3
GROUPS = 9


def complex_blocks(direction):
    k = np.arange(N)
    angle = ((k[:, None] * k[None, :]) % N).astype(np.float32) * np.float32(2.0 * np.pi / N)
    factor = np.float32(1.0 / np.sqrt(N))
    cos, sin = np.cos(angle) * factor, direction * np.sin(angle) * factor
    return np.block([[cos, -sin], [sin, cos]]), np.block([[cos, sin], [-sin, cos]])


def first_selection():
    pick = np.zeros((4, 64, 144))
    for j in range(4):
        for a in range(3):
            for e in range(3):
                for c in range(2):
                    for t in range(3):
                        at = (a * 3 + e) * 16 + (j + t) // 4 * 8 + c * 4 + (j + t) % 4
                        pick[j, (9 * a + 3 * t + e) * 2 + c, at] = 1
    return pick


def last_selection():
    pick = np.zeros((2, 3, 2, 3, 4, 2, 2, 64))
    for a in range(3):
        for delta in range(2):
            for e in range(3):
                for line in range(4):
                    for j in range(4):
                        c = j + 4 * delta - line
                        if 0 <= c < 3:
                            for o in range(2):
                                pick[j // 2, 2 - a, delta, e, line, o, j % 2, (9 * a + 3 * c + e) * 2 + o] = 1
    return pick


def constant_tables():
    rows_forward, cols_forward = complex_blocks(-1.0)
    rows_inverse, cols_inverse = complex_blocks(1.0)
    deint = np.zeros((256, 256))
    for c in range(2):
        for l in range(N):
            deint[c * N + l, 2 * l + c] = 1
    window = np.zeros((2 * ZS * WIN, 256))
    for c in range(2):
        for z in range(ZS):
            for w in range(SHARE + 4):
                l = SHARE * z - 2 + w
                if 0 <= l < N:
                    window[(c * ZS + z) * WIN + w, c * N + l] = 1
    base = np.zeros((64, 256))
    gather = np.zeros((64, 256))
    for l in range(SHARE):
        for o in range(2):
            base[2 * l + o, (l + 2) // 4 * 8 + o * 4 + (l + 2) % 4] = 1
            gather[o * SHARE + l, 2 * l + o] = 1
    return {
        "deint": deint,
        "deint_window": window @ deint,
        "rows_forward": rows_forward,
        "cols_forward": cols_forward,
        "cols_inverse": cols_inverse,
        "rows_inverse": window @ rows_inverse,
        "base": base,
        "gather": gather,
        "eye": np.eye(128),
        "first": first_selection().reshape(4 * 64, 144),
        "last": last_selection().reshape(2 * 144, 128),
    }


def tables_array():
    tables = constant_tables()
    where, parts, at = {}, [], 0
    for name, table in tables.items():
        where[name] = (at, table.shape[0])
        parts.append(np.pad(table, ((0, 0), (0, 256 - table.shape[1]))))
        at += table.shape[0]
    return where, np.concatenate(parts, 0).astype(jnp.bfloat16)


WHERE, TABLES = tables_array()
EARLY = sum(WHERE[name][1] for name in ("deint", "deint_window"))
LATE = TABLES.shape[0] - EARLY


def dot(a, b):
    return jnp.dot(a, b, preferred_element_type=F32)


def dot_turned(a, b):
    return lax.dot_general(a, b, (((1,), (1,)), ((), ())), preferred_element_type=F32)


def swap_blocks(x):
    return jnp.concatenate(
        [
            jnp.concatenate([x[:N, :N], x[N:, :N]], 1),
            jnp.concatenate([x[:N, N:], x[N:, N:]], 1),
        ],
        0,
    )


def twice(x):
    return jnp.concatenate([x, x], 1)


def kernel(
    tables_in, initial, coil_maps, kspace, sampled, first_in, time_in, last_in,
    out,
    tab, maps_raw, ksp_raw, img_raw, mask,
    first_r, time_r, last_r, first_s, time_s, last_s,
    maps_d, maps_w, ksp_d, img, acc, rs_send, rs_recv, halo, slab, total, outs,
    local_sem, core_send, core_recv, w_send, w_recv, rs_ssem, rs_rsem, h_ssem, h_rsem,
    ag_ssem, ag_rsem, o_ssem, o_rsem,
):
    cas, coil, ro = lax.axis_index("cascade"), lax.axis_index("coil"), lax.axis_index("readout")
    z, core = coil // 2, coil % 2
    hi = ro % 2
    block = 1 - (hi + cas - 2 * hi * cas)
    other_core = (cas, coil + 1 - 2 * core, ro)
    other_cas = (1 - cas, coil, ro)
    other_both = (1 - cas, coil + 1 - 2 * core, ro)
    peers = [(cas, 2 * ((z + d) % ZS) + core, ro) for d in (1, 2, 3)]
    before, after = (1 - cas, coil, ro - 1), (1 - cas, coil, ro + 1)
    has_before, has_after = ro > 0, ro < 7

    def table(name, columns=256):
        at, count = WHERE[name]
        return tab[at:at + count, :columns]

    def local(number, source, target):
        return pltpu.make_async_copy(source, target, local_sem.at[number])

    def remote(source, target, ssem, rsem, device):
        return pltpu.make_async_remote_copy(
            src_ref=source, dst_ref=target, send_sem=ssem, recv_sem=rsem, device_id=device, device_id_type=MESH
        )

    loads = [
        local(0, tables_in.at[pl.ds(0, EARLY)], tab.at[pl.ds(0, EARLY)]),
        local(1, coil_maps.at[block], maps_raw.at[pl.ds(0, 2)]),
        local(2, kspace.at[block, :, :, core], ksp_raw.at[pl.ds(0, 2)]),
        local(4, initial.at[block, :, core], img_raw),
        local(3, sampled.at[:, :, core], mask.at[pl.ds(0, 2)]),
        local(10, tables_in.at[pl.ds(EARLY, LATE)], tab.at[pl.ds(EARLY, LATE)]),
        local(5, first_in, first_r.at[cas]),
        local(6, time_in, time_r.at[cas]),
        local(7, last_in, last_r.at[cas]),
    ]
    for copy in loads:
        copy.start()

    barrier = pltpu.get_barrier_semaphore()
    for device in [other_core, other_cas, other_both, *peers]:
        pl.semaphore_signal(barrier, inc=1, device_id=device, device_id_type=MESH)

    @pl.when(has_before)
    def _():
        pl.semaphore_signal(barrier, inc=1, device_id=before, device_id_type=MESH)

    @pl.when(has_after)
    def _():
        pl.semaphore_signal(barrier, inc=1, device_id=after, device_id_type=MESH)

    exchange = [remote(sampled.at[:, :, 1 - core], mask.at[pl.ds(2, 2)], core_send.at[4], core_recv.at[4], other_core)]
    for r in range(2):
        exchange += [
            remote(
                kspace.at[block, :, :, 1 - core, r], ksp_raw.at[pl.ds(2, 2), :, r],
                core_send.at[2 * r], core_recv.at[2 * r], other_core,
            ),
            remote(
                coil_maps.at[block, :, r], maps_raw.at[pl.ds(2, 2), r],
                core_send.at[2 * r + 1], core_recv.at[2 * r + 1], other_core,
            ),
        ]
    weights = [
        remote(source, target.at[cas], w_send.at[n], w_recv.at[n], other_cas)
        for n, (source, target) in enumerate(((first_in, first_r), (time_in, time_r), (last_in, last_r)))
    ]
    weights_in = [
        remote(source, target.at[1 - cas], w_send.at[n], w_recv.at[n], other_cas)
        for n, (source, target) in enumerate(((first_in, first_r), (time_in, time_r), (last_in, last_r)))
    ]

    zero_rows = jnp.zeros((2 * WIN, 256), BF)
    for s in range(2):
        @pl.when(ro == 0)
        def _():
            halo[s, 0] = zero_rows
            halo[s, 1] = zero_rows

        @pl.when(ro == 7)
        def _():
            halo[s, 4] = zero_rows
            halo[s, 5] = zero_rows

    def prepare(pair, r):
        both = jnp.concatenate([maps_raw[2 * pair, r], maps_raw[2 * pair + 1, r]], 1)
        maps_d[pair, r] = dot(table("deint"), both)
        maps_w[pair, r] = dot(table("deint_window"), both)
        for j in (2 * pair, 2 * pair + 1):
            phases = jnp.concatenate([ksp_raw[j, 0, r], ksp_raw[j, 1, r]], 1)
            ksp_d[j, r] = swap_blocks(dot(table("deint"), phases)).astype(BF)

    def consistency(s, r, coils):
        image = img[s, r].astype(F32)
        real, imag = image[:, 0].reshape(N, 256), image[:, 1].reshape(N, 256)
        stage = []
        for j in coils:
            lanes = slice(j % 2 * N, j % 2 * N + N)
            map_r, map_i = twice(maps_d[j // 2, r, :N, lanes]), twice(maps_d[j // 2, r, N:, lanes])
            stage.append(jnp.concatenate([map_r * real - map_i * imag, map_r * imag + map_i * real], 0).astype(BF))
        forward = table("rows_forward")
        stage = [swap_blocks(dot(forward, x).astype(BF)) for x in stage]
        forward = table("cols_forward")
        stage = [dot(x, forward) for x in stage]
        stage = [
            jnp.where(twice(mask[j].reshape(256, N)) != 0, ksp_d[j, r].astype(F32), x).astype(BF)
            for j, x in zip(coils, stage)
        ]
        inverse = table("cols_inverse")
        stage = [swap_blocks(dot(x, inverse).astype(BF)) for x in stage]
        inverse = table("rows_inverse")
        stage = [dot(inverse, x) for x in stage]
        rows = ZS * WIN
        sum_r, sum_i = 0.0, 0.0
        for j, x in zip(coils, stage):
            value_r, value_i = x[:rows], x[rows:]
            lanes = slice(j % 2 * N, j % 2 * N + N)
            win_r, win_i = twice(maps_w[j // 2, r, :rows, lanes]), twice(maps_w[j // 2, r, rows:, lanes])
            sum_r = sum_r + win_r * value_r + win_i * value_i
            sum_i = sum_i + win_r * value_i - win_i * value_r
        return sum_r, sum_i

    def reduce_copies(s, r):
        return [
            remote(
                rs_send.at[s, r, (z + d) % ZS], rs_recv.at[s, r, d - 1],
                rs_ssem.at[s, r, d - 1], rs_rsem.at[s, r, d - 1], peers[d - 1],
            )
            for d in (1, 2, 3)
        ]

    def reduce_send(s, r, sum_r, sum_i):
        for share in range(ZS):
            at = share * WIN
            rs_send[s, r, share] = jnp.concatenate([sum_r[at:at + WIN], sum_i[at:at + WIN]], 0).astype(BF)
        for copy in reduce_copies(s, r):
            copy.start()

    def halo_copies(s, r):
        return (
            remote(halo.at[s, 2 + r], halo.at[s, 4 + r], h_ssem.at[s, r, 0], h_rsem.at[s, r, 0], before),
            remote(halo.at[s, 2 + r], halo.at[s, r], h_ssem.at[s, r, 1], h_rsem.at[s, r, 1], after),
        )

    def combine(s, r):
        for copy in reduce_copies(s, r):
            copy.wait_recv()
        summed = rs_send[s, r, z].astype(F32)
        for d in range(3):
            summed = summed + rs_recv[s, r, d].astype(F32)
        top = lax.broadcasted_iota(jnp.int32, (8, 256), 0) < 4
        parts = []
        for at in range(0, WIN, 8):
            real, imag = summed[at:at + 8], summed[WIN + at:WIN + at + 8]
            parts.append(jnp.where(top, real, pltpu.roll(imag, 4, 0)))
            parts.append(jnp.where(top, pltpu.roll(real, 4, 0), imag))
        halo[s, 2 + r] = jnp.concatenate(parts, 0).astype(BF)
        to_before, to_after = halo_copies(s, r)

        @pl.when(has_before)
        def _():
            to_before.start()

        @pl.when(has_after)
        def _():
            to_after.start()

    def weights_of(s):
        @pl.when(cas != s)
        def _():
            for copy in weights_in:
                copy.wait_recv()

        eye = table("eye", 128)
        small = table("eye", 64)[:64]
        rows = dot_turned(small, first_r[s].reshape(54, 64)).astype(BF)
        for j in range(4):
            at = WHERE["first"][0] + 64 * j
            first_s[64 * j:64 * j + 64] = dot(rows, tab[at:at + 54, :144]).astype(BF)
        steps = time_r[s]
        time_s[:64, :N] = dot_turned(small, steps[64:]).astype(BF)
        time_s[64:, :N] = dot_turned(small, steps[:128]).astype(BF)
        time_s[:, N:] = eye
        taps = last_r[s].reshape(54, 64)
        low, high = dot(taps, eye[:64]).astype(BF), dot(taps, eye[64:]).astype(BF)
        parts = []
        for n in range(2):
            at = WHERE["last"][0] + 144 * n
            parts.append(dot(tab[at:at + 144, :54], low) + dot(tab[at:at + 144, 64:118], high))
        last = jnp.concatenate(parts, 1)
        line = lax.broadcasted_iota(jnp.int32, (144, 256), 1) // 64
        for place in range(3):
            mine = last
            if place == 0:
                mine = jnp.where((line == 0) & (z == 0), 0.0, last)
            if place == 2:
                mine = jnp.where((line > 0) & (z == ZS - 1), 0.0, last)
            last_s[place, :144] = mine.astype(BF)
            last_s[place, 144:192] = (mine[96:] * jnp.where(ro == 0, 0.0, 1.0)).astype(BF)
            last_s[place, 192:] = (mine[:48] * jnp.where(ro == 7, 0.0, 1.0)).astype(BF)

    def moved(x, by):
        lane = lax.broadcasted_iota(jnp.int32, (x.shape[0], N), 1)
        dead = lane == (0 if by == 1 else N - 1)
        halves = [pltpu.roll(x[:, at:at + N], by % N, 1) for at in (0, N)]
        return jnp.concatenate([jnp.where(dead, 0.0, half) for half in halves], 1)

    def spread(s, rows):
        for row in rows:
            cells = halo[s, row].astype(F32)
            for e, x in enumerate((moved(cells, 1), cells, moved(cells, -1))):
                at = (row * 3 + e) * 16
                for g in range(GROUPS):
                    slab[g, at:at + 16] = x[8 * g:8 * g + 16].astype(BF)

    def lifted(row, g):
        return jnp.maximum(dot(first_s[...], slab[g, 48 * row:48 * row + 144]), 0.0).astype(BF)

    def in_time(hidden):
        columns = []
        for u in range(2):
            lines = []
            for j in (2 * u, 2 * u + 1):
                one = hidden[64 * j:64 * j + 64]
                lines.append(jnp.concatenate([one[:, :N], one[:, N:]], 0))
            lines = jnp.concatenate(lines, 1)
            columns.append(lines)
        weight = time_s[:, :N]
        columns = [jnp.maximum(dot(weight, x) + x.astype(F32), 0.0).astype(BF) for x in columns]
        stack = []
        for u in range(2):
            for j in range(2):
                one = columns[u][:, j * N:j * N + N]
                stack.append(jnp.concatenate([one[:64], one[64:]], 1))
        return jnp.concatenate(stack, 0)

    def projected(row, g, stack):
        low, high = {0: (144, 192), 1: (48, 144), 2: (0, 96), 3: (192, 240)}[row]
        result = dot(last_s[0 if g == 0 else 2 if g == GROUPS - 1 else 1, low:high], stack)
        for n, target in enumerate({0: (0,), 1: (0, 1), 2: (0, 1), 3: (1,)}[row]):
            total[target, g + 1] += result[48 * n:48 * n + 24]
            total[target, g] += result[48 * n + 24:48 * n + 48]

    def sweep(rows):
        units = [(row, g) for g in range(GROUPS) for row in rows]
        hidden, stacks = {}, {}
        for n in range(len(units) + 2 * LAG):
            if n < len(units):
                hidden[n] = lifted(*units[n])
            if 0 <= n - LAG < len(units):
                stacks[n - LAG] = in_time(hidden.pop(n - LAG))
            if 0 <= n - 2 * LAG:
                projected(*units[n - 2 * LAG], stacks.pop(n - 2 * LAG))

    def halo_wait(s, r):
        to_before, to_after = halo_copies(s, r)

        @pl.when(has_after)
        def _():
            to_before.wait_recv()

        @pl.when(has_before)
        def _():
            to_after.wait_recv()

    def finish(s, r):
        taps = [total[r, 1:9, 8 * e:8 * e + 8].reshape(64, 256) for e in range(3)]
        change = moved(taps[0], 1) + taps[1] + moved(taps[2], -1)
        image = (dot(table("base", 2 * WIN), halo[s, 2 + r]) + change).astype(BF)
        if s == 0:
            share = dot(table("gather", 64), image).astype(BF)
            for c in range(2):
                img[1, r, z, c] = share[c * SHARE:c * SHARE + SHARE]
            for copy in gather_copies(r, False):
                copy.start()
        for half in range(2):
            for q in range(2):
                outs[s, r, half, q] = image[32 * half:32 * half + 32, q * N:q * N + N]
        send_output(s, r)

    def gather_copies(r, arriving):
        return [
            remote(
                img.at[1, r, z], img.at[1, r, (z + ZS - d) % ZS if arriving else z],
                ag_ssem.at[r, d - 1], ag_rsem.at[r, d - 1], peers[d - 1],
            )
            for d in (1, 2, 3)
        ]

    def near_copies(s, r):
        return (
            local(8 + r, outs.at[s, r, core], out.at[block, :, core, r]),
            remote(outs.at[s, r, 1 - core], out.at[block, :, core, r], o_ssem.at[r, 0], o_rsem.at[r, 0], other_core),
        )

    def far_copies(s, r):
        return (
            remote(outs.at[s, r, core], out.at[block, :, core, r], o_ssem.at[r, 1], o_rsem.at[r, 1], other_cas),
            remote(outs.at[s, r, 1 - core], out.at[block, :, core, r], o_ssem.at[r, 2], o_rsem.at[r, 2], other_both),
        )

    def send_output(s, r):
        @pl.when(cas == s)
        def _():
            for copy in near_copies(s, r):
                copy.start()

        @pl.when(cas != s)
        def _():
            for copy in far_copies(s, r):
                copy.start()

    pl.semaphore_wait(barrier, 6 + jnp.where(has_before, 1, 0) + jnp.where(has_after, 1, 0))
    for copy in exchange + weights:
        copy.start()
    for copy in loads[:4]:
        copy.wait()
    for r in range(2):
        phases = jnp.concatenate([img_raw[0, r], img_raw[1, r]], 1)
        plain = dot(table("deint"), phases).astype(BF)
        for share in range(ZS):
            for c in range(2):
                at = c * N + share * SHARE
                img[0, r, share, c] = plain[at:at + SHARE]
        prepare(0, r)
    for copy in loads[4:]:
        copy.wait()
    acc[0, 0], acc[0, 1] = consistency(0, 0, (0, 1))

    acc[1, 0], acc[1, 1] = consistency(0, 1, (0, 1))
    exchange[0].wait_recv()
    for r in range(2):
        for copy in exchange[1 + 2 * r:3 + 2 * r]:
            copy.wait_recv()
        prepare(1, r)
        sum_r, sum_i = consistency(0, r, (2, 3))
        reduce_send(0, r, acc[r, 0] + sum_r, acc[r, 1] + sum_i)

    for s in range(2):
        if s == 1:
            for r in range(2):
                for copy in gather_copies(r, True):
                    copy.wait_recv()
                reduce_send(1, r, *consistency(1, r, (0, 1, 2, 3)))
        weights_of(s)
        total[...] = jnp.zeros_like(total)
        combine(s, 0)
        spread(s, (2,))
        combine(s, 1)
        spread(s, (3,))
        halo_wait(s, 0)
        spread(s, (0, 4))
        sweep((2,))
        halo_wait(s, 1)
        spread(s, (1, 5))
        sweep((1, 0))
        finish(s, 0)
        sweep((3,))
        finish(s, 1)

    for copy in exchange + weights + gather_copies(0, False) + gather_copies(1, False):
        copy.wait_send()
    for s in range(2):
        for r in range(2):
            for copy in reduce_copies(s, r):
                copy.wait_send()
            to_before, to_after = halo_copies(s, r)

            @pl.when(has_before)
            def _():
                to_before.wait_send()

            @pl.when(has_after)
            def _():
                to_after.wait_send()

            @pl.when(cas == s)
            def _():
                keep, give = near_copies(s, r)
                keep.wait()
                give.wait_send()

            @pl.when(cas != s)
            def _():
                for copy in far_copies(s, r):
                    copy.wait_send()

    for r in range(2):
        source = outs.at[0, r, 0]
        arriving = (
            remote(source, out.at[block, :, 1 - core, r], o_ssem.at[r, 0], o_rsem.at[r, 0], other_core),
            remote(source, out.at[1 - block, :, core, r], o_ssem.at[r, 1], o_rsem.at[r, 1], other_cas),
            remote(source, out.at[1 - block, :, 1 - core, r], o_ssem.at[r, 2], o_rsem.at[r, 2], other_both),
        )
        for copy in arriving:
            copy.wait_recv()


def per_device(initial, coil_maps, kspace, sampled, first_w, time_w, last_w):
    dma = pltpu.SemaphoreType.DMA
    out = pl.pallas_call(
        kernel,
        out_shape=jax.ShapeDtypeStruct((2, 2, 2, 2, 32, N), BF),
        in_specs=[pl.BlockSpec(memory_space=pl.ANY)] * 8,
        out_specs=pl.BlockSpec(memory_space=pl.ANY),
        scratch_shapes=[
            pltpu.VMEM(TABLES.shape, BF),
            pltpu.VMEM((4, 2, 256, N), BF),
            pltpu.VMEM((4, 2, 2, 256, N), BF),
            pltpu.VMEM((2, 2, 256, N), BF),
            pltpu.VMEM((4, 2, N, N), jnp.int32),
            pltpu.VMEM((2, 27, 2, 64), BF),
            pltpu.VMEM((2, 192, 64), BF),
            pltpu.VMEM((2, 27, 2, 64), BF),
            pltpu.VMEM((256, 144), BF),
            pltpu.VMEM((128, 256), BF),
            pltpu.VMEM((3, 240, 256), BF),
            pltpu.VMEM((2, 2, 256, 256), F32),
            pltpu.VMEM((2, 2, 2 * ZS * WIN, 256), F32),
            pltpu.VMEM((4, 2, 256, 256), BF),
            pltpu.VMEM((2, 2, ZS, 2, SHARE, 256), BF),
            pltpu.VMEM((2, 2, ZS * WIN, 256), F32),
            pltpu.VMEM((2, 2, ZS, 2 * WIN, 256), BF),
            pltpu.VMEM((2, 2, 3, 2 * WIN, 256), BF),
            pltpu.VMEM((2, 6, 2 * WIN, 256), BF),
            pltpu.VMEM((GROUPS, 288, 256), BF),
            pltpu.VMEM((2, 10, 24, 256), F32),
            pltpu.VMEM((2, 2, 2, 2, 32, N), BF),
            dma((11,)),
            dma((5,)),
            dma((5,)),
            dma((3,)),
            dma((3,)),
            dma((2, 2, 3)),
            dma((2, 2, 3)),
            dma((2, 2, 2)),
            dma((2, 2, 2)),
            dma((2, 3)),
            dma((2, 3)),
            dma((2, 3)),
            dma((2, 3)),
        ],
        compiler_params=pltpu.CompilerParams(
            collective_id=0, has_side_effects=True, vmem_limit_bytes=60_000_000
        ),
    )(
        jnp.asarray(TABLES),
        initial.reshape(2, 2, 2, 2, 256, N),
        coil_maps.reshape(2, 2, 2, 256, N),
        kspace.reshape(2, 2, 2, 2, 2, 256, N),
        sampled.reshape(2, 2, 2, N, N),
        first_w[0],
        time_w[0].reshape(192, 64),
        jnp.swapaxes(last_w[0], 1, 2),
    )
    return out.reshape(1, 2, 4, 2, 16, 2, N)


def solution(mesh):
    in_specs = (
        P(None, None, "readout", None, None, None),
        P(None, "coil", "readout", None, None, None),
        P(None, "coil", None, "readout", None, None, None),
        P("coil", None, None, None),
        P("cascade", None, None, None),
        P("cascade", None, None, None),
        P("cascade", None, None, None),
    )
    out_specs = P("cascade", None, None, "readout", "coil", None, None)
    return jax.shard_map(per_device, mesh=mesh, in_specs=in_specs, out_specs=out_specs, check_vma=False)
```

```python
import functools

import jax
import jax.numpy as jnp
import numpy as np
from jax import lax
from jax.experimental import pallas as pl
from jax.experimental.pallas import tpu as pltpu
from jax.sharding import PartitionSpec as P

MESH = pl.DeviceIdType.MESH
BF = jnp.bfloat16
F32 = jnp.float32
N = 128
ZS = 4
SHARE = N // ZS
WIN = 40
LAG = 3
GROUPS = 9


def complex_blocks(direction):
    k = np.arange(N)
    angle = ((k[:, None] * k[None, :]) % N).astype(np.float32) * np.float32(2.0 * np.pi / N)
    factor = np.float32(1.0 / np.sqrt(N))
    cos, sin = np.cos(angle) * factor, direction * np.sin(angle) * factor
    return np.block([[cos, -sin], [sin, cos]]), np.block([[cos, sin], [-sin, cos]])


def first_selection():
    pick = np.zeros((4, 64, 144))
    for j in range(4):
        for a in range(3):
            for e in range(3):
                for c in range(2):
                    for t in range(3):
                        at = (a * 3 + e) * 16 + (j + t) // 4 * 8 + c * 4 + (j + t) % 4
                        pick[j, (9 * a + 3 * t + e) * 2 + c, at] = 1
    return pick


def last_selection():
    pick = np.zeros((2, 3, 2, 3, 4, 2, 2, 64))
    for a in range(3):
        for delta in range(2):
            for e in range(3):
                for line in range(4):
                    for j in range(4):
                        c = j + 4 * delta - line
                        if 0 <= c < 3:
                            for o in range(2):
                                pick[j // 2, 2 - a, delta, e, line, o, j % 2, (9 * a + 3 * c + e) * 2 + o] = 1
    return pick


def constant_tables():
    rows_forward, cols_forward = complex_blocks(-1.0)
    rows_inverse, cols_inverse = complex_blocks(1.0)
    deint = np.zeros((256, 256))
    for c in range(2):
        for l in range(N):
            deint[c * N + l, 2 * l + c] = 1
    window = np.zeros((2 * ZS * WIN, 256))
    for c in range(2):
        for z in range(ZS):
            for w in range(SHARE + 4):
                l = SHARE * z - 2 + w
                if 0 <= l < N:
                    window[(c * ZS + z) * WIN + w, c * N + l] = 1
    base = np.zeros((64, 256))
    gather = np.zeros((64, 256))
    for l in range(SHARE):
        for o in range(2):
            base[2 * l + o, (l + 2) // 4 * 8 + o * 4 + (l + 2) % 4] = 1
            gather[o * SHARE + l, 2 * l + o] = 1
    return {
        "deint": deint,
        "deint_window": window @ deint,
        "rows_forward": rows_forward,
        "cols_forward": cols_forward,
        "cols_inverse": cols_inverse,
        "rows_inverse": window @ rows_inverse,
        "base": base,
        "gather": gather,
        "eye": np.eye(128),
        "first": first_selection().reshape(4 * 64, 144),
        "last": last_selection().reshape(2 * 144, 128),
    }


def tables_array():
    tables = constant_tables()
    where, parts, at = {}, [], 0
    for name, table in tables.items():
        where[name] = (at, table.shape[0])
        parts.append(np.pad(table, ((0, 0), (0, 256 - table.shape[1]))))
        at += table.shape[0]
    return where, np.concatenate(parts, 0).astype(jnp.bfloat16)


WHERE, TABLES = tables_array()
EARLY = sum(WHERE[name][1] for name in ("deint", "deint_window"))
LATE = TABLES.shape[0] - EARLY


def dot(a, b):
    return jnp.dot(a, b, preferred_element_type=F32)


def dot_turned(a, b):
    return lax.dot_general(a, b, (((1,), (1,)), ((), ())), preferred_element_type=F32)


def swap_blocks(x):
    return jnp.concatenate(
        [
            jnp.concatenate([x[:N, :N], x[N:, :N]], 1),
            jnp.concatenate([x[:N, N:], x[N:, N:]], 1),
        ],
        0,
    )


def twice(x):
    return jnp.concatenate([x, x], 1)


def kernel(
    tables_in, initial, coil_maps, kspace, sampled, first_in, time_in, last_in,
    out,
    tab, maps_raw, ksp_raw, img_raw, mask,
    first_r, time_r, last_r, first_s, time_s, last_s,
    maps_d, maps_w, ksp_d, img, acc, rs_send, rs_recv, halo, slab, total, outs,
    local_sem, core_send, core_recv, w_send, w_recv, rs_ssem, rs_rsem, h_ssem, h_rsem,
    ag_ssem, ag_rsem, o_ssem, o_rsem,
):
    cas, coil, ro = lax.axis_index("cascade"), lax.axis_index("coil"), lax.axis_index("readout")
    z, core = coil // 2, coil % 2
    hi = ro % 2
    block = 1 - (hi + cas - 2 * hi * cas)
    other_core = (cas, coil + 1 - 2 * core, ro)
    other_cas = (1 - cas, coil, ro)
    other_both = (1 - cas, coil + 1 - 2 * core, ro)
    peers = [(cas, 2 * ((z + d) % ZS) + core, ro) for d in (1, 2, 3)]
    before, after = (1 - cas, coil, ro - 1), (1 - cas, coil, ro + 1)
    has_before, has_after = ro > 0, ro < 7

    def table(name, columns=256):
        at, count = WHERE[name]
        return tab[at:at + count, :columns]

    def local(number, source, target):
        return pltpu.make_async_copy(source, target, local_sem.at[number])

    def remote(source, target, ssem, rsem, device):
        return pltpu.make_async_remote_copy(
            src_ref=source, dst_ref=target, send_sem=ssem, recv_sem=rsem, device_id=device, device_id_type=MESH
        )

    barrier = pltpu.get_barrier_semaphore()
    for device in [other_core, other_cas, other_both, *peers]:
        pl.semaphore_signal(barrier, inc=1, device_id=device, device_id_type=MESH)

    @pl.when(has_before)
    def _():
        pl.semaphore_signal(barrier, inc=1, device_id=before, device_id_type=MESH)

    @pl.when(has_after)
    def _():
        pl.semaphore_signal(barrier, inc=1, device_id=after, device_id_type=MESH)

    loads = [
        local(0, tables_in.at[pl.ds(0, EARLY)], tab.at[pl.ds(0, EARLY)]),
        local(1, coil_maps.at[block], maps_raw.at[pl.ds(0, 2)]),
        local(2, kspace.at[block, :, :, core], ksp_raw.at[pl.ds(0, 2)]),
        local(4, initial.at[block, :, core], img_raw),
        local(3, sampled.at[:, :, core], mask.at[pl.ds(0, 2)]),
        local(10, tables_in.at[pl.ds(EARLY, LATE)], tab.at[pl.ds(EARLY, LATE)]),
        local(5, first_in, first_r.at[cas]),
        local(6, time_in, time_r.at[cas]),
        local(7, last_in, last_r.at[cas]),
    ]
    for copy in loads:
        copy.start()

    exchange = [remote(sampled.at[:, :, 1 - core], mask.at[pl.ds(2, 2)], core_send.at[4], core_recv.at[4], other_core)]
    for r in range(2):
        exchange += [
            remote(
                kspace.at[block, :, :, 1 - core, r], ksp_raw.at[pl.ds(2, 2), :, r],
                core_send.at[2 * r], core_recv.at[2 * r], other_core,
            ),
            remote(
                coil_maps.at[block, :, r], maps_raw.at[pl.ds(2, 2), r],
                core_send.at[2 * r + 1], core_recv.at[2 * r + 1], other_core,
            ),
        ]
    weights = [
        remote(source, target.at[cas], w_send.at[n], w_recv.at[n], other_cas)
        for n, (source, target) in enumerate(((first_in, first_r), (time_in, time_r), (last_in, last_r)))
    ]
    weights_in = [
        remote(source, target.at[1 - cas], w_send.at[n], w_recv.at[n], other_cas)
        for n, (source, target) in enumerate(((first_in, first_r), (time_in, time_r), (last_in, last_r)))
    ]

    zero_rows = jnp.zeros((2 * WIN, 256), BF)
    for s in range(2):
        @pl.when(ro == 0)
        def _():
            halo[s, 0] = zero_rows
            halo[s, 1] = zero_rows

        @pl.when(ro == 7)
        def _():
            halo[s, 4] = zero_rows
            halo[s, 5] = zero_rows

    def prepare(pair, r):
        both = jnp.concatenate([maps_raw[2 * pair, r], maps_raw[2 * pair + 1, r]], 1)
        maps_d[pair, r] = dot(table("deint"), both)
        maps_w[pair, r] = dot(table("deint_window"), both)
        for j in (2 * pair, 2 * pair + 1):
            phases = jnp.concatenate([ksp_raw[j, 0, r], ksp_raw[j, 1, r]], 1)
            ksp_d[j, r] = swap_blocks(dot(table("deint"), phases)).astype(BF)

    def consistency(s, r, coils):
        image = img[s, r].astype(F32)
        real, imag = image[:, 0].reshape(N, 256), image[:, 1].reshape(N, 256)
        stage = []
        for j in coils:
            lanes = slice(j % 2 * N, j % 2 * N + N)
            map_r, map_i = twice(maps_d[j // 2, r, :N, lanes]), twice(maps_d[j // 2, r, N:, lanes])
            stage.append(jnp.concatenate([map_r * real - map_i * imag, map_r * imag + map_i * real], 0).astype(BF))
        forward = table("rows_forward")
        stage = [swap_blocks(dot(forward, x).astype(BF)) for x in stage]
        forward = table("cols_forward")
        stage = [dot(x, forward) for x in stage]
        stage = [
            jnp.where(twice(mask[j].reshape(256, N)) != 0, ksp_d[j, r].astype(F32), x).astype(BF)
            for j, x in zip(coils, stage)
        ]
        inverse = table("cols_inverse")
        stage = [swap_blocks(dot(x, inverse).astype(BF)) for x in stage]
        inverse = table("rows_inverse")
        stage = [dot(inverse, x) for x in stage]
        rows = ZS * WIN
        sum_r, sum_i = 0.0, 0.0
        for j, x in zip(coils, stage):
            value_r, value_i = x[:rows], x[rows:]
            lanes = slice(j % 2 * N, j % 2 * N + N)
            win_r, win_i = twice(maps_w[j // 2, r, :rows, lanes]), twice(maps_w[j // 2, r, rows:, lanes])
            sum_r = sum_r + win_r * value_r + win_i * value_i
            sum_i = sum_i + win_r * value_i - win_i * value_r
        return sum_r, sum_i

    def reduce_copies(s, r):
        return [
            remote(
                rs_send.at[s, r, (z + d) % ZS], rs_recv.at[s, r, d - 1],
                rs_ssem.at[s, r, d - 1], rs_rsem.at[s, r, d - 1], peers[d - 1],
            )
            for d in (1, 2, 3)
        ]

    def reduce_send(s, r, sum_r, sum_i):
        for share in range(ZS):
            at = share * WIN
            rs_send[s, r, share] = jnp.concatenate([sum_r[at:at + WIN], sum_i[at:at + WIN]], 0).astype(BF)
        for copy in reduce_copies(s, r):
            copy.start()

    def halo_copies(s, r):
        return (
            remote(halo.at[s, 2 + r], halo.at[s, 4 + r], h_ssem.at[s, r, 0], h_rsem.at[s, r, 0], before),
            remote(halo.at[s, 2 + r], halo.at[s, r], h_ssem.at[s, r, 1], h_rsem.at[s, r, 1], after),
        )

    def combine(s, r):
        for copy in reduce_copies(s, r):
            copy.wait_recv()
        summed = rs_send[s, r, z].astype(F32)
        for d in range(3):
            summed = summed + rs_recv[s, r, d].astype(F32)
        top = lax.broadcasted_iota(jnp.int32, (8, 256), 0) < 4
        parts = []
        for at in range(0, WIN, 8):
            real, imag = summed[at:at + 8], summed[WIN + at:WIN + at + 8]
            parts.append(jnp.where(top, real, pltpu.roll(imag, 4, 0)))
            parts.append(jnp.where(top, pltpu.roll(real, 4, 0), imag))
        halo[s, 2 + r] = jnp.concatenate(parts, 0).astype(BF)
        to_before, to_after = halo_copies(s, r)

        @pl.when(has_before)
        def _():
            to_before.start()

        @pl.when(has_after)
        def _():
            to_after.start()

    def weights_of(s):
        @pl.when(cas != s)
        def _():
            for copy in weights_in:
                copy.wait_recv()

        eye = table("eye", 128)
        small = table("eye", 64)[:64]
        rows = dot_turned(small, first_r[s].reshape(54, 64)).astype(BF)
        for j in range(4):
            at = WHERE["first"][0] + 64 * j
            first_s[64 * j:64 * j + 64] = dot(rows, tab[at:at + 54, :144]).astype(BF)
        steps = time_r[s]
        time_s[:64, :N] = dot_turned(small, steps[64:]).astype(BF)
        time_s[64:, :N] = dot_turned(small, steps[:128]).astype(BF)
        time_s[:, N:] = eye
        taps = last_r[s].reshape(54, 64)
        low, high = dot(taps, eye[:64]).astype(BF), dot(taps, eye[64:]).astype(BF)
        parts = []
        for n in range(2):
            at = WHERE["last"][0] + 144 * n
            parts.append(dot(tab[at:at + 144, :54], low) + dot(tab[at:at + 144, 64:118], high))
        last = jnp.concatenate(parts, 1)
        line = lax.broadcasted_iota(jnp.int32, (144, 256), 1) // 64
        for place in range(3):
            mine = last
            if place == 0:
                mine = jnp.where((line == 0) & (z == 0), 0.0, last)
            if place == 2:
                mine = jnp.where((line > 0) & (z == ZS - 1), 0.0, last)
            last_s[place, :144] = mine.astype(BF)
            last_s[place, 144:192] = (mine[96:] * jnp.where(ro == 0, 0.0, 1.0)).astype(BF)
            last_s[place, 192:] = (mine[:48] * jnp.where(ro == 7, 0.0, 1.0)).astype(BF)

    def moved(x, by):
        lane = lax.broadcasted_iota(jnp.int32, (x.shape[0], N), 1)
        dead = lane == (0 if by == 1 else N - 1)
        halves = [pltpu.roll(x[:, at:at + N], by % N, 1) for at in (0, N)]
        return jnp.concatenate([jnp.where(dead, 0.0, half) for half in halves], 1)

    def spread(s, rows):
        for row in rows:
            cells = halo[s, row].astype(F32)
            for e, x in enumerate((moved(cells, 1), cells, moved(cells, -1))):
                at = (row * 3 + e) * 16
                for g in range(GROUPS):
                    slab[g, at:at + 16] = x[8 * g:8 * g + 16].astype(BF)

    def lifted(row, g):
        return jnp.maximum(dot(first_s[...], slab[g, 48 * row:48 * row + 144]), 0.0).astype(BF)

    def in_time(hidden):
        columns = []
        for u in range(2):
            lines = []
            for j in (2 * u, 2 * u + 1):
                one = hidden[64 * j:64 * j + 64]
                lines.append(jnp.concatenate([one[:, :N], one[:, N:]], 0))
            lines = jnp.concatenate(lines, 1)
            columns.append(lines)
        weight = time_s[:, :N]
        columns = [jnp.maximum(dot(weight, x) + x.astype(F32), 0.0).astype(BF) for x in columns]
        stack = []
        for u in range(2):
            for j in range(2):
                one = columns[u][:, j * N:j * N + N]
                stack.append(jnp.concatenate([one[:64], one[64:]], 1))
        return jnp.concatenate(stack, 0)

    def projected(row, g, stack):
        low, high = {0: (144, 192), 1: (48, 144), 2: (0, 96), 3: (192, 240)}[row]
        result = dot(last_s[0 if g == 0 else 2 if g == GROUPS - 1 else 1, low:high], stack)
        for n, target in enumerate({0: (0,), 1: (0, 1), 2: (0, 1), 3: (1,)}[row]):
            total[target, g + 1] += result[48 * n:48 * n + 24]
            total[target, g] += result[48 * n + 24:48 * n + 48]

    def sweep(rows):
        units = [(row, g) for g in range(GROUPS) for row in rows]
        hidden, stacks = {}, {}
        for n in range(len(units) + 2 * LAG):
            if n < len(units):
                hidden[n] = lifted(*units[n])
            if 0 <= n - LAG < len(units):
                stacks[n - LAG] = in_time(hidden.pop(n - LAG))
            if 0 <= n - 2 * LAG:
                projected(*units[n - 2 * LAG], stacks.pop(n - 2 * LAG))

    def halo_wait(s, r):
        to_before, to_after = halo_copies(s, r)

        @pl.when(has_after)
        def _():
            to_before.wait_recv()

        @pl.when(has_before)
        def _():
            to_after.wait_recv()

    def finish(s, r):
        taps = [total[r, 1:9, 8 * e:8 * e + 8].reshape(64, 256) for e in range(3)]
        change = moved(taps[0], 1) + taps[1] + moved(taps[2], -1)
        image = (dot(table("base", 2 * WIN), halo[s, 2 + r]) + change).astype(BF)
        if s == 0:
            share = dot(table("gather", 64), image).astype(BF)
            for c in range(2):
                img[1, r, z, c] = share[c * SHARE:c * SHARE + SHARE]
            for copy in gather_copies(r, False):
                copy.start()
        for half in range(2):
            for q in range(2):
                outs[s, r, half, q] = image[32 * half:32 * half + 32, q * N:q * N + N]
        if s == 1:
            send_output(s, r)

    def gather_copies(r, arriving):
        return [
            remote(
                img.at[1, r, z], img.at[1, r, (z + ZS - d) % ZS if arriving else z],
                ag_ssem.at[r, d - 1], ag_rsem.at[r, d - 1], peers[d - 1],
            )
            for d in (1, 2, 3)
        ]

    def near_copies(s, r):
        return (
            local(8 + r, outs.at[s, r, core], out.at[block, :, core, r]),
            remote(outs.at[s, r, 1 - core], out.at[block, :, core, r], o_ssem.at[r, 0], o_rsem.at[r, 0], other_core),
        )

    def far_copies(s, r):
        return (
            remote(outs.at[s, r, core], out.at[block, :, core, r], o_ssem.at[r, 1], o_rsem.at[r, 1], other_cas),
            remote(outs.at[s, r, 1 - core], out.at[block, :, core, r], o_ssem.at[r, 2], o_rsem.at[r, 2], other_both),
        )

    def send_output(s, r):
        @pl.when(cas == s)
        def _():
            for copy in near_copies(s, r):
                copy.start()

        @pl.when(cas != s)
        def _():
            for copy in far_copies(s, r):
                copy.start()

    pl.semaphore_wait(barrier, 6 + jnp.where(has_before, 1, 0) + jnp.where(has_after, 1, 0))
    for copy in exchange + weights:
        copy.start()
    for copy in loads[:4]:
        copy.wait()
    for r in range(2):
        phases = jnp.concatenate([img_raw[0, r], img_raw[1, r]], 1)
        plain = dot(table("deint"), phases).astype(BF)
        for share in range(ZS):
            for c in range(2):
                at = c * N + share * SHARE
                img[0, r, share, c] = plain[at:at + SHARE]
        prepare(0, r)
    for copy in loads[4:]:
        copy.wait()
    acc[0, 0], acc[0, 1] = consistency(0, 0, (0, 1))

    acc[1, 0], acc[1, 1] = consistency(0, 1, (0, 1))
    exchange[0].wait_recv()
    for r in range(2):
        for copy in exchange[1 + 2 * r:3 + 2 * r]:
            copy.wait_recv()
        prepare(1, r)
        sum_r, sum_i = consistency(0, r, (2, 3))
        reduce_send(0, r, acc[r, 0] + sum_r, acc[r, 1] + sum_i)

    for s in range(2):
        if s == 1:
            for r in range(2):
                for copy in gather_copies(r, True):
                    copy.wait_recv()
                reduce_send(1, r, *consistency(1, r, (0, 1, 2, 3)))
            send_output(0, 0)
            send_output(0, 1)
        weights_of(s)
        total[...] = jnp.zeros_like(total)
        combine(s, 0)
        spread(s, (2,))
        combine(s, 1)
        spread(s, (3,))
        halo_wait(s, 0)
        spread(s, (0, 4))
        sweep((2,))
        halo_wait(s, 1)
        spread(s, (1, 5))
        sweep((1, 0))
        finish(s, 0)
        sweep((3,))
        finish(s, 1)

    for copy in exchange + weights + gather_copies(0, False) + gather_copies(1, False):
        copy.wait_send()
    for s in range(2):
        for r in range(2):
            for copy in reduce_copies(s, r):
                copy.wait_send()
            to_before, to_after = halo_copies(s, r)

            @pl.when(has_before)
            def _():
                to_before.wait_send()

            @pl.when(has_after)
            def _():
                to_after.wait_send()

            @pl.when(cas == s)
            def _():
                keep, give = near_copies(s, r)
                keep.wait()
                give.wait_send()

            @pl.when(cas != s)
            def _():
                for copy in far_copies(s, r):
                    copy.wait_send()

    for r in range(2):
        source = outs.at[0, r, 0]
        arriving = (
            remote(source, out.at[block, :, 1 - core, r], o_ssem.at[r, 0], o_rsem.at[r, 0], other_core),
            remote(source, out.at[1 - block, :, core, r], o_ssem.at[r, 1], o_rsem.at[r, 1], other_cas),
            remote(source, out.at[1 - block, :, 1 - core, r], o_ssem.at[r, 2], o_rsem.at[r, 2], other_both),
        )
        for copy in arriving:
            copy.wait_recv()


def per_device(initial, coil_maps, kspace, sampled, first_w, time_w, last_w):
    dma = pltpu.SemaphoreType.DMA
    out = pl.pallas_call(
        kernel,
        out_shape=jax.ShapeDtypeStruct((2, 2, 2, 2, 32, N), BF),
        in_specs=[pl.BlockSpec(memory_space=pl.ANY)] * 8,
        out_specs=pl.BlockSpec(memory_space=pl.ANY),
        scratch_shapes=[
            pltpu.VMEM(TABLES.shape, BF),
            pltpu.VMEM((4, 2, 256, N), BF),
            pltpu.VMEM((4, 2, 2, 256, N), BF),
            pltpu.VMEM((2, 2, 256, N), BF),
            pltpu.VMEM((4, 2, N, N), jnp.int32),
            pltpu.VMEM((2, 27, 2, 64), BF),
            pltpu.VMEM((2, 192, 64), BF),
            pltpu.VMEM((2, 27, 2, 64), BF),
            pltpu.VMEM((256, 144), BF),
            pltpu.VMEM((128, 256), BF),
            pltpu.VMEM((3, 240, 256), BF),
            pltpu.VMEM((2, 2, 256, 256), F32),
            pltpu.VMEM((2, 2, 2 * ZS * WIN, 256), F32),
            pltpu.VMEM((4, 2, 256, 256), BF),
            pltpu.VMEM((2, 2, ZS, 2, SHARE, 256), BF),
            pltpu.VMEM((2, 2, ZS * WIN, 256), F32),
            pltpu.VMEM((2, 2, ZS, 2 * WIN, 256), BF),
            pltpu.VMEM((2, 2, 3, 2 * WIN, 256), BF),
            pltpu.VMEM((2, 6, 2 * WIN, 256), BF),
            pltpu.VMEM((GROUPS, 288, 256), BF),
            pltpu.VMEM((2, 10, 24, 256), F32),
            pltpu.VMEM((2, 2, 2, 2, 32, N), BF),
            dma((11,)),
            dma((5,)),
            dma((5,)),
            dma((3,)),
            dma((3,)),
            dma((2, 2, 3)),
            dma((2, 2, 3)),
            dma((2, 2, 2)),
            dma((2, 2, 2)),
            dma((2, 3)),
            dma((2, 3)),
            dma((2, 3)),
            dma((2, 3)),
        ],
        compiler_params=pltpu.CompilerParams(
            collective_id=0, has_side_effects=True, vmem_limit_bytes=60_000_000
        ),
    )(
        jnp.asarray(TABLES),
        initial.reshape(2, 2, 2, 2, 256, N),
        coil_maps.reshape(2, 2, 2, 256, N),
        kspace.reshape(2, 2, 2, 2, 2, 256, N),
        sampled.reshape(2, 2, 2, N, N),
        first_w[0],
        time_w[0].reshape(192, 64),
        jnp.swapaxes(last_w[0], 1, 2),
    )
    return out.reshape(1, 2, 4, 2, 16, 2, N)


def solution(mesh):
    in_specs = (
        P(None, None, "readout", None, None, None),
        P(None, "coil", "readout", None, None, None),
        P(None, "coil", None, "readout", None, None, None),
        P("coil", None, None, None),
        P("cascade", None, None, None),
        P("cascade", None, None, None),
        P("cascade", None, None, None),
    )
    out_specs = P("cascade", None, None, "readout", "coil", None, None)
    return jax.shard_map(per_device, mesh=mesh, in_specs=in_specs, out_specs=out_specs, check_vma=False)
```

```python
import functools

import jax
import jax.numpy as jnp
import numpy as np
from jax import lax
from jax.experimental import pallas as pl
from jax.experimental.pallas import tpu as pltpu
from jax.sharding import PartitionSpec as P

MESH = pl.DeviceIdType.MESH
BF = jnp.bfloat16
F32 = jnp.float32
N = 128
ZS = 4
SHARE = N // ZS
WIN = 40
LAG = 3
GROUPS = 9


def complex_blocks(direction):
    k = np.arange(N)
    angle = ((k[:, None] * k[None, :]) % N).astype(np.float32) * np.float32(2.0 * np.pi / N)
    factor = np.float32(1.0 / np.sqrt(N))
    cos, sin = np.cos(angle) * factor, direction * np.sin(angle) * factor
    return np.block([[cos, -sin], [sin, cos]]), np.block([[cos, sin], [-sin, cos]])


def first_selection():
    pick = np.zeros((4, 64, 144))
    for j in range(4):
        for a in range(3):
            for e in range(3):
                for c in range(2):
                    for t in range(3):
                        at = (a * 3 + e) * 16 + (j + t) // 4 * 8 + c * 4 + (j + t) % 4
                        pick[j, (9 * a + 3 * t + e) * 2 + c, at] = 1
    return pick


def last_selection():
    pick = np.zeros((2, 3, 2, 3, 4, 2, 2, 64))
    for a in range(3):
        for delta in range(2):
            for e in range(3):
                for line in range(4):
                    for j in range(4):
                        c = j + 4 * delta - line
                        if 0 <= c < 3:
                            for o in range(2):
                                pick[j // 2, 2 - a, delta, e, line, o, j % 2, (9 * a + 3 * c + e) * 2 + o] = 1
    return pick


def constant_tables():
    rows_forward, cols_forward = complex_blocks(-1.0)
    rows_inverse, cols_inverse = complex_blocks(1.0)
    deint = np.zeros((256, 256))
    for c in range(2):
        for l in range(N):
            deint[c * N + l, 2 * l + c] = 1
    window = np.zeros((2 * ZS * WIN, 256))
    for c in range(2):
        for z in range(ZS):
            for w in range(SHARE + 4):
                l = SHARE * z - 2 + w
                if 0 <= l < N:
                    window[(c * ZS + z) * WIN + w, c * N + l] = 1
    base = np.zeros((64, 256))
    gather = np.zeros((64, 256))
    for l in range(SHARE):
        for o in range(2):
            base[2 * l + o, (l + 2) // 4 * 8 + o * 4 + (l + 2) % 4] = 1
            gather[o * SHARE + l, 2 * l + o] = 1
    return {
        "deint": deint,
        "deint_window": window @ deint,
        "rows_forward": rows_forward,
        "cols_forward": cols_forward,
        "cols_inverse": cols_inverse,
        "rows_inverse": window @ rows_inverse,
        "base": base,
        "gather": gather,
        "eye": np.eye(128),
        "first": first_selection().reshape(4 * 64, 144),
        "last": last_selection().reshape(2 * 144, 128),
    }


def tables_array():
    tables = constant_tables()
    where, parts, at = {}, [], 0
    for name, table in tables.items():
        where[name] = (at, table.shape[0])
        parts.append(np.pad(table, ((0, 0), (0, 256 - table.shape[1]))))
        at += table.shape[0]
    return where, np.concatenate(parts, 0).astype(jnp.bfloat16)


WHERE, TABLES = tables_array()
EARLY = sum(WHERE[name][1] for name in ("deint", "deint_window"))
LATE = TABLES.shape[0] - EARLY


def dot(a, b):
    return jnp.dot(a, b, preferred_element_type=F32)


def dot_turned(a, b):
    return lax.dot_general(a, b, (((1,), (1,)), ((), ())), preferred_element_type=F32)


def swap_blocks(x):
    return jnp.concatenate(
        [
            jnp.concatenate([x[:N, :N], x[N:, :N]], 1),
            jnp.concatenate([x[:N, N:], x[N:, N:]], 1),
        ],
        0,
    )


def twice(x):
    return jnp.concatenate([x, x], 1)


def kernel(
    tables_in, initial, coil_maps, kspace, sampled, first_in, time_in, last_in,
    out,
    tab, maps_raw, ksp_raw, img_raw, mask_raw, mask_send, mask,
    first_r, time_r, last_r, first_s, time_s, last_s,
    maps_d, maps_w, ksp_d, img, acc, rs_send, rs_recv, halo, slab, total, outs,
    local_sem, core_send, core_recv, w_send, w_recv, rs_ssem, rs_rsem, h_ssem, h_rsem,
    ag_ssem, ag_rsem, o_ssem, o_rsem,
):
    cas, coil, ro = lax.axis_index("cascade"), lax.axis_index("coil"), lax.axis_index("readout")
    z, core = coil // 2, coil % 2
    hi = ro % 2
    block = 1 - (hi + cas - 2 * hi * cas)
    other_core = (cas, coil + 1 - 2 * core, ro)
    other_cas = (1 - cas, coil, ro)
    other_both = (1 - cas, coil + 1 - 2 * core, ro)
    peers = [(cas, 2 * ((z + d) % ZS) + core, ro) for d in (1, 2, 3)]
    before, after = (1 - cas, coil, ro - 1), (1 - cas, coil, ro + 1)
    has_before, has_after = ro > 0, ro < 7

    def table(name, columns=256):
        at, count = WHERE[name]
        return tab[at:at + count, :columns]

    def local(number, source, target):
        return pltpu.make_async_copy(source, target, local_sem.at[number])

    def remote(source, target, ssem, rsem, device):
        return pltpu.make_async_remote_copy(
            src_ref=source, dst_ref=target, send_sem=ssem, recv_sem=rsem, device_id=device, device_id_type=MESH
        )

    barrier = pltpu.get_barrier_semaphore()
    for device in [other_core, other_cas, other_both, *peers]:
        pl.semaphore_signal(barrier, inc=1, device_id=device, device_id_type=MESH)

    @pl.when(has_before)
    def _():
        pl.semaphore_signal(barrier, inc=1, device_id=before, device_id_type=MESH)

    @pl.when(has_after)
    def _():
        pl.semaphore_signal(barrier, inc=1, device_id=after, device_id_type=MESH)

    loads = [
        local(3, sampled, mask_raw),
        local(0, tables_in.at[pl.ds(0, EARLY)], tab.at[pl.ds(0, EARLY)]),
        local(1, coil_maps.at[block], maps_raw.at[pl.ds(0, 2)]),
        local(2, kspace.at[block, :, :, core], ksp_raw.at[pl.ds(0, 2)]),
        local(4, initial.at[block, :, core], img_raw),
        local(10, tables_in.at[pl.ds(EARLY, LATE)], tab.at[pl.ds(EARLY, LATE)]),
        local(5, first_in, first_r.at[cas]),
        local(6, time_in, time_r.at[cas]),
        local(7, last_in, last_r.at[cas]),
    ]
    for copy in loads:
        copy.start()

    exchange = [remote(mask_send, mask.at[pl.ds(2, 2)], core_send.at[4], core_recv.at[4], other_core)]
    for r in range(2):
        exchange += [
            remote(
                kspace.at[block, :, :, 1 - core, r], ksp_raw.at[pl.ds(2, 2), :, r],
                core_send.at[2 * r], core_recv.at[2 * r], other_core,
            ),
            remote(
                coil_maps.at[block, :, r], maps_raw.at[pl.ds(2, 2), r],
                core_send.at[2 * r + 1], core_recv.at[2 * r + 1], other_core,
            ),
        ]
    weights = [
        remote(source, target.at[cas], w_send.at[n], w_recv.at[n], other_cas)
        for n, (source, target) in enumerate(((first_in, first_r), (time_in, time_r), (last_in, last_r)))
    ]
    weights_in = [
        remote(source, target.at[1 - cas], w_send.at[n], w_recv.at[n], other_cas)
        for n, (source, target) in enumerate(((first_in, first_r), (time_in, time_r), (last_in, last_r)))
    ]

    zero_rows = jnp.zeros((2 * WIN, 256), BF)
    for s in range(2):
        @pl.when(ro == 0)
        def _():
            halo[s, 0] = zero_rows
            halo[s, 1] = zero_rows

        @pl.when(ro == 7)
        def _():
            halo[s, 4] = zero_rows
            halo[s, 5] = zero_rows

    def prepare(pair, r):
        both = jnp.concatenate([maps_raw[2 * pair, r], maps_raw[2 * pair + 1, r]], 1)
        maps_d[pair, r] = dot(table("deint"), both)
        maps_w[pair, r] = dot(table("deint_window"), both)
        for j in (2 * pair, 2 * pair + 1):
            phases = jnp.concatenate([ksp_raw[j, 0, r], ksp_raw[j, 1, r]], 1)
            ksp_d[j, r] = swap_blocks(dot(table("deint"), phases)).astype(BF)

    def consistency(s, r, coils):
        image = img[s, r].astype(F32)
        real, imag = image[:, 0].reshape(N, 256), image[:, 1].reshape(N, 256)
        stage = []
        for j in coils:
            lanes = slice(j % 2 * N, j % 2 * N + N)
            map_r, map_i = twice(maps_d[j // 2, r, :N, lanes]), twice(maps_d[j // 2, r, N:, lanes])
            stage.append(jnp.concatenate([map_r * real - map_i * imag, map_r * imag + map_i * real], 0).astype(BF))
        forward = table("rows_forward")
        stage = [swap_blocks(dot(forward, x).astype(BF)) for x in stage]
        forward = table("cols_forward")
        stage = [dot(x, forward) for x in stage]
        stage = [
            jnp.where(twice(mask[j].reshape(256, N).astype(F32)) > 0.5, ksp_d[j, r].astype(F32), x).astype(BF)
            for j, x in zip(coils, stage)
        ]
        inverse = table("cols_inverse")
        stage = [swap_blocks(dot(x, inverse).astype(BF)) for x in stage]
        inverse = table("rows_inverse")
        stage = [dot(inverse, x) for x in stage]
        rows = ZS * WIN
        sum_r, sum_i = 0.0, 0.0
        for j, x in zip(coils, stage):
            value_r, value_i = x[:rows], x[rows:]
            lanes = slice(j % 2 * N, j % 2 * N + N)
            win_r, win_i = twice(maps_w[j // 2, r, :rows, lanes]), twice(maps_w[j // 2, r, rows:, lanes])
            sum_r = sum_r + win_r * value_r + win_i * value_i
            sum_i = sum_i + win_r * value_i - win_i * value_r
        return sum_r, sum_i

    def reduce_copies(s, r):
        return [
            remote(
                rs_send.at[s, r, (z + d) % ZS], rs_recv.at[s, r, d - 1],
                rs_ssem.at[s, r, d - 1], rs_rsem.at[s, r, d - 1], peers[d - 1],
            )
            for d in (1, 2, 3)
        ]

    def reduce_send(s, r, sum_r, sum_i):
        for share in range(ZS):
            at = share * WIN
            rs_send[s, r, share] = jnp.concatenate([sum_r[at:at + WIN], sum_i[at:at + WIN]], 0).astype(BF)
        for copy in reduce_copies(s, r):
            copy.start()

    def halo_copies(s, r):
        return (
            remote(halo.at[s, 2 + r], halo.at[s, 4 + r], h_ssem.at[s, r, 0], h_rsem.at[s, r, 0], before),
            remote(halo.at[s, 2 + r], halo.at[s, r], h_ssem.at[s, r, 1], h_rsem.at[s, r, 1], after),
        )

    def combine(s, r):
        for copy in reduce_copies(s, r):
            copy.wait_recv()
        summed = rs_send[s, r, z].astype(F32)
        for d in range(3):
            summed = summed + rs_recv[s, r, d].astype(F32)
        top = lax.broadcasted_iota(jnp.int32, (8, 256), 0) < 4
        parts = []
        for at in range(0, WIN, 8):
            real, imag = summed[at:at + 8], summed[WIN + at:WIN + at + 8]
            parts.append(jnp.where(top, real, pltpu.roll(imag, 4, 0)))
            parts.append(jnp.where(top, pltpu.roll(real, 4, 0), imag))
        halo[s, 2 + r] = jnp.concatenate(parts, 0).astype(BF)
        to_before, to_after = halo_copies(s, r)

        @pl.when(has_before)
        def _():
            to_before.start()

        @pl.when(has_after)
        def _():
            to_after.start()

    def weights_of(s):
        @pl.when(cas != s)
        def _():
            for copy in weights_in:
                copy.wait_recv()

        eye = table("eye", 128)
        small = table("eye", 64)[:64]
        rows = dot_turned(small, first_r[s].reshape(54, 64)).astype(BF)
        for j in range(4):
            at = WHERE["first"][0] + 64 * j
            first_s[64 * j:64 * j + 64] = dot(rows, tab[at:at + 54, :144]).astype(BF)
        steps = time_r[s]
        time_s[:64, :N] = dot_turned(small, steps[64:]).astype(BF)
        time_s[64:, :N] = dot_turned(small, steps[:128]).astype(BF)
        time_s[:, N:] = eye
        taps = last_r[s].reshape(54, 64)
        low, high = dot(taps, eye[:64]).astype(BF), dot(taps, eye[64:]).astype(BF)
        parts = []
        for n in range(2):
            at = WHERE["last"][0] + 144 * n
            parts.append(dot(tab[at:at + 144, :54], low) + dot(tab[at:at + 144, 64:118], high))
        last = jnp.concatenate(parts, 1)
        line = lax.broadcasted_iota(jnp.int32, (144, 256), 1) // 64
        for place in range(3):
            mine = last
            if place == 0:
                mine = jnp.where((line == 0) & (z == 0), 0.0, last)
            if place == 2:
                mine = jnp.where((line > 0) & (z == ZS - 1), 0.0, last)
            last_s[place, :144] = mine.astype(BF)
            last_s[place, 144:192] = (mine[96:] * jnp.where(ro == 0, 0.0, 1.0)).astype(BF)
            last_s[place, 192:] = (mine[:48] * jnp.where(ro == 7, 0.0, 1.0)).astype(BF)

    def moved(x, by):
        lane = lax.broadcasted_iota(jnp.int32, (x.shape[0], N), 1)
        dead = lane == (0 if by == 1 else N - 1)
        halves = [pltpu.roll(x[:, at:at + N], by % N, 1) for at in (0, N)]
        return jnp.concatenate([jnp.where(dead, 0.0, half) for half in halves], 1)

    def spread(s, rows):
        for row in rows:
            cells = halo[s, row].astype(F32)
            for e, x in enumerate((moved(cells, 1), cells, moved(cells, -1))):
                at = (row * 3 + e) * 16
                for g in range(GROUPS):
                    slab[g, at:at + 16] = x[8 * g:8 * g + 16].astype(BF)

    def lifted(row, g):
        return jnp.maximum(dot(first_s[...], slab[g, 48 * row:48 * row + 144]), 0.0).astype(BF)

    def in_time(hidden):
        columns = []
        for u in range(2):
            lines = []
            for j in (2 * u, 2 * u + 1):
                one = hidden[64 * j:64 * j + 64]
                lines.append(jnp.concatenate([one[:, :N], one[:, N:]], 0))
            lines = jnp.concatenate(lines, 1)
            columns.append(lines)
        weight = time_s[:, :N]
        columns = [jnp.maximum(dot(weight, x) + x.astype(F32), 0.0).astype(BF) for x in columns]
        stack = []
        for u in range(2):
            for j in range(2):
                one = columns[u][:, j * N:j * N + N]
                stack.append(jnp.concatenate([one[:64], one[64:]], 1))
        return jnp.concatenate(stack, 0)

    def projected(row, g, stack):
        low, high = {0: (144, 192), 1: (48, 144), 2: (0, 96), 3: (192, 240)}[row]
        result = dot(last_s[0 if g == 0 else 2 if g == GROUPS - 1 else 1, low:high], stack)
        for n, target in enumerate({0: (0,), 1: (0, 1), 2: (0, 1), 3: (1,)}[row]):
            total[target, g + 1] += result[48 * n:48 * n + 24]
            total[target, g] += result[48 * n + 24:48 * n + 48]

    def sweep(rows):
        units = [(row, g) for g in range(GROUPS) for row in rows]
        hidden, stacks = {}, {}
        for n in range(len(units) + 2 * LAG):
            if n < len(units):
                hidden[n] = lifted(*units[n])
            if 0 <= n - LAG < len(units):
                stacks[n - LAG] = in_time(hidden.pop(n - LAG))
            if 0 <= n - 2 * LAG:
                projected(*units[n - 2 * LAG], stacks.pop(n - 2 * LAG))

    def halo_wait(s, r):
        to_before, to_after = halo_copies(s, r)

        @pl.when(has_after)
        def _():
            to_before.wait_recv()

        @pl.when(has_before)
        def _():
            to_after.wait_recv()

    def finish(s, r):
        taps = [total[r, 1:9, 8 * e:8 * e + 8].reshape(64, 256) for e in range(3)]
        change = moved(taps[0], 1) + taps[1] + moved(taps[2], -1)
        image = (dot(table("base", 2 * WIN), halo[s, 2 + r]) + change).astype(BF)
        if s == 0:
            share = dot(table("gather", 64), image).astype(BF)
            for c in range(2):
                img[1, r, z, c] = share[c * SHARE:c * SHARE + SHARE]
            for copy in gather_copies(r, False):
                copy.start()
        for half in range(2):
            for q in range(2):
                outs[s, r, half, q] = image[32 * half:32 * half + 32, q * N:q * N + N]
        if s == 1:
            send_output(s, r)

    def gather_copies(r, arriving):
        return [
            remote(
                img.at[1, r, z], img.at[1, r, (z + ZS - d) % ZS if arriving else z],
                ag_ssem.at[r, d - 1], ag_rsem.at[r, d - 1], peers[d - 1],
            )
            for d in (1, 2, 3)
        ]

    def near_copies(s, r):
        return (
            local(8 + r, outs.at[s, r, core], out.at[block, :, core, r]),
            remote(outs.at[s, r, 1 - core], out.at[block, :, core, r], o_ssem.at[r, 0], o_rsem.at[r, 0], other_core),
        )

    def far_copies(s, r):
        return (
            remote(outs.at[s, r, core], out.at[block, :, core, r], o_ssem.at[r, 1], o_rsem.at[r, 1], other_cas),
            remote(outs.at[s, r, 1 - core], out.at[block, :, core, r], o_ssem.at[r, 2], o_rsem.at[r, 2], other_both),
        )

    def send_output(s, r):
        @pl.when(cas == s)
        def _():
            for copy in near_copies(s, r):
                copy.start()

        @pl.when(cas != s)
        def _():
            for copy in far_copies(s, r):
                copy.start()

    loads[0].wait()
    for j in range(2):
        for q in range(2):
            mask[j, q] = mask_raw[j, q, core].astype(F32).astype(BF)
            mask_send[j, q] = mask_raw[j, q, 1 - core].astype(F32).astype(BF)
    pl.semaphore_wait(barrier, 6 + jnp.where(has_before, 1, 0) + jnp.where(has_after, 1, 0))
    for copy in exchange + weights:
        copy.start()
    for copy in loads[1:5]:
        copy.wait()
    for r in range(2):
        phases = jnp.concatenate([img_raw[0, r], img_raw[1, r]], 1)
        plain = dot(table("deint"), phases).astype(BF)
        for share in range(ZS):
            for c in range(2):
                at = c * N + share * SHARE
                img[0, r, share, c] = plain[at:at + SHARE]
        prepare(0, r)
    for copy in loads[5:]:
        copy.wait()
    acc[0, 0], acc[0, 1] = consistency(0, 0, (0, 1))

    acc[1, 0], acc[1, 1] = consistency(0, 1, (0, 1))
    exchange[0].wait_recv()
    for r in range(2):
        for copy in exchange[1 + 2 * r:3 + 2 * r]:
            copy.wait_recv()
        prepare(1, r)
        sum_r, sum_i = consistency(0, r, (2, 3))
        reduce_send(0, r, acc[r, 0] + sum_r, acc[r, 1] + sum_i)

    for s in range(2):
        if s == 1:
            for r in range(2):
                for copy in gather_copies(r, True):
                    copy.wait_recv()
                reduce_send(1, r, *consistency(1, r, (0, 1, 2, 3)))
            send_output(0, 0)
            send_output(0, 1)
        weights_of(s)
        total[...] = jnp.zeros_like(total)
        combine(s, 0)
        spread(s, (2,))
        combine(s, 1)
        spread(s, (3,))
        halo_wait(s, 0)
        spread(s, (0, 4))
        sweep((2,))
        halo_wait(s, 1)
        spread(s, (1, 5))
        sweep((1, 0))
        finish(s, 0)
        sweep((3,))
        finish(s, 1)

    for copy in exchange + weights + gather_copies(0, False) + gather_copies(1, False):
        copy.wait_send()
    for s in range(2):
        for r in range(2):
            for copy in reduce_copies(s, r):
                copy.wait_send()
            to_before, to_after = halo_copies(s, r)

            @pl.when(has_before)
            def _():
                to_before.wait_send()

            @pl.when(has_after)
            def _():
                to_after.wait_send()

            @pl.when(cas == s)
            def _():
                keep, give = near_copies(s, r)
                keep.wait()
                give.wait_send()

            @pl.when(cas != s)
            def _():
                for copy in far_copies(s, r):
                    copy.wait_send()

    for r in range(2):
        source = outs.at[0, r, 0]
        arriving = (
            remote(source, out.at[block, :, 1 - core, r], o_ssem.at[r, 0], o_rsem.at[r, 0], other_core),
            remote(source, out.at[1 - block, :, core, r], o_ssem.at[r, 1], o_rsem.at[r, 1], other_cas),
            remote(source, out.at[1 - block, :, 1 - core, r], o_ssem.at[r, 2], o_rsem.at[r, 2], other_both),
        )
        for copy in arriving:
            copy.wait_recv()


def per_device(initial, coil_maps, kspace, sampled, first_w, time_w, last_w):
    dma = pltpu.SemaphoreType.DMA
    out = pl.pallas_call(
        kernel,
        out_shape=jax.ShapeDtypeStruct((2, 2, 2, 2, 32, N), BF),
        in_specs=[pl.BlockSpec(memory_space=pl.ANY)] * 8,
        out_specs=pl.BlockSpec(memory_space=pl.ANY),
        scratch_shapes=[
            pltpu.VMEM(TABLES.shape, BF),
            pltpu.VMEM((4, 2, 256, N), BF),
            pltpu.VMEM((4, 2, 2, 256, N), BF),
            pltpu.VMEM((2, 2, 256, N), BF),
            pltpu.VMEM((2, 2, 2, N, N), jnp.int32),
            pltpu.VMEM((2, 2, N, N), BF),
            pltpu.VMEM((4, 2, N, N), BF),
            pltpu.VMEM((2, 27, 2, 64), BF),
            pltpu.VMEM((2, 192, 64), BF),
            pltpu.VMEM((2, 27, 2, 64), BF),
            pltpu.VMEM((256, 144), BF),
            pltpu.VMEM((128, 256), BF),
            pltpu.VMEM((3, 240, 256), BF),
            pltpu.VMEM((2, 2, 256, 256), F32),
            pltpu.VMEM((2, 2, 2 * ZS * WIN, 256), F32),
            pltpu.VMEM((4, 2, 256, 256), BF),
            pltpu.VMEM((2, 2, ZS, 2, SHARE, 256), BF),
            pltpu.VMEM((2, 2, ZS * WIN, 256), F32),
            pltpu.VMEM((2, 2, ZS, 2 * WIN, 256), BF),
            pltpu.VMEM((2, 2, 3, 2 * WIN, 256), BF),
            pltpu.VMEM((2, 6, 2 * WIN, 256), BF),
            pltpu.VMEM((GROUPS, 288, 256), BF),
            pltpu.VMEM((2, 10, 24, 256), F32),
            pltpu.VMEM((2, 2, 2, 2, 32, N), BF),
            dma((11,)),
            dma((5,)),
            dma((5,)),
            dma((3,)),
            dma((3,)),
            dma((2, 2, 3)),
            dma((2, 2, 3)),
            dma((2, 2, 2)),
            dma((2, 2, 2)),
            dma((2, 3)),
            dma((2, 3)),
            dma((2, 3)),
            dma((2, 3)),
        ],
        compiler_params=pltpu.CompilerParams(
            collective_id=0, has_side_effects=True, vmem_limit_bytes=60_000_000
        ),
    )(
        jnp.asarray(TABLES),
        initial.reshape(2, 2, 2, 2, 256, N),
        coil_maps.reshape(2, 2, 2, 256, N),
        kspace.reshape(2, 2, 2, 2, 2, 256, N),
        sampled.reshape(2, 2, 2, N, N),
        first_w[0],
        time_w[0].reshape(192, 64),
        jnp.swapaxes(last_w[0], 1, 2),
    )
    return out.reshape(1, 2, 4, 2, 16, 2, N)


def solution(mesh):
    in_specs = (
        P(None, None, "readout", None, None, None),
        P(None, "coil", "readout", None, None, None),
        P(None, "coil", None, "readout", None, None, None),
        P("coil", None, None, None),
        P("cascade", None, None, None),
        P("cascade", None, None, None),
        P("cascade", None, None, None),
    )
    out_specs = P("cascade", None, None, "readout", "coil", None, None)
    return jax.shard_map(per_device, mesh=mesh, in_specs=in_specs, out_specs=out_specs, check_vma=False)
```

```python
import functools

import jax
import jax.numpy as jnp
import numpy as np
from jax import lax
from jax.experimental import pallas as pl
from jax.experimental.pallas import tpu as pltpu
from jax.sharding import PartitionSpec as P

MESH = pl.DeviceIdType.MESH
BF = jnp.bfloat16
F32 = jnp.float32
N = 128
ZS = 4
SHARE = N // ZS
WIN = 40
LAG = 3
GROUPS = 9


def complex_blocks(direction):
    k = np.arange(N)
    angle = ((k[:, None] * k[None, :]) % N).astype(np.float32) * np.float32(2.0 * np.pi / N)
    factor = np.float32(1.0 / np.sqrt(N))
    cos, sin = np.cos(angle) * factor, direction * np.sin(angle) * factor
    return np.block([[cos, -sin], [sin, cos]]), np.block([[cos, sin], [-sin, cos]])


def first_selection():
    pick = np.zeros((4, 64, 144))
    for j in range(4):
        for a in range(3):
            for e in range(3):
                for c in range(2):
                    for t in range(3):
                        at = (a * 3 + e) * 16 + (j + t) // 4 * 8 + c * 4 + (j + t) % 4
                        pick[j, (9 * a + 3 * t + e) * 2 + c, at] = 1
    return pick


def last_selection():
    pick = np.zeros((2, 3, 2, 3, 4, 2, 2, 64))
    for a in range(3):
        for delta in range(2):
            for e in range(3):
                for line in range(4):
                    for j in range(4):
                        c = j + 4 * delta - line
                        if 0 <= c < 3:
                            for o in range(2):
                                pick[j // 2, 2 - a, delta, e, line, o, j % 2, (9 * a + 3 * c + e) * 2 + o] = 1
    return pick


def constant_tables():
    rows_forward, cols_forward = complex_blocks(-1.0)
    rows_inverse, cols_inverse = complex_blocks(1.0)
    deint = np.zeros((256, 256))
    for c in range(2):
        for l in range(N):
            deint[c * N + l, 2 * l + c] = 1
    window = np.zeros((2 * ZS * WIN, 256))
    for c in range(2):
        for z in range(ZS):
            for w in range(SHARE + 4):
                l = SHARE * z - 2 + w
                if 0 <= l < N:
                    window[(c * ZS + z) * WIN + w, c * N + l] = 1
    base = np.zeros((64, 256))
    gather = np.zeros((64, 256))
    for l in range(SHARE):
        for o in range(2):
            base[2 * l + o, (l + 2) // 4 * 8 + o * 4 + (l + 2) % 4] = 1
            gather[o * SHARE + l, 2 * l + o] = 1
    return {
        "deint": deint,
        "deint_window": window @ deint,
        "rows_forward": rows_forward,
        "cols_forward": cols_forward,
        "cols_inverse": cols_inverse,
        "rows_inverse": window @ rows_inverse,
        "base": base,
        "gather": gather,
        "eye": np.eye(128),
        "first": first_selection().reshape(4 * 64, 144),
        "last": last_selection().reshape(2 * 144, 128),
    }


def tables_array():
    tables = constant_tables()
    where, parts, at = {}, [], 0
    for name, table in tables.items():
        where[name] = (at, table.shape[0])
        parts.append(np.pad(table, ((0, 0), (0, 256 - table.shape[1]))))
        at += table.shape[0]
    return where, np.concatenate(parts, 0).astype(jnp.bfloat16)


WHERE, TABLES = tables_array()
EARLY = sum(WHERE[name][1] for name in ("deint", "deint_window"))
LATE = TABLES.shape[0] - EARLY


def dot(a, b):
    return jnp.dot(a, b, preferred_element_type=F32)


def dot_turned(a, b):
    return lax.dot_general(a, b, (((1,), (1,)), ((), ())), preferred_element_type=F32)


def swap_blocks(x):
    return jnp.concatenate(
        [
            jnp.concatenate([x[:N, :N], x[N:, :N]], 1),
            jnp.concatenate([x[:N, N:], x[N:, N:]], 1),
        ],
        0,
    )


def twice(x):
    return jnp.concatenate([x, x], 1)


def kernel(
    tables_in, initial, coil_maps, kspace, sampled, first_in, time_in, last_in,
    out,
    tab, maps_raw, ksp_raw, img_raw, mask,
    first_r, time_r, last_r, first_s, time_s, last_s,
    maps_d, maps_w, ksp_d, img, acc, rs_send, rs_recv, halo, slab, total, outs,
    local_sem, core_send, core_recv, w_send, w_recv, rs_ssem, rs_rsem, h_ssem, h_rsem,
    ag_ssem, ag_rsem, o_ssem, o_rsem,
):
    cas, coil, ro = lax.axis_index("cascade"), lax.axis_index("coil"), lax.axis_index("readout")
    z, core = coil // 2, coil % 2
    hi = ro % 2
    block = 1 - (hi + cas - 2 * hi * cas)
    other_core = (cas, coil + 1 - 2 * core, ro)
    other_cas = (1 - cas, coil, ro)
    other_both = (1 - cas, coil + 1 - 2 * core, ro)
    peers = [(cas, 2 * ((z + d) % ZS) + core, ro) for d in (1, 2, 3)]
    before, after = (1 - cas, coil, ro - 1), (1 - cas, coil, ro + 1)
    has_before, has_after = ro > 0, ro < 7

    def table(name, columns=256):
        at, count = WHERE[name]
        return tab[at:at + count, :columns]

    def local(number, source, target):
        return pltpu.make_async_copy(source, target, local_sem.at[number])

    def remote(source, target, ssem, rsem, device):
        return pltpu.make_async_remote_copy(
            src_ref=source, dst_ref=target, send_sem=ssem, recv_sem=rsem, device_id=device, device_id_type=MESH
        )

    barrier = pltpu.get_barrier_semaphore()
    for device in [other_core, other_cas, other_both, *peers]:
        pl.semaphore_signal(barrier, inc=1, device_id=device, device_id_type=MESH)

    @pl.when(has_before)
    def _():
        pl.semaphore_signal(barrier, inc=1, device_id=before, device_id_type=MESH)

    @pl.when(has_after)
    def _():
        pl.semaphore_signal(barrier, inc=1, device_id=after, device_id_type=MESH)

    loads = [
        local(0, tables_in.at[pl.ds(0, EARLY)], tab.at[pl.ds(0, EARLY)]),
        local(1, coil_maps.at[block], maps_raw.at[pl.ds(0, 2)]),
        local(2, kspace.at[block, :, :, core], ksp_raw.at[pl.ds(0, 2)]),
        local(4, initial.at[block, :, core], img_raw),
        local(3, sampled.at[:, :, core], mask.at[pl.ds(0, 2)]),
        local(10, tables_in.at[pl.ds(EARLY, LATE)], tab.at[pl.ds(EARLY, LATE)]),
        local(5, first_in, first_r.at[cas]),
        local(6, time_in, time_r.at[cas]),
        local(7, last_in, last_r.at[cas]),
    ]
    for copy in loads:
        copy.start()

    exchange = [remote(sampled.at[:, :, 1 - core], mask.at[pl.ds(2, 2)], core_send.at[4], core_recv.at[4], other_core)]
    for r in range(2):
        exchange += [
            remote(
                kspace.at[block, :, :, 1 - core, r], ksp_raw.at[pl.ds(2, 2), :, r],
                core_send.at[2 * r], core_recv.at[2 * r], other_core,
            ),
            remote(
                coil_maps.at[block, :, r], maps_raw.at[pl.ds(2, 2), r],
                core_send.at[2 * r + 1], core_recv.at[2 * r + 1], other_core,
            ),
        ]
    weights = [
        remote(source, target.at[cas], w_send.at[n], w_recv.at[n], other_cas)
        for n, (source, target) in enumerate(((first_in, first_r), (time_in, time_r), (last_in, last_r)))
    ]
    weights_in = [
        remote(source, target.at[1 - cas], w_send.at[n], w_recv.at[n], other_cas)
        for n, (source, target) in enumerate(((first_in, first_r), (time_in, time_r), (last_in, last_r)))
    ]

    zero_rows = jnp.zeros((2 * WIN, 256), BF)
    for s in range(2):
        @pl.when(ro == 0)
        def _():
            halo[s, 0] = zero_rows
            halo[s, 1] = zero_rows

        @pl.when(ro == 7)
        def _():
            halo[s, 4] = zero_rows
            halo[s, 5] = zero_rows

    def prepare(pair, r):
        both = jnp.concatenate([maps_raw[2 * pair, r], maps_raw[2 * pair + 1, r]], 1)
        maps_d[pair, r] = dot(table("deint"), both)
        maps_w[pair, r] = dot(table("deint_window"), both)
        for j in (2 * pair, 2 * pair + 1):
            phases = jnp.concatenate([ksp_raw[j, 0, r], ksp_raw[j, 1, r]], 1)
            ksp_d[j, r] = swap_blocks(dot(table("deint"), phases)).astype(BF)

    def consistency(s, r, coils):
        image = img[s, r].astype(F32)
        real, imag = image[:, 0].reshape(N, 256), image[:, 1].reshape(N, 256)
        stage = []
        for j in coils:
            lanes = slice(j % 2 * N, j % 2 * N + N)
            map_r, map_i = twice(maps_d[j // 2, r, :N, lanes]), twice(maps_d[j // 2, r, N:, lanes])
            stage.append(jnp.concatenate([map_r * real - map_i * imag, map_r * imag + map_i * real], 0).astype(BF))
        forward = table("rows_forward")
        stage = [swap_blocks(dot(forward, x).astype(BF)) for x in stage]
        forward = table("cols_forward")
        stage = [dot(x, forward) for x in stage]
        stage = [
            jnp.where(twice(mask[j].reshape(256, N)) != 0, ksp_d[j, r].astype(F32), x).astype(BF)
            for j, x in zip(coils, stage)
        ]
        inverse = table("cols_inverse")
        stage = [swap_blocks(dot(x, inverse).astype(BF)) for x in stage]
        inverse = table("rows_inverse")
        stage = [dot(inverse, x) for x in stage]
        rows = ZS * WIN
        sum_r, sum_i = 0.0, 0.0
        for j, x in zip(coils, stage):
            value_r, value_i = x[:rows], x[rows:]
            lanes = slice(j % 2 * N, j % 2 * N + N)
            win_r, win_i = twice(maps_w[j // 2, r, :rows, lanes]), twice(maps_w[j // 2, r, rows:, lanes])
            sum_r = sum_r + win_r * value_r + win_i * value_i
            sum_i = sum_i + win_r * value_i - win_i * value_r
        return sum_r, sum_i

    def reduce_copies(s, r):
        return [
            remote(
                rs_send.at[s, r, (z + d) % ZS], rs_recv.at[s, r, d - 1],
                rs_ssem.at[s, r, d - 1], rs_rsem.at[s, r, d - 1], peers[d - 1],
            )
            for d in (1, 2, 3)
        ]

    def reduce_send(s, r, sum_r, sum_i):
        for share in range(ZS):
            at = share * WIN
            rs_send[s, r, share] = jnp.concatenate([sum_r[at:at + WIN], sum_i[at:at + WIN]], 0).astype(BF)
        for copy in reduce_copies(s, r):
            copy.start()

    def halo_copies(s, r):
        return (
            remote(halo.at[s, 2 + r], halo.at[s, 4 + r], h_ssem.at[s, r, 0], h_rsem.at[s, r, 0], before),
            remote(halo.at[s, 2 + r], halo.at[s, r], h_ssem.at[s, r, 1], h_rsem.at[s, r, 1], after),
        )

    def combine(s, r):
        for copy in reduce_copies(s, r):
            copy.wait_recv()
        summed = rs_send[s, r, z].astype(F32)
        for d in range(3):
            summed = summed + rs_recv[s, r, d].astype(F32)
        top = lax.broadcasted_iota(jnp.int32, (8, 256), 0) < 4
        parts = []
        for at in range(0, WIN, 8):
            real, imag = summed[at:at + 8], summed[WIN + at:WIN + at + 8]
            parts.append(jnp.where(top, real, pltpu.roll(imag, 4, 0)))
            parts.append(jnp.where(top, pltpu.roll(real, 4, 0), imag))
        halo[s, 2 + r] = jnp.concatenate(parts, 0).astype(BF)
        to_before, to_after = halo_copies(s, r)

        @pl.when(has_before)
        def _():
            to_before.start()

        @pl.when(has_after)
        def _():
            to_after.start()

    def weights_of(s):
        @pl.when(cas != s)
        def _():
            for copy in weights_in:
                copy.wait_recv()

        eye = table("eye", 128)
        small = table("eye", 64)[:64]
        rows = dot_turned(small, first_r[s].reshape(54, 64)).astype(BF)
        for j in range(4):
            at = WHERE["first"][0] + 64 * j
            first_s[64 * j:64 * j + 64] = dot(rows, tab[at:at + 54, :144]).astype(BF)
        steps = time_r[s]
        time_s[:64, :N] = dot_turned(small, steps[64:]).astype(BF)
        time_s[64:, :N] = dot_turned(small, steps[:128]).astype(BF)
        time_s[:, N:] = eye
        taps = last_r[s].reshape(54, 64)
        low, high = dot(taps, eye[:64]).astype(BF), dot(taps, eye[64:]).astype(BF)
        parts = []
        for n in range(2):
            at = WHERE["last"][0] + 144 * n
            parts.append(dot(tab[at:at + 144, :54], low) + dot(tab[at:at + 144, 64:118], high))
        last = jnp.concatenate(parts, 1)
        line = lax.broadcasted_iota(jnp.int32, (144, 256), 1) // 64
        for place in range(3):
            mine = last
            if place == 0:
                mine = jnp.where((line == 0) & (z == 0), 0.0, last)
            if place == 2:
                mine = jnp.where((line > 0) & (z == ZS - 1), 0.0, last)
            last_s[place, :144] = mine.astype(BF)
            last_s[place, 144:192] = (mine[96:] * jnp.where(ro == 0, 0.0, 1.0)).astype(BF)
            last_s[place, 192:] = (mine[:48] * jnp.where(ro == 7, 0.0, 1.0)).astype(BF)

    def moved(x, by):
        lane = lax.broadcasted_iota(jnp.int32, (x.shape[0], N), 1)
        dead = lane == (0 if by == 1 else N - 1)
        halves = [pltpu.roll(x[:, at:at + N], by % N, 1) for at in (0, N)]
        return jnp.concatenate([jnp.where(dead, 0.0, half) for half in halves], 1)

    def spread(s, rows):
        for row in rows:
            cells = halo[s, row].astype(F32)
            for e, x in enumerate((moved(cells, 1), cells, moved(cells, -1))):
                at = (row * 3 + e) * 16
                for g in range(GROUPS):
                    slab[g, at:at + 16] = x[8 * g:8 * g + 16].astype(BF)

    def lifted(row, g):
        return jnp.maximum(dot(first_s[...], slab[g, 48 * row:48 * row + 144]), 0.0).astype(BF)

    def in_time(hidden):
        columns = []
        for u in range(2):
            lines = []
            for j in (2 * u, 2 * u + 1):
                one = hidden[64 * j:64 * j + 64]
                lines.append(jnp.concatenate([one[:, :N], one[:, N:]], 0))
            lines = jnp.concatenate(lines, 1)
            columns.append(lines)
        weight = time_s[:, :N]
        columns = [jnp.maximum(dot(weight, x) + x.astype(F32), 0.0).astype(BF) for x in columns]
        stack = []
        for u in range(2):
            for j in range(2):
                one = columns[u][:, j * N:j * N + N]
                stack.append(jnp.concatenate([one[:64], one[64:]], 1))
        return jnp.concatenate(stack, 0)

    def projected(row, g, stack):
        low, high = {0: (144, 192), 1: (48, 144), 2: (0, 96), 3: (192, 240)}[row]
        result = dot(last_s[0 if g == 0 else 2 if g == GROUPS - 1 else 1, low:high], stack)
        for n, target in enumerate({0: (0,), 1: (0, 1), 2: (0, 1), 3: (1,)}[row]):
            total[target, g + 1] += result[48 * n:48 * n + 24]
            total[target, g] += result[48 * n + 24:48 * n + 48]

    def sweep(rows):
        units = [(row, g) for g in range(GROUPS) for row in rows]
        hidden, stacks = {}, {}
        for n in range(len(units) + 2 * LAG):
            if n < len(units):
                hidden[n] = lifted(*units[n])
            if 0 <= n - LAG < len(units):
                stacks[n - LAG] = in_time(hidden.pop(n - LAG))
            if 0 <= n - 2 * LAG:
                projected(*units[n - 2 * LAG], stacks.pop(n - 2 * LAG))

    def wait_after(s, r):
        @pl.when(has_after)
        def _():
            halo_copies(s, r)[0].wait_recv()

    def wait_before(s, r):
        @pl.when(has_before)
        def _():
            halo_copies(s, r)[1].wait_recv()

    def finish(s, r):
        taps = [total[r, 1:9, 8 * e:8 * e + 8].reshape(64, 256) for e in range(3)]
        change = moved(taps[0], 1) + taps[1] + moved(taps[2], -1)
        image = (dot(table("base", 2 * WIN), halo[s, 2 + r]) + change).astype(BF)
        if s == 0:
            share = dot(table("gather", 64), image).astype(BF)
            for c in range(2):
                img[1, r, z, c] = share[c * SHARE:c * SHARE + SHARE]
            for copy in gather_copies(r, False):
                copy.start()
        for half in range(2):
            for q in range(2):
                outs[s, r, half, q] = image[32 * half:32 * half + 32, q * N:q * N + N]
        if s == 1:
            send_output(s, r)

    def gather_copies(r, arriving):
        return [
            remote(
                img.at[1, r, z], img.at[1, r, (z + ZS - d) % ZS if arriving else z],
                ag_ssem.at[r, d - 1], ag_rsem.at[r, d - 1], peers[d - 1],
            )
            for d in (1, 2, 3)
        ]

    def near_copies(s, r):
        return (
            local(8 + r, outs.at[s, r, core], out.at[block, :, core, r]),
            remote(outs.at[s, r, 1 - core], out.at[block, :, core, r], o_ssem.at[r, 0], o_rsem.at[r, 0], other_core),
        )

    def far_copies(s, r):
        return (
            remote(outs.at[s, r, core], out.at[block, :, core, r], o_ssem.at[r, 1], o_rsem.at[r, 1], other_cas),
            remote(outs.at[s, r, 1 - core], out.at[block, :, core, r], o_ssem.at[r, 2], o_rsem.at[r, 2], other_both),
        )

    def send_output(s, r):
        @pl.when(cas == s)
        def _():
            for copy in near_copies(s, r):
                copy.start()

        @pl.when(cas != s)
        def _():
            for copy in far_copies(s, r):
                copy.start()

    pl.semaphore_wait(barrier, 6 + jnp.where(has_before, 1, 0) + jnp.where(has_after, 1, 0))
    for copy in exchange + weights:
        copy.start()
    for copy in loads[:4]:
        copy.wait()
    for r in range(2):
        phases = jnp.concatenate([img_raw[0, r], img_raw[1, r]], 1)
        plain = dot(table("deint"), phases).astype(BF)
        for share in range(ZS):
            for c in range(2):
                at = c * N + share * SHARE
                img[0, r, share, c] = plain[at:at + SHARE]
        prepare(0, r)
    for copy in loads[4:]:
        copy.wait()
    acc[0, 0], acc[0, 1] = consistency(0, 0, (0, 1))

    acc[1, 0], acc[1, 1] = consistency(0, 1, (0, 1))
    exchange[0].wait_recv()
    for r in range(2):
        for copy in exchange[1 + 2 * r:3 + 2 * r]:
            copy.wait_recv()
        prepare(1, r)
        sum_r, sum_i = consistency(0, r, (2, 3))
        reduce_send(0, r, acc[r, 0] + sum_r, acc[r, 1] + sum_i)

    for s in range(2):
        if s == 1:
            for r in range(2):
                for copy in gather_copies(r, True):
                    copy.wait_recv()
                reduce_send(1, r, *consistency(1, r, (0, 1, 2, 3)))
            send_output(0, 0)
            send_output(0, 1)
        weights_of(s)
        total[...] = jnp.zeros_like(total)
        combine(s, 0)
        spread(s, (2,))
        combine(s, 1)
        spread(s, (3,))
        wait_after(s, 0)
        spread(s, (4,))
        sweep((2,))
        wait_before(s, 0)
        wait_before(s, 1)
        wait_after(s, 1)
        spread(s, (0, 1, 5))
        sweep((1, 0))
        finish(s, 0)
        sweep((3,))
        finish(s, 1)

    for copy in exchange + weights + gather_copies(0, False) + gather_copies(1, False):
        copy.wait_send()
    for s in range(2):
        for r in range(2):
            for copy in reduce_copies(s, r):
                copy.wait_send()
            to_before, to_after = halo_copies(s, r)

            @pl.when(has_before)
            def _():
                to_before.wait_send()

            @pl.when(has_after)
            def _():
                to_after.wait_send()

            @pl.when(cas == s)
            def _():
                keep, give = near_copies(s, r)
                keep.wait()
                give.wait_send()

            @pl.when(cas != s)
            def _():
                for copy in far_copies(s, r):
                    copy.wait_send()

    for r in range(2):
        source = outs.at[0, r, 0]
        arriving = (
            remote(source, out.at[block, :, 1 - core, r], o_ssem.at[r, 0], o_rsem.at[r, 0], other_core),
            remote(source, out.at[1 - block, :, core, r], o_ssem.at[r, 1], o_rsem.at[r, 1], other_cas),
            remote(source, out.at[1 - block, :, 1 - core, r], o_ssem.at[r, 2], o_rsem.at[r, 2], other_both),
        )
        for copy in arriving:
            copy.wait_recv()


def per_device(initial, coil_maps, kspace, sampled, first_w, time_w, last_w):
    dma = pltpu.SemaphoreType.DMA
    out = pl.pallas_call(
        kernel,
        out_shape=jax.ShapeDtypeStruct((2, 2, 2, 2, 32, N), BF),
        in_specs=[pl.BlockSpec(memory_space=pl.ANY)] * 8,
        out_specs=pl.BlockSpec(memory_space=pl.ANY),
        scratch_shapes=[
            pltpu.VMEM(TABLES.shape, BF),
            pltpu.VMEM((4, 2, 256, N), BF),
            pltpu.VMEM((4, 2, 2, 256, N), BF),
            pltpu.VMEM((2, 2, 256, N), BF),
            pltpu.VMEM((4, 2, N, N), jnp.int32),
            pltpu.VMEM((2, 27, 2, 64), BF),
            pltpu.VMEM((2, 192, 64), BF),
            pltpu.VMEM((2, 27, 2, 64), BF),
            pltpu.VMEM((256, 144), BF),
            pltpu.VMEM((128, 256), BF),
            pltpu.VMEM((3, 240, 256), BF),
            pltpu.VMEM((2, 2, 256, 256), F32),
            pltpu.VMEM((2, 2, 2 * ZS * WIN, 256), F32),
            pltpu.VMEM((4, 2, 256, 256), BF),
            pltpu.VMEM((2, 2, ZS, 2, SHARE, 256), BF),
            pltpu.VMEM((2, 2, ZS * WIN, 256), F32),
            pltpu.VMEM((2, 2, ZS, 2 * WIN, 256), BF),
            pltpu.VMEM((2, 2, 3, 2 * WIN, 256), BF),
            pltpu.VMEM((2, 6, 2 * WIN, 256), BF),
            pltpu.VMEM((GROUPS, 288, 256), BF),
            pltpu.VMEM((2, 10, 24, 256), F32),
            pltpu.VMEM((2, 2, 2, 2, 32, N), BF),
            dma((11,)),
            dma((5,)),
            dma((5,)),
            dma((3,)),
            dma((3,)),
            dma((2, 2, 3)),
            dma((2, 2, 3)),
            dma((2, 2, 2)),
            dma((2, 2, 2)),
            dma((2, 3)),
            dma((2, 3)),
            dma((2, 3)),
            dma((2, 3)),
        ],
        compiler_params=pltpu.CompilerParams(
            collective_id=0, has_side_effects=True, vmem_limit_bytes=60_000_000
        ),
    )(
        jnp.asarray(TABLES),
        initial.reshape(2, 2, 2, 2, 256, N),
        coil_maps.reshape(2, 2, 2, 256, N),
        kspace.reshape(2, 2, 2, 2, 2, 256, N),
        sampled.reshape(2, 2, 2, N, N),
        first_w[0],
        time_w[0].reshape(192, 64),
        jnp.swapaxes(last_w[0], 1, 2),
    )
    return out.reshape(1, 2, 4, 2, 16, 2, N)


def solution(mesh):
    in_specs = (
        P(None, None, "readout", None, None, None),
        P(None, "coil", "readout", None, None, None),
        P(None, "coil", None, "readout", None, None, None),
        P("coil", None, None, None),
        P("cascade", None, None, None),
        P("cascade", None, None, None),
        P("cascade", None, None, None),
    )
    out_specs = P("cascade", None, None, "readout", "coil", None, None)
    return jax.shard_map(per_device, mesh=mesh, in_specs=in_specs, out_specs=out_specs, check_vma=False)
```
